32 devices in a mesh: ctx: 8 (over z, core), fsdp: 4 (over y, x).
Axes of the slice: x: 2, y: 2, z: 4, core: 2. Of those that a mesh axis runs over, the one named last changes fastest.
Arguments:
- inputs: bfloat16 [4096, 5376], P('ctx'), may hold values from -400 to 400
- output_cotangent: bfloat16 [4096, 4096], P('ctx', 'fsdp'), may hold values from -96 to 96
- w_query: bfloat16 [5376, 4096], P('ctx', 'fsdp'), may hold values from -0.078125 to 0.078125
- key_projection: bfloat16 [5376, 2048], P('ctx', 'fsdp'), may hold values from -0.078125 to 0.078125
- value_projection: bfloat16 [5376, 2048], P('ctx', 'fsdp'), may hold values from -0.078125 to 0.078125
- norm_gain: float32 [5376], replicated, may hold values from 0.25 to 1.75
- q_gain: float32 [128], replicated, may hold values from 0.25 to 1.75
- key_norm_gain: float32 [128], replicated, may hold values from 0.25 to 1.75
- half_lengths: int32 [4], replicated, may hold values from 1 to 3072, 4096 in all
Outputs:
- grad_inputs: bfloat16 [4096, 5376], P('ctx', 'fsdp')
- grad_w_query: bfloat16 [5376, 4096], P('ctx', 'fsdp')
- grad_w_key: bfloat16 [5376, 2048], P('ctx', 'fsdp')
- grad_w_value: bfloat16 [5376, 2048], P('ctx', 'fsdp')
- grad_norm_gain: float32 [5376], P(('fsdp', 'ctx'))
- grad_q_gain: float32 [128], replicated
- grad_k_gain: float32 [128], replicated
- norm_row_dots: float32 [4096], P('ctx')
The draws below stay inside these ranges and needn't reach their ends.
Inputs may be any that keep to these rules, and one draw needn't show every extreme that they name: `half_lengths`: the halves add up to 4096 tokens, and the longest holds exactly 3072.
All inputs are finite; a program needn't handle non-finite values.
Results may differ from the reference program's by a relative error of at most 0.035.
Values may be sent and summed in bfloat16 or wider, within the bound.
No kernel may reach another device: no remote copies, remote signals or barrier semaphores. Data moves between devices by JAX's collectives and lax.ppermute only.
A program may use at most 192 MiB of HBM per device.

```python
import math
import jax
import jax.numpy as jnp
import numpy as np
from jax import lax

MODEL_DIMENSION = 5376
QUERY_HEADS = 32
KEY_VALUE_HEADS = 16
HEAD_SIZE = 128
WIN = 1024
TOK_DEV = 512
PACKED_TOKENS = 4096
SEGS = 4
LONGEST = 3072
REACH = 2
N_FSDP = 4


def draw_inputs(key, part):
    keys_list = jax.random.split(key, 3)
    row_scale = jnp.exp(jax.random.uniform(keys_list[0], (PACKED_TOKENS, 1), jnp.float32, 0.0, math.log(10.0)))
    rough_cols = jnp.exp(jax.random.uniform(keys_list[1], (1, MODEL_DIMENSION), jnp.float32, 0.0, math.log(3.0)))
    feature_frac = lax_free_ramp(MODEL_DIMENSION)
    low_end = 0.1
    gauss_base = jax.random.normal(keys_list[2], (PACKED_TOKENS, MODEL_DIMENSION), jnp.float32)
    rising = jnp.exp(math.log(low_end) + (math.log(3.0) - math.log(low_end)) * feature_frac)
    col_scale = rising * rough_cols
    gauss_base = jnp.clip(gauss_base, -4.0, 4.0)
    return (gauss_base * row_scale * col_scale).astype(jnp.bfloat16)


def lax_free_ramp(width_count):
    return (jnp.arange(width_count, dtype=jnp.float32) / float(max(width_count - 1, 1)))[None, :]


def shard_levels(key, shape, cuts, smallest, high):
    factor_of = 1.0
    for axis_at, blocks in cuts:
        draws = jax.random.uniform(jax.random.fold_in(jax.random.fold_in(key, 6), axis_at), (blocks,), jnp.float32, smallest / len(cuts), high / len(cuts))
        factor_of = factor_of * jnp.repeat(jnp.exp(draws), shape[axis_at] // blocks).reshape((-1,) + (1,) * (len(shape) - 1 - axis_at))
    return factor_of


def profile(count, total, most, lean):
    portions = [(1 << 20) // math.isqrt(rank ** lean) + 1 for rank in range(2, count + 1)]
    surplus, holding = total - most - (count - 1), [1] * (count - 1)
    while surplus > 0:
        candidates = [i for i in range(count - 1) if holding[i] < most]
        mass, budget = sum([portions[i] for i in candidates]), surplus
        for i in candidates:
            addition = min(most - holding[i], max(1, budget * portions[i] // mass), surplus)
            holding[i] = holding[i] + addition
            surplus = surplus - addition
    return np.array([most] + holding)


def uneven_parts(rng, count, total, reach, slope):
    if count == 2:
        one = jax.random.randint(rng, (), max(1, total - reach), min(reach, total - 1) + 1)
        return jnp.stack([one, total - one])
    sizes = jnp.asarray(profile(count, total, reach, slope), jnp.int32)
    couples = (count - 1) // 2
    source_of, sink = sizes[1:1 + 2 * couples:2], sizes[2:2 + 2 * couples:2]
    room = jnp.minimum(source_of - 1, reach - sink)
    shifted = jax.random.randint(jax.random.fold_in(rng, 1), (couples,), 0, 1 << 20) % (room + 1)
    sizes = sizes.at[1:1 + 2 * couples:2].set(source_of - shifted).at[2:2 + 2 * couples:2].set(sink + shifted)
    return sizes[jax.random.permutation(jax.random.fold_in(rng, 2), count)]


def centred(key, extent, spread, most, cuts=(), held_as=jnp.bfloat16):
    gain = shard_levels(key, extent, cuts, -0.22, 0.18) if cuts else 1.0
    result = jax.random.normal(key, extent, jnp.float32) * spread * gain
    return jnp.minimum(jnp.maximum(result, -most), most).astype(held_as)


def setup_inputs(seed: int = 0) -> dict:
    splits = jax.random.split(jax.random.key(seed), 10)
    inputs = draw_inputs(jax.random.fold_in(splits[9], 71), 0)
    output_cotangent = centred(splits[1], (PACKED_TOKENS, QUERY_HEADS * HEAD_SIZE), 16.0, 96.0, ((0, 8), (1, 4)))
    w_query = centred(splits[2], (MODEL_DIMENSION, QUERY_HEADS * HEAD_SIZE), MODEL_DIMENSION ** -0.5, 0.078125, ((0, 8), (1, 4)))
    key_projection = centred(splits[3], (MODEL_DIMENSION, KEY_VALUE_HEADS * HEAD_SIZE), MODEL_DIMENSION ** -0.5, 0.078125, ((0, 8), (1, 4)))
    value_projection = centred(splits[4], (MODEL_DIMENSION, KEY_VALUE_HEADS * HEAD_SIZE), MODEL_DIMENSION ** -0.5, 0.078125, ((0, 8), (1, 4)))
    norm_gain = jnp.clip(1.0 + 0.15 * jax.random.normal(splits[5], (MODEL_DIMENSION,), jnp.float32), 0.25, 1.75)
    q_gain = jnp.clip(1.0 + 0.15 * jax.random.normal(splits[6], (HEAD_SIZE,), jnp.float32), 0.25, 1.75)
    key_norm_gain = jnp.clip(1.0 + 0.15 * jax.random.normal(splits[7], (HEAD_SIZE,), jnp.float32), 0.25, 1.75)
    half_lengths = uneven_parts(splits[8], SEGS, PACKED_TOKENS, LONGEST, 2).astype(jnp.int32)
    return {"inputs": inputs, "output_cotangent": output_cotangent, "w_query": w_query, "key_projection": key_projection, "value_projection": value_projection, "norm_gain": norm_gain, "q_gain": q_gain, "key_norm_gain": key_norm_gain, "half_lengths": half_lengths}


epsilon = 1e-06
query_scale = 168.0 ** (-0.5)

def round_half(value_rows):
    return lax.optimization_barrier(value_rows.astype(jnp.bfloat16)).astype(jnp.float32)

def segment_of(half_lengths, positions):
    segment_ends = jnp.cumsum(half_lengths).astype(jnp.int32)
    return lax.optimization_barrier(jnp.sum((segment_ends[None, :] <= positions[:, None]).astype(jnp.int32), axis=1)).astype(jnp.int32)

def head_normalize(projected, head_count):
    shaped = projected.reshape(projected.shape[0], head_count, HEAD_SIZE)
    inverse = lax.rsqrt(lax.optimization_barrier(jnp.mean(shaped * shaped, axis=2, keepdims=True)) + epsilon)
    return (shaped * inverse, inverse)

def head_normalize_backward(upstream_grad, normal_part, inverse, gain_vector):
    upstream = upstream_grad * gain_vector
    return inverse * (upstream - normal_part * lax.optimization_barrier(jnp.mean(upstream * normal_part, axis=2, keepdims=True)))

def reference(inputs, output_cotangent, w_query, key_projection, value_projection, norm_gain, q_gain, key_norm_gain, half_lengths):
    queries_per_group = QUERY_HEADS // KEY_VALUE_HEADS
    window_reach_rows = REACH * TOK_DEV
    span_rows = window_reach_rows + TOK_DEV
    grad_scale = float(PACKED_TOKENS) ** (-0.5)
    widened = inputs.astype(jnp.float32)
    inv_rms = lax.rsqrt(lax.optimization_barrier(jnp.mean(widened * widened, axis=1, keepdims=True)) + epsilon)
    x_hat = widened * inv_rms
    normed = (x_hat * norm_gain).astype(jnp.bfloat16)
    q_raw = jnp.dot(normed, w_query, preferred_element_type=jnp.float32)
    key_unnormed = jnp.dot(normed, key_projection, preferred_element_type=jnp.float32)
    value_rows = jnp.dot(normed, value_projection, preferred_element_type=jnp.float32).astype(jnp.bfloat16)
    query_normalized, q_inverse = head_normalize(q_raw, QUERY_HEADS)
    key_normalized, key_inverse_rms = head_normalize(key_unnormed, KEY_VALUE_HEADS)
    query_multiplier = q_gain * query_scale
    query_rows = (query_normalized * query_multiplier).astype(jnp.bfloat16).reshape(PACKED_TOKENS, KEY_VALUE_HEADS, queries_per_group, HEAD_SIZE)
    key_rows = (key_normalized * key_norm_gain).astype(jnp.bfloat16)
    per_head_grads = output_cotangent.reshape(PACKED_TOKENS, KEY_VALUE_HEADS, queries_per_group, HEAD_SIZE)
    segments = segment_of(half_lengths, lax.iota(jnp.int32, PACKED_TOKENS))
    key_rows_padded = jnp.concatenate([jnp.zeros((window_reach_rows, KEY_VALUE_HEADS, HEAD_SIZE), jnp.bfloat16), key_rows], axis=0)
    value_rows_padded = jnp.concatenate([jnp.zeros((window_reach_rows, KEY_VALUE_HEADS, HEAD_SIZE), jnp.bfloat16), value_rows.reshape(PACKED_TOKENS, KEY_VALUE_HEADS, HEAD_SIZE)], axis=0)
    padded_segments = jnp.concatenate([jnp.zeros((window_reach_rows,), jnp.int32), segments], axis=0)

    def one_block(carry, block_index):
        acc_keys, acc_values = carry
        first_row = (block_index * TOK_DEV).astype(jnp.int32)
        block_q = lax.dynamic_slice_in_dim(query_rows, first_row, TOK_DEV, 0).astype(jnp.float32)
        block_grad = lax.dynamic_slice_in_dim(per_head_grads, first_row, TOK_DEV, 0).astype(jnp.float32)
        block_keys = lax.dynamic_slice_in_dim(key_rows_padded, first_row, span_rows, 0).astype(jnp.float32)
        block_values = lax.dynamic_slice_in_dim(value_rows_padded, first_row, span_rows, 0).astype(jnp.float32)
        query_pos = first_row + lax.iota(jnp.int32, TOK_DEV)
        key_pos = first_row - window_reach_rows + lax.iota(jnp.int32, span_rows)
        query_seg = lax.dynamic_slice_in_dim(segments, first_row, TOK_DEV, 0)
        key_seg = lax.dynamic_slice_in_dim(padded_segments, first_row, span_rows, 0)
        distance = query_pos[:, None] - key_pos[None, :]
        allowed = (query_seg[:, None] == key_seg[None, :]) & (distance >= 0) & (distance < WIN) & (key_pos[None, :] >= 0)
        scores = jnp.einsum('ikgd,jkd->kgij', block_q, block_keys)
        weights = jnp.where(allowed, jnp.exp(scores), 0.0)
        totals = lax.optimization_barrier(jnp.sum(weights, axis=3))
        numer = jnp.einsum('kgij,jkd->ikgd', round_half(weights), block_values)
        attn_out = numer / jnp.transpose(totals, (2, 0, 1))[..., None]
        delta = lax.optimization_barrier(jnp.sum(block_grad * attn_out, axis=3))
        probs = weights / totals[..., None]
        d_probs = jnp.einsum('ikgd,jkd->kgij', block_grad, block_values)
        d_scores = round_half(probs * (d_probs - jnp.transpose(delta, (1, 2, 0))[..., None]))
        d_query = jnp.einsum('kgij,jkd->ikgd', d_scores, block_keys)
        d_key = jnp.einsum('kgij,ikgd->jkd', d_scores, block_q)
        d_value = jnp.einsum('kgij,ikgd->jkd', round_half(probs), block_grad)
        acc_keys = lax.dynamic_update_slice_in_dim(acc_keys, lax.dynamic_slice_in_dim(acc_keys, first_row, span_rows, 0) + d_key, first_row, 0)
        acc_values = lax.dynamic_update_slice_in_dim(acc_values, lax.dynamic_slice_in_dim(acc_values, first_row, span_rows, 0) + d_value, first_row, 0)
        return ((acc_keys, acc_values), d_query)
    zeroed_accumulator = jnp.zeros((window_reach_rows + PACKED_TOKENS, KEY_VALUE_HEADS, HEAD_SIZE), jnp.float32)
    carried, d_query_blocks = lax.scan(one_block, (zeroed_accumulator, zeroed_accumulator), jnp.arange(PACKED_TOKENS // TOK_DEV, dtype=jnp.int32))
    d_queries = d_query_blocks.reshape(PACKED_TOKENS, QUERY_HEADS, HEAD_SIZE)
    key_grads = carried[0][window_reach_rows:]
    value_grads = carried[1][window_reach_rows:]
    dq16 = head_normalize_backward(d_queries, query_normalized, q_inverse, query_multiplier).reshape(PACKED_TOKENS, QUERY_HEADS * HEAD_SIZE).astype(jnp.bfloat16)
    key_grads_half16 = head_normalize_backward(key_grads, key_normalized, key_inverse_rms, key_norm_gain).reshape(PACKED_TOKENS, KEY_VALUE_HEADS * HEAD_SIZE).astype(jnp.bfloat16)
    value_grads_half16 = value_grads.reshape(PACKED_TOKENS, KEY_VALUE_HEADS * HEAD_SIZE).astype(jnp.bfloat16)
    q_group = QUERY_HEADS * HEAD_SIZE // N_FSDP
    key_value_group = KEY_VALUE_HEADS * HEAD_SIZE // N_FSDP
    d_normed = jnp.zeros((PACKED_TOKENS, MODEL_DIMENSION), jnp.float32)
    for group_index in range(N_FSDP):
        q_cols = slice(group_index * q_group, (group_index + 1) * q_group)
        kv_cols = slice(group_index * key_value_group, (group_index + 1) * key_value_group)
        term = jnp.dot(dq16[:, q_cols], w_query[:, q_cols].T, preferred_element_type=jnp.float32)
        term = term + jnp.dot(key_grads_half16[:, kv_cols], key_projection[:, kv_cols].T, preferred_element_type=jnp.float32)
        term = term + jnp.dot(value_grads_half16[:, kv_cols], value_projection[:, kv_cols].T, preferred_element_type=jnp.float32)
        d_normed = d_normed + round_half(term)
    upstream = d_normed * norm_gain
    row_dot = lax.optimization_barrier(jnp.sum(upstream * x_hat, axis=1, keepdims=True))
    grad_inputs = (inv_rms * (upstream - x_hat * row_dot / MODEL_DIMENSION)).astype(jnp.bfloat16)
    norm_row_dots = row_dot[:, 0] * float(MODEL_DIMENSION) ** (-0.5)

    def shard_grads(carry, shard_index):
        first_row = (shard_index * TOK_DEV).astype(jnp.int32)
        normed_block = lax.dynamic_slice_in_dim(normed, first_row, TOK_DEV, 0)
        query_term = round_half(grad_scale * jnp.dot(normed_block.T, lax.dynamic_slice_in_dim(dq16, first_row, TOK_DEV, 0), preferred_element_type=jnp.float32))
        key_term = round_half(grad_scale * jnp.dot(normed_block.T, lax.dynamic_slice_in_dim(key_grads_half16, first_row, TOK_DEV, 0), preferred_element_type=jnp.float32))
        value_term = round_half(grad_scale * jnp.dot(normed_block.T, lax.dynamic_slice_in_dim(value_grads_half16, first_row, TOK_DEV, 0), preferred_element_type=jnp.float32))
        gain_term = round_half(grad_scale * lax.optimization_barrier(jnp.sum(lax.dynamic_slice_in_dim(d_normed, first_row, TOK_DEV, 0) * lax.dynamic_slice_in_dim(x_hat, first_row, TOK_DEV, 0), axis=0)))
        return ((carry[0] + query_term, carry[1] + key_term, carry[2] + value_term, carry[3] + gain_term), None)
    initial_sums = (jnp.zeros((MODEL_DIMENSION, QUERY_HEADS * HEAD_SIZE), jnp.float32), jnp.zeros((MODEL_DIMENSION, KEY_VALUE_HEADS * HEAD_SIZE), jnp.float32), jnp.zeros((MODEL_DIMENSION, KEY_VALUE_HEADS * HEAD_SIZE), jnp.float32), jnp.zeros((MODEL_DIMENSION,), jnp.float32))
    sums, unused = lax.scan(shard_grads, initial_sums, jnp.arange(PACKED_TOKENS // TOK_DEV, dtype=jnp.int32))
    grad_q_gain = grad_scale * lax.optimization_barrier(jnp.sum(d_queries * query_normalized * query_scale, axis=(0, 1)))
    grad_k_gain = grad_scale * lax.optimization_barrier(jnp.sum(key_grads * key_normalized, axis=(0, 1)))
    return (grad_inputs, sums[0].astype(jnp.bfloat16), sums[1].astype(jnp.bfloat16), sums[2].astype(jnp.bfloat16), sums[3], grad_q_gain, grad_k_gain, norm_row_dots)
```

```python
import functools

import jax
import jax.numpy as jnp
from jax import lax
from jax.experimental import pallas as pl
from jax.experimental.pallas import tpu as pltpu
from jax.sharding import PartitionSpec as P

WIN = 1024
REACH = 2
BLOCKED = -1e30

epsilon = 1e-06
query_scale = 168.0 ** (-0.5)

NT = (((1,), (1,)), ((), ()))


def shift(value, axis, steps):
    count = lax.axis_size(axis)
    initial, last = (max(0, -steps), min(count, count - steps))
    return lax.ppermute(value, axis, [(s, s + steps) for s in range(initial, last)])


def swap(value, axis, flip):
    return lax.ppermute(value, axis, [(s, s ^ flip) for s in range(lax.axis_size(axis))])


def dot(a, b, dims=(((1,), (0,)), ((), ()))):
    return lax.dot_general(a, b, dims, preferred_element_type=jnp.float32)


def key_body(k_ref, v_ref, gain_ref, kv_ref):
    k = k_ref[...]
    inv = lax.rsqrt(jnp.mean(k * k, axis=1, keepdims=True) + epsilon)
    kv_ref[0] = (k * inv * gain_ref[...]).astype(jnp.bfloat16)
    kv_ref[1] = v_ref[...].astype(jnp.bfloat16)


def key_rows_of(projected, gain, kv_heads, head_dim):
    tokens = projected.shape[0]
    return pl.pallas_call(
        key_body,
        grid=(kv_heads,),
        in_specs=[
            pl.BlockSpec((tokens, head_dim), lambda g: (0, g)),
            pl.BlockSpec((tokens, head_dim), lambda g: (0, kv_heads + g)),
            pl.BlockSpec((1, head_dim), lambda g: (0, 0)),
        ],
        out_specs=pl.BlockSpec((2, tokens, head_dim), lambda g: (0, 0, g)),
        out_shape=jax.ShapeDtypeStruct((2, tokens, kv_heads * head_dim), jnp.bfloat16),
        name="key_rows",
    )(projected, projected, gain[None, :])


def key_grad_body(own_ref, near_ref, far_ref, k_ref, gain_ref, dk_ref, dv_ref, sum_ref):
    total = own_ref[...] + near_ref[...].astype(jnp.float32) + far_ref[...].astype(jnp.float32)
    k = k_ref[...]
    inv = lax.rsqrt(jnp.mean(k * k, axis=1, keepdims=True) + epsilon)
    k_hat = k * inv
    d = total[0]
    u = d * gain_ref[...]
    dk_ref[...] = (inv * (u - k_hat * jnp.mean(u * k_hat, axis=1, keepdims=True))).astype(
        jnp.bfloat16
    )
    dv_ref[...] = total[1].astype(jnp.bfloat16)

    @pl.when(pl.program_id(0) == 0)
    def _():
        sum_ref[...] = jnp.zeros_like(sum_ref)

    sum_ref[...] += jnp.sum(d * k_hat, axis=0, keepdims=True)


def key_grads_of(own, near, far, projected, gain, kv_heads, head_dim):
    tokens = projected.shape[0]
    stacked = pl.BlockSpec((2, tokens, head_dim), lambda g: (0, 0, g))
    flat = pl.BlockSpec((tokens, head_dim), lambda g: (0, g))
    row = pl.BlockSpec((1, head_dim), lambda g: (0, 0))
    half = jax.ShapeDtypeStruct((tokens, kv_heads * head_dim), jnp.bfloat16)
    return pl.pallas_call(
        key_grad_body,
        grid=(kv_heads,),
        in_specs=[stacked, stacked, stacked, flat, row],
        out_specs=(flat, flat, row),
        out_shape=(half, half, jax.ShapeDtypeStruct((1, head_dim), jnp.float32)),
        name="key_grads",
    )(own, near, far, projected, gain[None, :])


def attention_body(
    start_ref,
    ends_ref,
    q_ref,
    go_ref,
    own_ref,
    near_ref,
    far_ref,
    mult_ref,
    dq_ref,
    d_own_ref,
    d_near_ref,
    d_far_ref,
    sum_ref,
    bias_ref,
    k_ref,
    v_ref,
    kt_ref,
    vt_ref,
    dk_ref,
    dv_ref,
    *,
    rows,
    heads,
    segments,
):
    g = pl.program_id(0)
    s = pl.program_id(1)
    last = pl.num_programs(1) - 1
    tokens, head_dim = own_ref.shape[1:]
    reach = WIN
    span = reach + rows
    offset = pl.multiple_of(s * rows, rows)

    @pl.when(g == 0)
    def _():
        first = start_ref[0]
        key_pos = (first - reach + s * rows) + lax.broadcasted_iota(jnp.int32, (span, 1), 0)
        query_pos = (first + s * rows) + lax.broadcasted_iota(jnp.int32, (1, rows), 1)
        key_seg = jnp.zeros((span, 1), jnp.int32)
        query_seg = jnp.zeros((1, rows), jnp.int32)
        for i in range(segments):
            key_seg += (ends_ref[i] <= key_pos).astype(jnp.int32)
            query_seg += (ends_ref[i] <= query_pos).astype(jnp.int32)
        distance = query_pos - key_pos
        allowed = (
            (key_seg == query_seg) & (distance >= 0) & (distance < WIN) & (key_pos >= 0)
        )
        bias_ref[s] = jnp.where(allowed, 0.0, BLOCKED)

    @pl.when(s == 0)
    def _():
        for at, ref in enumerate((far_ref, near_ref, own_ref)):
            k_ref[pl.ds(at * tokens, tokens), :] = ref[0]
            v_ref[pl.ds(at * tokens, tokens), :] = ref[1]
        dk_ref[...] = jnp.zeros_like(dk_ref)
        dv_ref[...] = jnp.zeros_like(dv_ref)

    @pl.when((s == 0) & (g == 0))
    def _():
        sum_ref[...] = jnp.zeros_like(sum_ref)

    k = k_ref[pl.ds(offset, span), :]
    v = v_ref[pl.ds(offset, span), :]
    kt_ref[...] = jnp.transpose(k)
    vt_ref[...] = jnp.transpose(v)
    mult = mult_ref[...]
    bias = bias_ref[s]
    for h in range(heads):
        at = slice(h * head_dim, (h + 1) * head_dim)
        q = q_ref[:, at]
        inv = lax.rsqrt(jnp.mean(q * q, axis=1, keepdims=True) + epsilon)
        q_hat = q * inv
        q16 = (q_hat * mult).astype(jnp.bfloat16)
        go = go_ref[:, at]
        weights = jnp.exp(dot(k, q16, NT) + bias)
        over = 1.0 / jnp.sum(weights, axis=0, keepdims=True)
        out_t = dot(vt_ref[...], weights.astype(jnp.bfloat16)) * over
        delta = jnp.sum(jnp.transpose(go.astype(jnp.float32)) * out_t, axis=0, keepdims=True)
        probs = weights * over
        dv_ref[pl.ds(offset, span), :] += dot(probs.astype(jnp.bfloat16), go)
        d_scores = (probs * (dot(v, go, NT) - delta)).astype(jnp.bfloat16)
        dk_ref[pl.ds(offset, span), :] += dot(d_scores, q16)
        d_query = jnp.transpose(dot(kt_ref[...], d_scores))
        u = d_query * mult
        dq_ref[:, at] = (
            inv * (u - q_hat * jnp.mean(u * q_hat, axis=1, keepdims=True))
        ).astype(jnp.bfloat16)
        sum_ref[...] += jnp.sum(d_query * q_hat, axis=0, keepdims=True)

    @pl.when(s == last)
    def _():
        for at, ref in enumerate((d_far_ref, d_near_ref, d_own_ref)):
            ref[0] = dk_ref[pl.ds(at * tokens, tokens), :].astype(ref.dtype)
            ref[1] = dv_ref[pl.ds(at * tokens, tokens), :].astype(ref.dtype)


def attention(start, ends, q_raw, go, own, near, far, mult, kv_heads, head_dim):
    tokens, q_cols = q_raw.shape
    heads = q_cols // (kv_heads * head_dim)
    rows = min(256, tokens)
    steps = tokens // rows
    span = WIN + rows
    stacked = pl.BlockSpec((2, tokens, head_dim), lambda g, s, *_: (0, 0, g))
    by_query = pl.BlockSpec((rows, heads * head_dim), lambda g, s, *_: (s, g))
    row = pl.BlockSpec((1, head_dim), lambda g, s, *_: (0, 0))
    half = jax.ShapeDtypeStruct(own.shape, jnp.bfloat16)
    keys = WIN + tokens
    return pl.pallas_call(
        functools.partial(attention_body, rows=rows, heads=heads, segments=ends.shape[0]),
        grid_spec=pltpu.PrefetchScalarGridSpec(
            num_scalar_prefetch=2,
            grid=(kv_heads, steps),
            in_specs=[by_query, by_query, stacked, stacked, stacked, row],
            out_specs=(by_query, stacked, stacked, stacked, row),
            scratch_shapes=[
                pltpu.VMEM((steps, span, rows), jnp.float32),
                pltpu.VMEM((keys, head_dim), jnp.bfloat16),
                pltpu.VMEM((keys, head_dim), jnp.bfloat16),
                pltpu.VMEM((head_dim, span), jnp.bfloat16),
                pltpu.VMEM((head_dim, span), jnp.bfloat16),
                pltpu.VMEM((keys, head_dim), jnp.float32),
                pltpu.VMEM((keys, head_dim), jnp.float32),
            ],
        ),
        out_shape=(
            jax.ShapeDtypeStruct((tokens, q_cols), jnp.bfloat16),
            jax.ShapeDtypeStruct(own.shape, jnp.float32),
            half,
            half,
            jax.ShapeDtypeStruct((1, head_dim), jnp.float32),
        ),
        compiler_params=pltpu.CompilerParams(
            dimension_semantics=("arbitrary", "arbitrary"), vmem_limit_bytes=48 << 20
        ),
        name="attention",
    )(start, ends, q_raw, go, own, near, far, mult)


def on_device(
    inputs,
    output_cotangent,
    w_query,
    key_projection,
    value_projection,
    norm_gain,
    q_gain,
    key_norm_gain,
    half_lengths,
):
    tokens, model_width = inputs.shape
    head_dim = q_gain.shape[0]
    kv_cols = key_projection.shape[1]
    kv_heads = kv_cols // head_dim
    ctx_count = lax.axis_size("ctx")
    fsdp_count = lax.axis_size("fsdp")
    ctx_index = lax.axis_index("ctx")
    fsdp_index = lax.axis_index("fsdp")
    on_first_core = ctx_index % 2 == 0
    grad_scale = float(tokens * ctx_count) ** (-0.5)
    shard_rows = w_query.shape[0]
    features = model_width // fsdp_count

    key_value = jnp.concatenate([key_projection, value_projection], axis=1)
    wide_kv = lax.all_gather(key_value, "ctx", axis=0, tiled=True)
    wide_q = lax.all_gather(w_query, "ctx", axis=0, tiled=True)

    widened = inputs.astype(jnp.float32)
    inv_rms = lax.rsqrt(jnp.mean(widened * widened, axis=1, keepdims=True) + epsilon)
    x_hat = widened * inv_rms
    normed = (x_hat * norm_gain).astype(jnp.bfloat16)

    kv_raw = dot(normed, wide_kv)
    own = key_rows_of(kv_raw, key_norm_gain, kv_heads, head_dim)
    far = shift(own, "ctx", REACH)
    near = swap(jnp.where(on_first_core, own, far), "ctx", 1)

    q_raw = dot(normed, wide_q)
    query_multiplier = (q_gain * query_scale)[None, :]
    dq16, d_own, d_near, d_far, q_sum = attention(
        jnp.full((1,), ctx_index * tokens, jnp.int32),
        jnp.cumsum(half_lengths).astype(jnp.int32),
        q_raw,
        output_cotangent,
        own,
        near,
        far,
        query_multiplier,
        kv_heads,
        head_dim,
    )

    piece = shard_rows // fsdp_count
    blocks = jnp.transpose(normed).reshape(ctx_count, fsdp_count, piece, tokens)
    blocks = lax.dynamic_index_in_dim(blocks, fsdp_index, 1, keepdims=False)
    blocks, _ = lax.optimization_barrier((blocks, wide_q))
    blocks = lax.all_to_all(blocks, "ctx", 0, 0, tiled=True)
    blocks = jnp.transpose(blocks, (1, 0, 2)).reshape(piece, ctx_count * tokens)
    columns = lax.all_gather(blocks, "fsdp", axis=0, tiled=True)

    all_dq = lax.all_gather(dq16, "ctx", axis=0, tiled=True)

    crossed = swap(d_near, "ctx", 1)
    nothing = jnp.zeros_like(crossed)
    outgoing = d_far + jnp.where(on_first_core, nothing, crossed)
    returned = shift(outgoing, "ctx", -REACH)
    dk16, dv16, k_sum = key_grads_of(
        d_own,
        jnp.where(on_first_core, crossed, nothing),
        returned,
        kv_raw,
        key_norm_gain,
        kv_heads,
        head_dim,
    )
    dkv16 = jnp.concatenate([dk16, dv16], axis=1)
    all_dkv = lax.all_gather(dkv16, "ctx", axis=0, tiled=True)

    head_part = (dot(dq16, wide_q, NT) + dot(dkv16, wide_kv, NT)).astype(jnp.bfloat16)
    hat_gained = x_hat * norm_gain
    row_dot = lax.psum(
        jnp.sum(head_part.astype(jnp.float32) * hat_gained, axis=1, keepdims=True), "fsdp"
    )

    def part_for(index):
        return lax.dynamic_slice_in_dim(head_part, index * features, features, 1)

    d_mine = part_for(fsdp_index).astype(jnp.float32)
    for flip in range(1, fsdp_count):
        d_mine = d_mine + swap(part_for(fsdp_index ^ flip), "fsdp", flip).astype(jnp.float32)
    hat_mine = lax.dynamic_slice_in_dim(x_hat, fsdp_index * features, features, 1)
    gain_mine = lax.dynamic_slice_in_dim(norm_gain, fsdp_index * features, features, 0)
    upstream = d_mine * gain_mine
    grad_inputs = (inv_rms * (upstream - hat_mine * row_dot / model_width)).astype(jnp.bfloat16)
    norm_row_dots = row_dot[:, 0] * float(model_width) ** (-0.5)
    gain_term = grad_scale * jnp.sum(d_mine * hat_mine, axis=0)
    gain_sum = lax.psum_scatter(
        gain_term.astype(jnp.bfloat16), "ctx", scatter_dimension=0, tiled=True
    ).astype(jnp.float32)

    q_weights = (grad_scale * dot(columns, all_dq)).astype(jnp.bfloat16)
    k_weights = (grad_scale * dot(columns, all_dkv[:, :kv_cols])).astype(jnp.bfloat16)
    v_weights = (grad_scale * dot(columns, all_dkv[:, kv_cols:])).astype(jnp.bfloat16)

    grad_q_gain, grad_k_gain = lax.psum(
        (q_sum[0] * (grad_scale * query_scale), k_sum[0] * grad_scale), ("ctx", "fsdp")
    )
    return (
        grad_inputs,
        q_weights,
        k_weights,
        v_weights,
        gain_sum,
        grad_q_gain,
        grad_k_gain,
        norm_row_dots,
    )


def solution(mesh):
    placed = (
        P("ctx", None),
        P("ctx", "fsdp"),
        P("ctx", "fsdp"),
        P("ctx", "fsdp"),
        P("ctx", "fsdp"),
        P(),
        P(),
        P(),
        P(),
    )
    return jax.shard_map(
        on_device,
        mesh=mesh,
        in_specs=placed,
        out_specs=(
            P("ctx", "fsdp"),
            P("ctx", "fsdp"),
            P("ctx", "fsdp"),
            P("ctx", "fsdp"),
            P(("fsdp", "ctx")),
            P(),
            P(),
            P("ctx"),
        ),
        check_vma=False,
    )
```

```python
import functools

import jax
import jax.numpy as jnp
from jax import lax
from jax.experimental import pallas as pl
from jax.experimental.pallas import tpu as pltpu
from jax.sharding import PartitionSpec as P

WIN = 1024
REACH = 2
BLOCKED = -1e30

epsilon = 1e-06
query_scale = 168.0 ** (-0.5)

NT = (((1,), (1,)), ((), ()))


def shift(value, axis, steps):
    count = lax.axis_size(axis)
    initial, last = (max(0, -steps), min(count, count - steps))
    return lax.ppermute(value, axis, [(s, s + steps) for s in range(initial, last)])


def swap(value, axis, flip):
    return lax.ppermute(value, axis, [(s, s ^ flip) for s in range(lax.axis_size(axis))])


def dot(a, b, dims=(((1,), (0,)), ((), ()))):
    return lax.dot_general(a, b, dims, preferred_element_type=jnp.float32)


def everywhere(value, axes):
    for axis in axes:
        flip = 1
        while flip < lax.axis_size(axis):
            value = value + swap(value, axis, flip)
            flip *= 2
    return value


def start_columns(normed_turned, gate, shard_rows):
    chips = lax.axis_size("ctx") // 2
    chip = lax.axis_index("ctx") // 2
    shares = lax.axis_size("fsdp")
    piece = shard_rows // shares
    tokens = normed_turned.shape[1]
    blocks = normed_turned.reshape(chips, 2, shares, piece, tokens)
    blocks = lax.dynamic_index_in_dim(blocks, lax.axis_index("fsdp"), 2, keepdims=False)
    blocks, _ = lax.optimization_barrier((blocks, gate))
    return [
        (lambda part, m: swap(part, "ctx", 2 * m) if m else part)(
            lax.dynamic_index_in_dim(blocks, chip ^ m, 0, keepdims=False), m
        )
        for m in range(chips)
    ]


def finish_columns(pieces, gate):
    chips = len(pieces)
    chip = lax.axis_index("ctx") // 2
    core = lax.axis_index("ctx") % 2
    shares = lax.axis_size("fsdp")
    share = lax.axis_index("fsdp")
    pieces, _ = lax.optimization_barrier((jnp.stack(pieces), gate))
    piece, tokens = pieces.shape[2:]
    kept = lax.dynamic_index_in_dim(pieces, core, 1, keepdims=False)
    other = swap(lax.dynamic_index_in_dim(pieces, 1 - core, 1, keepdims=False), "ctx", 1)
    first, second = jnp.where(core == 0, kept, other), jnp.where(core == 0, other, kept)
    both = jnp.stack([first, second], axis=1)
    bit = 1
    while bit < chips:
        grouped = both.reshape(chips // (2 * bit), 2, bit, 2, piece, tokens)
        both = jnp.where((chip & bit) > 0, grouped[:, ::-1], grouped).reshape(both.shape)
        bit *= 2
    mine = jnp.transpose(both, (2, 0, 1, 3)).reshape(piece, chips * 2 * tokens)
    columns = jnp.zeros((shares,) + mine.shape, mine.dtype)
    columns = lax.dynamic_update_index_in_dim(columns, mine, share, 0)
    for m in range(1, shares):
        columns = lax.dynamic_update_index_in_dim(
            columns, swap(mine, "fsdp", m), share ^ m, 0
        )
    return columns.reshape(shares * piece, chips * 2 * tokens)


def key_body(k_ref, v_ref, gain_ref, kv_ref):
    k = k_ref[...]
    inv = lax.rsqrt(jnp.mean(k * k, axis=1, keepdims=True) + epsilon)
    kv_ref[0] = (k * inv * gain_ref[...]).astype(jnp.bfloat16)
    kv_ref[1] = v_ref[...].astype(jnp.bfloat16)


def key_rows_of(projected, gain, kv_heads, head_dim):
    tokens = projected.shape[0]
    return pl.pallas_call(
        key_body,
        grid=(kv_heads,),
        in_specs=[
            pl.BlockSpec((tokens, head_dim), lambda g: (0, g)),
            pl.BlockSpec((tokens, head_dim), lambda g: (0, kv_heads + g)),
            pl.BlockSpec((1, head_dim), lambda g: (0, 0)),
        ],
        out_specs=pl.BlockSpec((2, tokens, head_dim), lambda g: (0, 0, g)),
        out_shape=jax.ShapeDtypeStruct((2, tokens, kv_heads * head_dim), jnp.bfloat16),
        name="key_rows",
    )(projected, projected, gain[None, :])


def key_grad_body(own_ref, near_ref, far_ref, k_ref, gain_ref, dk_ref, dv_ref, sum_ref):
    total = own_ref[...] + near_ref[...].astype(jnp.float32) + far_ref[...].astype(jnp.float32)
    k = k_ref[...]
    inv = lax.rsqrt(jnp.mean(k * k, axis=1, keepdims=True) + epsilon)
    k_hat = k * inv
    d = total[0]
    u = d * gain_ref[...]
    dk_ref[...] = (inv * (u - k_hat * jnp.mean(u * k_hat, axis=1, keepdims=True))).astype(
        jnp.bfloat16
    )
    dv_ref[...] = total[1].astype(jnp.bfloat16)

    @pl.when(pl.program_id(0) == 0)
    def _():
        sum_ref[...] = jnp.zeros_like(sum_ref)

    sum_ref[...] += jnp.sum(d * k_hat, axis=0, keepdims=True)


def key_grads_of(own, near, far, projected, gain, kv_heads, head_dim):
    tokens = projected.shape[0]
    stacked = pl.BlockSpec((2, tokens, head_dim), lambda g: (0, 0, g))
    flat = pl.BlockSpec((tokens, head_dim), lambda g: (0, g))
    row = pl.BlockSpec((1, head_dim), lambda g: (0, 0))
    half = jax.ShapeDtypeStruct((tokens, kv_heads * head_dim), jnp.bfloat16)
    return pl.pallas_call(
        key_grad_body,
        grid=(kv_heads,),
        in_specs=[stacked, stacked, stacked, flat, row],
        out_specs=(flat, flat, row),
        out_shape=(half, half, jax.ShapeDtypeStruct((1, head_dim), jnp.float32)),
        name="key_grads",
    )(own, near, far, projected, gain[None, :])


def attention_body(
    start_ref,
    ends_ref,
    q_ref,
    go_ref,
    own_ref,
    near_ref,
    far_ref,
    mult_ref,
    dq_ref,
    d_own_ref,
    d_near_ref,
    d_far_ref,
    sum_ref,
    bias_ref,
    k_ref,
    v_ref,
    kt_ref,
    vt_ref,
    dk_ref,
    dv_ref,
    *,
    rows,
    heads,
    segments,
):
    g = pl.program_id(0)
    s = pl.program_id(1)
    last = pl.num_programs(1) - 1
    tokens, head_dim = own_ref.shape[1:]
    reach = WIN
    span = reach + rows
    offset = pl.multiple_of(s * rows, rows)

    @pl.when(g == 0)
    def _():
        first = start_ref[0]
        key_pos = (first - reach + s * rows) + lax.broadcasted_iota(jnp.int32, (span, 1), 0)
        query_pos = (first + s * rows) + lax.broadcasted_iota(jnp.int32, (1, rows), 1)
        key_seg = jnp.zeros((span, 1), jnp.int32)
        query_seg = jnp.zeros((1, rows), jnp.int32)
        for i in range(segments):
            key_seg += (ends_ref[i] <= key_pos).astype(jnp.int32)
            query_seg += (ends_ref[i] <= query_pos).astype(jnp.int32)
        distance = query_pos - key_pos
        allowed = (
            (key_seg == query_seg) & (distance >= 0) & (distance < WIN) & (key_pos >= 0)
        )
        bias_ref[s] = jnp.where(allowed, 0.0, BLOCKED)

    @pl.when(s == 0)
    def _():
        for at, ref in enumerate((far_ref, near_ref, own_ref)):
            k_ref[pl.ds(at * tokens, tokens), :] = ref[0]
            v_ref[pl.ds(at * tokens, tokens), :] = ref[1]
        dk_ref[...] = jnp.zeros_like(dk_ref)
        dv_ref[...] = jnp.zeros_like(dv_ref)

    @pl.when((s == 0) & (g == 0))
    def _():
        sum_ref[...] = jnp.zeros_like(sum_ref)

    k = k_ref[pl.ds(offset, span), :]
    v = v_ref[pl.ds(offset, span), :]
    kt_ref[...] = jnp.transpose(k)
    vt_ref[...] = jnp.transpose(v)
    mult = mult_ref[...]
    bias = bias_ref[s]
    for h in range(heads):
        at = slice(h * head_dim, (h + 1) * head_dim)
        q = q_ref[:, at]
        inv = lax.rsqrt(jnp.mean(q * q, axis=1, keepdims=True) + epsilon)
        q_hat = q * inv
        q16 = (q_hat * mult).astype(jnp.bfloat16)
        go = go_ref[:, at]
        weights = jnp.exp(dot(k, q16, NT) + bias)
        over = 1.0 / jnp.sum(weights, axis=0, keepdims=True)
        out_t = dot(vt_ref[...], weights.astype(jnp.bfloat16)) * over
        delta = jnp.sum(jnp.transpose(go.astype(jnp.float32)) * out_t, axis=0, keepdims=True)
        probs = weights * over
        dv_ref[pl.ds(offset, span), :] += dot(probs.astype(jnp.bfloat16), go)
        d_scores = (probs * (dot(v, go, NT) - delta)).astype(jnp.bfloat16)
        dk_ref[pl.ds(offset, span), :] += dot(d_scores, q16)
        d_query = jnp.transpose(dot(kt_ref[...], d_scores))
        u = d_query * mult
        dq_ref[:, at] = (
            inv * (u - q_hat * jnp.mean(u * q_hat, axis=1, keepdims=True))
        ).astype(jnp.bfloat16)
        sum_ref[...] += jnp.sum(d_query * q_hat, axis=0, keepdims=True)

    @pl.when(s == last)
    def _():
        for at, ref in enumerate((d_far_ref, d_near_ref, d_own_ref)):
            ref[0] = dk_ref[pl.ds(at * tokens, tokens), :].astype(ref.dtype)
            ref[1] = dv_ref[pl.ds(at * tokens, tokens), :].astype(ref.dtype)


def attention(start, ends, q_raw, go, own, near, far, mult, kv_heads, head_dim):
    tokens, q_cols = q_raw.shape
    heads = q_cols // (kv_heads * head_dim)
    rows = min(256, tokens)
    steps = tokens // rows
    span = WIN + rows
    stacked = pl.BlockSpec((2, tokens, head_dim), lambda g, s, *_: (0, 0, g))
    by_query = pl.BlockSpec((rows, heads * head_dim), lambda g, s, *_: (s, g))
    row = pl.BlockSpec((1, head_dim), lambda g, s, *_: (0, 0))
    half = jax.ShapeDtypeStruct(own.shape, jnp.bfloat16)
    keys = WIN + tokens
    return pl.pallas_call(
        functools.partial(attention_body, rows=rows, heads=heads, segments=ends.shape[0]),
        grid_spec=pltpu.PrefetchScalarGridSpec(
            num_scalar_prefetch=2,
            grid=(kv_heads, steps),
            in_specs=[by_query, by_query, stacked, stacked, stacked, row],
            out_specs=(by_query, stacked, stacked, stacked, row),
            scratch_shapes=[
                pltpu.VMEM((steps, span, rows), jnp.float32),
                pltpu.VMEM((keys, head_dim), jnp.bfloat16),
                pltpu.VMEM((keys, head_dim), jnp.bfloat16),
                pltpu.VMEM((head_dim, span), jnp.bfloat16),
                pltpu.VMEM((head_dim, span), jnp.bfloat16),
                pltpu.VMEM((keys, head_dim), jnp.float32),
                pltpu.VMEM((keys, head_dim), jnp.float32),
            ],
        ),
        out_shape=(
            jax.ShapeDtypeStruct((tokens, q_cols), jnp.bfloat16),
            jax.ShapeDtypeStruct(own.shape, jnp.float32),
            half,
            half,
            jax.ShapeDtypeStruct((1, head_dim), jnp.float32),
        ),
        compiler_params=pltpu.CompilerParams(
            dimension_semantics=("arbitrary", "arbitrary"), vmem_limit_bytes=48 << 20
        ),
        name="attention",
    )(start, ends, q_raw, go, own, near, far, mult)


def on_device(
    inputs,
    output_cotangent,
    w_query,
    key_projection,
    value_projection,
    norm_gain,
    q_gain,
    key_norm_gain,
    half_lengths,
):
    tokens, model_width = inputs.shape
    head_dim = q_gain.shape[0]
    kv_cols = key_projection.shape[1]
    kv_heads = kv_cols // head_dim
    ctx_count = lax.axis_size("ctx")
    fsdp_count = lax.axis_size("fsdp")
    ctx_index = lax.axis_index("ctx")
    fsdp_index = lax.axis_index("fsdp")
    on_first_core = ctx_index % 2 == 0
    grad_scale = float(tokens * ctx_count) ** (-0.5)
    shard_rows = w_query.shape[0]
    features = model_width // fsdp_count

    key_value = jnp.concatenate([key_projection, value_projection], axis=1)
    wide_kv = lax.all_gather(key_value, "ctx", axis=0, tiled=True)
    wide_q = lax.all_gather(w_query, "ctx", axis=0, tiled=True)

    widened = inputs.astype(jnp.float32)
    turned = jnp.transpose(inputs)
    inv_rms = lax.rsqrt(jnp.mean(widened * widened, axis=1, keepdims=True) + epsilon)
    x_hat = widened * inv_rms
    normed = (x_hat * norm_gain).astype(jnp.bfloat16)
    inv_row = jnp.transpose(inv_rms)

    kv_raw = dot(normed, wide_kv)
    own = key_rows_of(kv_raw, key_norm_gain, kv_heads, head_dim)
    far = shift(own, "ctx", REACH)
    near = swap(jnp.where(on_first_core, own, far), "ctx", 1)

    normed_turned = (turned.astype(jnp.float32) * inv_row * norm_gain[:, None]).astype(
        jnp.bfloat16
    )
    pieces = start_columns(normed_turned, wide_q, shard_rows)
    q_raw = dot(normed, wide_q)
    query_multiplier = (q_gain * query_scale)[None, :]
    dq16, d_own, d_near, d_far, q_sum = attention(
        jnp.full((1,), ctx_index * tokens, jnp.int32),
        jnp.cumsum(half_lengths).astype(jnp.int32),
        q_raw,
        output_cotangent,
        own,
        near,
        far,
        query_multiplier,
        kv_heads,
        head_dim,
    )

    all_dq = lax.all_gather(dq16, "ctx", axis=0, tiled=True)

    crossed = swap(d_near, "ctx", 1)
    nothing = jnp.zeros_like(crossed)
    outgoing = d_far + jnp.where(on_first_core, nothing, crossed)
    returned = shift(outgoing, "ctx", -REACH)
    query_part = lax.optimization_barrier(dot(wide_q, dq16, NT))
    dk16, dv16, k_sum = key_grads_of(
        d_own,
        jnp.where(on_first_core, crossed, nothing),
        returned,
        kv_raw,
        key_norm_gain,
        kv_heads,
        head_dim,
    )
    dkv16 = jnp.concatenate([dk16, dv16], axis=1)
    all_dkv = lax.all_gather(dkv16, "ctx", axis=0, tiled=True)

    columns = finish_columns(pieces, dq16)

    head_part = (query_part + dot(wide_kv, dkv16, NT)).astype(jnp.bfloat16)
    row_dot = everywhere(
        jnp.sum(
            head_part.astype(jnp.float32) * (turned.astype(jnp.float32) * norm_gain[:, None]),
            axis=0,
            keepdims=True,
        )
        * inv_row,
        ("fsdp",),
    )

    def part_of(array, index):
        return lax.dynamic_slice_in_dim(array, index * features, features, 0)

    sent = [swap(part_of(head_part, fsdp_index ^ m), "fsdp", m) for m in range(1, fsdp_count)]
    d_mine = part_of(head_part, fsdp_index).astype(jnp.float32)
    for part in sent:
        d_mine = d_mine + part.astype(jnp.float32)
    hat_mine = part_of(turned, fsdp_index).astype(jnp.float32) * inv_row
    upstream = d_mine * part_of(norm_gain, fsdp_index)[:, None]
    grad_inputs = jnp.transpose(
        (inv_row * (upstream - hat_mine * row_dot / model_width)).astype(jnp.bfloat16)
    )
    norm_row_dots = row_dot[0] * float(model_width) ** (-0.5)
    gain_term = grad_scale * jnp.sum(d_mine * hat_mine, axis=1)
    gain_sum = lax.dynamic_slice_in_dim(
        everywhere(gain_term, ("ctx",)),
        ctx_index * (features // ctx_count),
        features // ctx_count,
        0,
    )

    q_weights = (grad_scale * dot(columns, all_dq)).astype(jnp.bfloat16)
    k_weights = (grad_scale * dot(columns, all_dkv[:, :kv_cols])).astype(jnp.bfloat16)
    v_weights = (grad_scale * dot(columns, all_dkv[:, kv_cols:])).astype(jnp.bfloat16)

    gains = everywhere(
        jnp.concatenate([q_sum * (grad_scale * query_scale), k_sum * grad_scale], axis=0),
        ("fsdp", "ctx"),
    )
    return (
        grad_inputs,
        q_weights,
        k_weights,
        v_weights,
        gain_sum,
        gains[0],
        gains[1],
        norm_row_dots,
    )


def solution(mesh):
    placed = (
        P("ctx", None),
        P("ctx", "fsdp"),
        P("ctx", "fsdp"),
        P("ctx", "fsdp"),
        P("ctx", "fsdp"),
        P(),
        P(),
        P(),
        P(),
    )
    return jax.shard_map(
        on_device,
        mesh=mesh,
        in_specs=placed,
        out_specs=(
            P("ctx", "fsdp"),
            P("ctx", "fsdp"),
            P("ctx", "fsdp"),
            P("ctx", "fsdp"),
            P(("fsdp", "ctx")),
            P(),
            P(),
            P("ctx"),
        ),
        check_vma=False,
    )
```

```python
import functools

import jax
import jax.numpy as jnp
from jax import lax
from jax.experimental import pallas as pl
from jax.experimental.pallas import tpu as pltpu
from jax.sharding import PartitionSpec as P


WIN = 1024
REACH = 2
BLOCKED = -1e30

epsilon = 1e-06
query_scale = 168.0 ** (-0.5)

NT = (((1,), (1,)), ((), ()))


def shift(value, axis, steps):
    count = lax.axis_size(axis)
    initial, last = (max(0, -steps), min(count, count - steps))
    return lax.ppermute(value, axis, [(s, s + steps) for s in range(initial, last)])


def swap(value, axis, flip):
    return lax.ppermute(value, axis, [(s, s ^ flip) for s in range(lax.axis_size(axis))])


def dot(a, b, dims=(((1,), (0,)), ((), ()))):
    return lax.dot_general(a, b, dims, preferred_element_type=jnp.float32)


def everywhere(value, axes):
    for axis in axes:
        flip = 1
        while flip < lax.axis_size(axis):
            value = value + swap(value, axis, flip)
            flip *= 2
    return value


def share_of_columns(normed_turned, shard_rows):
    chips = lax.axis_size("ctx") // 2
    shares = lax.axis_size("fsdp")
    tokens = normed_turned.shape[1]
    blocks = normed_turned.reshape(chips, 2, shares, shard_rows // shares, tokens)
    return lax.dynamic_index_in_dim(blocks, lax.axis_index("fsdp"), 2, keepdims=False)


def start_columns(blocks):
    chips = blocks.shape[0]
    chip = lax.axis_index("ctx") // 2
    pieces = []
    for m in range(chips):
        piece = lax.dynamic_index_in_dim(blocks, chip ^ m, 0, keepdims=False)
        if m:
            piece = swap(piece, "ctx", 2 * m)
        pieces.append(piece)
    return pieces


def finish_columns(pieces, gate):
    chips = len(pieces)
    chip = lax.axis_index("ctx") // 2
    core = lax.axis_index("ctx") % 2
    shares = lax.axis_size("fsdp")
    share = lax.axis_index("fsdp")
    pieces, _ = lax.optimization_barrier((jnp.stack(pieces), gate))
    piece, tokens = pieces.shape[2:]
    kept = lax.dynamic_index_in_dim(pieces, core, 1, keepdims=False)
    other = swap(lax.dynamic_index_in_dim(pieces, 1 - core, 1, keepdims=False), "ctx", 1)
    first, second = jnp.where(core == 0, kept, other), jnp.where(core == 0, other, kept)
    both = jnp.stack([first, second], axis=1)
    bit = 1
    while bit < chips:
        grouped = both.reshape(chips // (2 * bit), 2, bit, 2, piece, tokens)
        both = jnp.where((chip & bit) > 0, grouped[:, ::-1], grouped).reshape(both.shape)
        bit *= 2
    mine = jnp.transpose(both, (2, 0, 1, 3)).reshape(piece, chips * 2 * tokens)
    columns = jnp.zeros((shares,) + mine.shape, mine.dtype)
    columns = lax.dynamic_update_index_in_dim(columns, mine, share, 0)
    for m in range(1, shares):
        part = swap(mine, "fsdp", m)
        columns = lax.dynamic_update_index_in_dim(columns, part, share ^ m, 0)
    return columns.reshape(shares * piece, chips * 2 * tokens)


def key_body(k_ref, v_ref, gain_ref, kv_ref):
    k = k_ref[...]
    inv = lax.rsqrt(jnp.mean(k * k, axis=1, keepdims=True) + epsilon)
    kv_ref[0] = (k * inv * gain_ref[...]).astype(jnp.bfloat16)
    kv_ref[1] = v_ref[...].astype(jnp.bfloat16)


def key_rows_of(projected, gain, kv_heads, head_dim):
    tokens = projected.shape[0]
    return pl.pallas_call(
        key_body,
        grid=(kv_heads,),
        in_specs=[
            pl.BlockSpec((tokens, head_dim), lambda g: (0, g)),
            pl.BlockSpec((tokens, head_dim), lambda g: (0, kv_heads + g)),
            pl.BlockSpec((1, head_dim), lambda g: (0, 0)),
        ],
        out_specs=pl.BlockSpec((2, tokens, head_dim), lambda g: (0, 0, g)),
        out_shape=jax.ShapeDtypeStruct((2, tokens, kv_heads * head_dim), jnp.bfloat16),
        name="key_rows",
    )(projected, projected, gain[None, :])


def key_grad_body(own_ref, near_ref, far_ref, k_ref, gain_ref, dk_ref, dv_ref, sum_ref):
    total = own_ref[...] + near_ref[...].astype(jnp.float32) + far_ref[...].astype(jnp.float32)
    k = k_ref[...]
    inv = lax.rsqrt(jnp.mean(k * k, axis=1, keepdims=True) + epsilon)
    k_hat = k * inv
    d = total[0]
    u = d * gain_ref[...]
    dk_ref[...] = (inv * (u - k_hat * jnp.mean(u * k_hat, axis=1, keepdims=True))).astype(
        jnp.bfloat16
    )
    dv_ref[...] = total[1].astype(jnp.bfloat16)

    @pl.when(pl.program_id(0) == 0)
    def _():
        sum_ref[...] = jnp.zeros_like(sum_ref)

    sum_ref[...] += jnp.sum(d * k_hat, axis=0, keepdims=True)


def key_grads_of(own, near, far, projected, gain, kv_heads, head_dim):
    tokens = projected.shape[0]
    stacked = pl.BlockSpec((2, tokens, head_dim), lambda g: (0, 0, g))
    flat = pl.BlockSpec((tokens, head_dim), lambda g: (0, g))
    row = pl.BlockSpec((1, head_dim), lambda g: (0, 0))
    half = jax.ShapeDtypeStruct((tokens, kv_heads * head_dim), jnp.bfloat16)
    return pl.pallas_call(
        key_grad_body,
        grid=(kv_heads,),
        in_specs=[stacked, stacked, stacked, flat, row],
        out_specs=(flat, flat, row),
        out_shape=(half, half, jax.ShapeDtypeStruct((1, head_dim), jnp.float32)),
        name="key_grads",
    )(own, near, far, projected, gain[None, :])


def attention_body(
    start_ref,
    ends_ref,
    q_ref,
    go_ref,
    own_ref,
    near_ref,
    far_ref,
    mult_ref,
    dq_ref,
    d_own_ref,
    d_near_ref,
    d_far_ref,
    sum_ref,
    bias_ref,
    k_ref,
    v_ref,
    kt_ref,
    vt_ref,
    dk_ref,
    dv_ref,
    *,
    rows,
    heads,
    segments,
):
    g = pl.program_id(0)
    s = pl.program_id(1)
    last = pl.num_programs(1) - 1
    tokens, head_dim = own_ref.shape[1:]
    reach = WIN
    span = reach + rows
    offset = pl.multiple_of(s * rows, rows)

    @pl.when(g == 0)
    def _():
        first = start_ref[0]
        key_pos = (first - reach + s * rows) + lax.broadcasted_iota(jnp.int32, (span, 1), 0)
        query_pos = (first + s * rows) + lax.broadcasted_iota(jnp.int32, (1, rows), 1)
        key_seg = jnp.zeros((span, 1), jnp.int32)
        query_seg = jnp.zeros((1, rows), jnp.int32)
        for i in range(segments):
            key_seg += (ends_ref[i] <= key_pos).astype(jnp.int32)
            query_seg += (ends_ref[i] <= query_pos).astype(jnp.int32)
        distance = query_pos - key_pos
        allowed = (
            (key_seg == query_seg) & (distance >= 0) & (distance < WIN) & (key_pos >= 0)
        )
        bias_ref[s] = jnp.where(allowed, 0.0, BLOCKED)

    @pl.when(s == 0)
    def _():
        for at, ref in enumerate((far_ref, near_ref, own_ref)):
            k_ref[pl.ds(at * tokens, tokens), :] = ref[0]
            v_ref[pl.ds(at * tokens, tokens), :] = ref[1]
        dk_ref[...] = jnp.zeros_like(dk_ref)
        dv_ref[...] = jnp.zeros_like(dv_ref)

    @pl.when((s == 0) & (g == 0))
    def _():
        sum_ref[...] = jnp.zeros_like(sum_ref)

    k = k_ref[pl.ds(offset, span), :]
    v = v_ref[pl.ds(offset, span), :]
    kt_ref[...] = jnp.transpose(k)
    vt_ref[...] = jnp.transpose(v)
    mult = mult_ref[...]
    bias = bias_ref[s]
    for h in range(heads):
        at = slice(h * head_dim, (h + 1) * head_dim)
        q = q_ref[:, at]
        inv = lax.rsqrt(jnp.mean(q * q, axis=1, keepdims=True) + epsilon)
        q_hat = q * inv
        q16 = (q_hat * mult).astype(jnp.bfloat16)
        go = go_ref[:, at]
        weights = jnp.exp(dot(k, q16, NT) + bias)
        over = 1.0 / jnp.sum(weights, axis=0, keepdims=True)
        out_t = dot(vt_ref[...], weights.astype(jnp.bfloat16)) * over
        delta = jnp.sum(jnp.transpose(go.astype(jnp.float32)) * out_t, axis=0, keepdims=True)
        probs = weights * over
        dv_ref[pl.ds(offset, span), :] += dot(probs.astype(jnp.bfloat16), go)
        d_scores = (probs * (dot(v, go, NT) - delta)).astype(jnp.bfloat16)
        dk_ref[pl.ds(offset, span), :] += dot(d_scores, q16)
        d_query = jnp.transpose(dot(kt_ref[...], d_scores))
        u = d_query * mult
        dq_ref[:, at] = (
            inv * (u - q_hat * jnp.mean(u * q_hat, axis=1, keepdims=True))
        ).astype(jnp.bfloat16)
        sum_ref[...] += jnp.sum(d_query * q_hat, axis=0, keepdims=True)

    @pl.when(s == last)
    def _():
        for at, ref in enumerate((d_far_ref, d_near_ref, d_own_ref)):
            ref[0] = dk_ref[pl.ds(at * tokens, tokens), :].astype(ref.dtype)
            ref[1] = dv_ref[pl.ds(at * tokens, tokens), :].astype(ref.dtype)


def attention(start, ends, q_raw, go, own, near, far, mult, kv_heads, head_dim):
    tokens, q_cols = q_raw.shape
    heads = q_cols // (kv_heads * head_dim)
    rows = min(256, tokens)
    steps = tokens // rows
    span = WIN + rows
    stacked = pl.BlockSpec((2, tokens, head_dim), lambda g, s, *_: (0, 0, g))
    by_query = pl.BlockSpec((rows, heads * head_dim), lambda g, s, *_: (s, g))
    row = pl.BlockSpec((1, head_dim), lambda g, s, *_: (0, 0))
    half = jax.ShapeDtypeStruct(own.shape, jnp.bfloat16)
    keys = WIN + tokens
    return pl.pallas_call(
        functools.partial(attention_body, rows=rows, heads=heads, segments=ends.shape[0]),
        grid_spec=pltpu.PrefetchScalarGridSpec(
            num_scalar_prefetch=2,
            grid=(kv_heads, steps),
            in_specs=[by_query, by_query, stacked, stacked, stacked, row],
            out_specs=(by_query, stacked, stacked, stacked, row),
            scratch_shapes=[
                pltpu.VMEM((steps, span, rows), jnp.float32),
                pltpu.VMEM((keys, head_dim), jnp.bfloat16),
                pltpu.VMEM((keys, head_dim), jnp.bfloat16),
                pltpu.VMEM((head_dim, span), jnp.bfloat16),
                pltpu.VMEM((head_dim, span), jnp.bfloat16),
                pltpu.VMEM((keys, head_dim), jnp.float32),
                pltpu.VMEM((keys, head_dim), jnp.float32),
            ],
        ),
        out_shape=(
            jax.ShapeDtypeStruct((tokens, q_cols), jnp.bfloat16),
            jax.ShapeDtypeStruct(own.shape, jnp.float32),
            half,
            half,
            jax.ShapeDtypeStruct((1, head_dim), jnp.float32),
        ),
        compiler_params=pltpu.CompilerParams(
            dimension_semantics=("arbitrary", "arbitrary"), vmem_limit_bytes=48 << 20
        ),
        name="attention",
    )(start, ends, q_raw, go, own, near, far, mult)


def layer(
    inputs,
    output_cotangent,
    w_query,
    key_projection,
    value_projection,
    norm_gain,
    q_gain,
    key_norm_gain,
    half_lengths,
):
    tokens, model_width = inputs.shape
    head_dim = q_gain.shape[0]
    kv_cols = key_projection.shape[1]
    kv_heads = kv_cols // head_dim
    ctx_count = lax.axis_size("ctx")
    fsdp_count = lax.axis_size("fsdp")
    ctx_index = lax.axis_index("ctx")
    fsdp_index = lax.axis_index("fsdp")
    on_first_core = ctx_index % 2 == 0
    grad_scale = float(tokens * ctx_count) ** (-0.5)
    shard_rows = w_query.shape[0]
    features = model_width // fsdp_count

    key_value = jnp.concatenate([key_projection, value_projection], axis=1)
    wide_kv = lax.all_gather(key_value, "ctx", axis=0, tiled=True)
    wide_q = lax.all_gather(w_query, "ctx", axis=0, tiled=True)

    widened = inputs.astype(jnp.float32)
    turned = jnp.transpose(inputs)
    inv_rms = lax.rsqrt(jnp.mean(widened * widened, axis=1, keepdims=True) + epsilon)
    x_hat = widened * inv_rms
    normed = lax.optimization_barrier((x_hat * norm_gain).astype(jnp.bfloat16))
    inv_row = jnp.transpose(inv_rms)

    kv_raw = dot(normed, wide_kv)
    own = key_rows_of(kv_raw, key_norm_gain, kv_heads, head_dim)
    normed_turned = (turned.astype(jnp.float32) * inv_row * norm_gain[:, None]).astype(
        jnp.bfloat16
    )
    blocks, own = lax.optimization_barrier((share_of_columns(normed_turned, shard_rows), own))
    far = shift(own, "ctx", REACH)
    picked = jnp.where(on_first_core, own, far)
    near = swap(picked, "ctx", 1)

    blocks, _ = lax.optimization_barrier((blocks, wide_q))
    pieces = start_columns(blocks)
    q_raw = dot(normed, wide_q)
    query_multiplier = (q_gain * query_scale)[None, :]
    dq16, d_own, d_near, d_far, q_sum = attention(
        jnp.full((1,), ctx_index * tokens, jnp.int32),
        jnp.cumsum(half_lengths).astype(jnp.int32),
        q_raw,
        output_cotangent,
        own,
        near,
        far,
        query_multiplier,
        kv_heads,
        head_dim,
    )

    all_dq = lax.all_gather(dq16, "ctx", axis=0, tiled=True)

    crossed = swap(d_near, "ctx", 1)
    nothing = jnp.zeros_like(crossed)
    outgoing = d_far + jnp.where(on_first_core, nothing, crossed)
    returned = shift(outgoing, "ctx", -REACH)
    query_part = dot(wide_q, dq16, NT)
    query_part = lax.optimization_barrier(query_part)
    dk16, dv16, k_sum = key_grads_of(
        d_own,
        jnp.where(on_first_core, crossed, nothing),
        returned,
        kv_raw,
        key_norm_gain,
        kv_heads,
        head_dim,
    )
    dkv16 = jnp.concatenate([dk16, dv16], axis=1)
    all_dkv = lax.all_gather(dkv16, "ctx", axis=0, tiled=True)

    columns = finish_columns(pieces, dq16)

    head_part = (query_part + dot(wide_kv, dkv16, NT)).astype(jnp.bfloat16)
    row_dot = everywhere(
        jnp.sum(
            head_part.astype(jnp.float32) * (turned.astype(jnp.float32) * norm_gain[:, None]),
            axis=0,
            keepdims=True,
        )
        * inv_row,
        ("fsdp",),
    )

    def part_of(array, index):
        return lax.dynamic_slice_in_dim(array, index * features, features, 0)

    sent = [swap(part_of(head_part, fsdp_index ^ m), "fsdp", m) for m in range(1, fsdp_count)]
    d_mine = part_of(head_part, fsdp_index).astype(jnp.float32)
    for part in sent:
        d_mine = d_mine + part.astype(jnp.float32)
    hat_mine = part_of(turned, fsdp_index).astype(jnp.float32) * inv_row
    upstream = d_mine * part_of(norm_gain, fsdp_index)[:, None]
    grad_inputs = jnp.transpose(
        (inv_row * (upstream - hat_mine * row_dot / model_width)).astype(jnp.bfloat16)
    )
    norm_row_dots = row_dot[0] * float(model_width) ** (-0.5)
    gain_term = grad_scale * jnp.sum(d_mine * hat_mine, axis=1)
    gain_sum = lax.dynamic_slice_in_dim(
        everywhere(gain_term, ("ctx",)),
        ctx_index * (features // ctx_count),
        features // ctx_count,
        0,
    )

    q_weights = (grad_scale * dot(columns, all_dq)).astype(jnp.bfloat16)
    k_weights = (grad_scale * dot(columns, all_dkv[:, :kv_cols])).astype(jnp.bfloat16)
    v_weights = (grad_scale * dot(columns, all_dkv[:, kv_cols:])).astype(jnp.bfloat16)

    gains = everywhere(
        jnp.concatenate([q_sum * (grad_scale * query_scale), k_sum * grad_scale], axis=0),
        ("fsdp", "ctx"),
    )
    return (
        grad_inputs,
        q_weights,
        k_weights,
        v_weights,
        gain_sum,
        gains[0],
        gains[1],
        norm_row_dots,
    )


def solution(mesh):
    placed = (
        P("ctx", None),
        P("ctx", "fsdp"),
        P("ctx", "fsdp"),
        P("ctx", "fsdp"),
        P("ctx", "fsdp"),
        P(),
        P(),
        P(),
        P(),
    )
    return jax.shard_map(
        layer,
        mesh=mesh,
        in_specs=placed,
        out_specs=(
            P("ctx", "fsdp"),
            P("ctx", "fsdp"),
            P("ctx", "fsdp"),
            P("ctx", "fsdp"),
            P(("fsdp", "ctx")),
            P(),
            P(),
            P("ctx"),
        ),
        check_vma=False,
    )
```

```python
import functools

import jax
import jax.numpy as jnp
from jax import lax
from jax.experimental import pallas as pl
from jax.experimental.pallas import tpu as pltpu
from jax.sharding import PartitionSpec as P


WIN = 1024
REACH = 2
BLOCKED = -1e30

epsilon = 1e-06
query_scale = 168.0 ** (-0.5)

NT = (((1,), (1,)), ((), ()))


def shift(value, axis, steps):
    count = lax.axis_size(axis)
    initial, last = (max(0, -steps), min(count, count - steps))
    return lax.ppermute(value, axis, [(s, s + steps) for s in range(initial, last)])


def swap(value, axis, flip):
    return lax.ppermute(value, axis, [(s, s ^ flip) for s in range(lax.axis_size(axis))])


def dot(a, b, dims=(((1,), (0,)), ((), ()))):
    return lax.dot_general(a, b, dims, preferred_element_type=jnp.float32)


def everywhere(value, axes):
    for axis in axes:
        flip = 1
        while flip < lax.axis_size(axis):
            value = value + swap(value, axis, flip)
            flip *= 2
    return value


def share_of_columns(normed_turned, shard_rows):
    chips = lax.axis_size("ctx") // 2
    shares = lax.axis_size("fsdp")
    tokens = normed_turned.shape[1]
    blocks = normed_turned.reshape(chips, 2, shares, shard_rows // shares, tokens)
    return lax.dynamic_index_in_dim(blocks, lax.axis_index("fsdp"), 2, keepdims=False)


def start_columns(blocks):
    chips = blocks.shape[0]
    chip = lax.axis_index("ctx") // 2
    pieces = []
    for m in range(chips):
        piece = lax.dynamic_index_in_dim(blocks, chip ^ m, 0, keepdims=False)
        if m:
            piece = swap(piece, "ctx", 2 * m)
        pieces.append(piece)
    return pieces


def finish_columns(pieces, gate):
    chips = len(pieces)
    chip = lax.axis_index("ctx") // 2
    core = lax.axis_index("ctx") % 2
    shares = lax.axis_size("fsdp")
    share = lax.axis_index("fsdp")
    pieces, _ = lax.optimization_barrier((jnp.stack(pieces), gate))
    piece, tokens = pieces.shape[2:]
    kept = lax.dynamic_index_in_dim(pieces, core, 1, keepdims=False)
    other = lax.dynamic_index_in_dim(pieces, 1 - core, 1, keepdims=False)
    other = swap(other, "ctx", 1)
    first, second = jnp.where(core == 0, kept, other), jnp.where(core == 0, other, kept)
    both = jnp.stack([first, second], axis=1)
    bit = 1
    while bit < chips:
        grouped = both.reshape(chips // (2 * bit), 2, bit, 2, piece, tokens)
        both = jnp.where((chip & bit) > 0, grouped[:, ::-1], grouped).reshape(both.shape)
        bit *= 2
    mine = jnp.transpose(both, (2, 0, 1, 3)).reshape(piece, chips * 2 * tokens)
    columns = jnp.zeros((shares,) + mine.shape, mine.dtype)
    columns = lax.dynamic_update_index_in_dim(columns, mine, share, 0)
    for m in range(1, shares):
        part = swap(mine, "fsdp", m)
        columns = lax.dynamic_update_index_in_dim(columns, part, share ^ m, 0)
    return columns.reshape(shares * piece, chips * 2 * tokens)


def key_body(k_ref, v_ref, gain_ref, kv_ref):
    k = k_ref[...]
    inv = lax.rsqrt(jnp.mean(k * k, axis=1, keepdims=True) + epsilon)
    kv_ref[0] = (k * inv * gain_ref[...]).astype(jnp.bfloat16)
    kv_ref[1] = v_ref[...].astype(jnp.bfloat16)


def key_rows_of(projected, gain, kv_heads, head_dim):
    tokens = projected.shape[0]
    return pl.pallas_call(
        key_body,
        grid=(kv_heads,),
        in_specs=[
            pl.BlockSpec((tokens, head_dim), lambda g: (0, g)),
            pl.BlockSpec((tokens, head_dim), lambda g: (0, kv_heads + g)),
            pl.BlockSpec((1, head_dim), lambda g: (0, 0)),
        ],
        out_specs=pl.BlockSpec((2, tokens, head_dim), lambda g: (0, 0, g)),
        out_shape=jax.ShapeDtypeStruct((2, tokens, kv_heads * head_dim), jnp.bfloat16),
        name="key_rows",
    )(projected, projected, gain[None, :])


def key_grad_body(own_ref, near_ref, far_ref, k_ref, gain_ref, dk_ref, dv_ref, sum_ref):
    total = own_ref[...] + near_ref[...].astype(jnp.float32) + far_ref[...].astype(jnp.float32)
    k = k_ref[...]
    inv = lax.rsqrt(jnp.mean(k * k, axis=1, keepdims=True) + epsilon)
    k_hat = k * inv
    d = total[0]
    u = d * gain_ref[...]
    dk_ref[...] = (inv * (u - k_hat * jnp.mean(u * k_hat, axis=1, keepdims=True))).astype(
        jnp.bfloat16
    )
    dv_ref[...] = total[1].astype(jnp.bfloat16)

    @pl.when(pl.program_id(0) == 0)
    def _():
        sum_ref[...] = jnp.zeros_like(sum_ref)

    sum_ref[...] += jnp.sum(d * k_hat, axis=0, keepdims=True)


def key_grads_of(own, near, far, projected, gain, kv_heads, head_dim):
    tokens = projected.shape[0]
    stacked = pl.BlockSpec((2, tokens, head_dim), lambda g: (0, 0, g))
    flat = pl.BlockSpec((tokens, head_dim), lambda g: (0, g))
    row = pl.BlockSpec((1, head_dim), lambda g: (0, 0))
    half = jax.ShapeDtypeStruct((tokens, kv_heads * head_dim), jnp.bfloat16)
    return pl.pallas_call(
        key_grad_body,
        grid=(kv_heads,),
        in_specs=[stacked, stacked, stacked, flat, row],
        out_specs=(flat, flat, row),
        out_shape=(half, half, jax.ShapeDtypeStruct((1, head_dim), jnp.float32)),
        name="key_grads",
    )(own, near, far, projected, gain[None, :])


def attention_body(
    start_ref,
    ends_ref,
    q_ref,
    go_ref,
    own_ref,
    near_ref,
    far_ref,
    mult_ref,
    dq_ref,
    d_own_ref,
    d_near_ref,
    d_far_ref,
    sum_ref,
    bias_ref,
    k_ref,
    v_ref,
    kt_ref,
    vt_ref,
    dk_ref,
    dv_ref,
    *,
    rows,
    heads,
    segments,
):
    g = pl.program_id(0)
    s = pl.program_id(1)
    last = pl.num_programs(1) - 1
    tokens, head_dim = own_ref.shape[1:]
    reach = WIN
    span = reach + rows
    offset = pl.multiple_of(s * rows, rows)

    @pl.when(g == 0)
    def _():
        first = start_ref[0]
        key_pos = (first - reach + s * rows) + lax.broadcasted_iota(jnp.int32, (span, 1), 0)
        query_pos = (first + s * rows) + lax.broadcasted_iota(jnp.int32, (1, rows), 1)
        key_seg = jnp.zeros((span, 1), jnp.int32)
        query_seg = jnp.zeros((1, rows), jnp.int32)
        for i in range(segments):
            key_seg += (ends_ref[i] <= key_pos).astype(jnp.int32)
            query_seg += (ends_ref[i] <= query_pos).astype(jnp.int32)
        distance = query_pos - key_pos
        allowed = (
            (key_seg == query_seg) & (distance >= 0) & (distance < WIN) & (key_pos >= 0)
        )
        bias_ref[s] = jnp.where(allowed, 0.0, BLOCKED)

    @pl.when(s == 0)
    def _():
        for at, ref in enumerate((far_ref, near_ref, own_ref)):
            k_ref[pl.ds(at * tokens, tokens), :] = ref[0]
            v_ref[pl.ds(at * tokens, tokens), :] = ref[1]
        dk_ref[...] = jnp.zeros_like(dk_ref)
        dv_ref[...] = jnp.zeros_like(dv_ref)

    @pl.when((s == 0) & (g == 0))
    def _():
        sum_ref[...] = jnp.zeros_like(sum_ref)

    k = k_ref[pl.ds(offset, span), :]
    v = v_ref[pl.ds(offset, span), :]
    kt_ref[...] = jnp.transpose(k)
    vt_ref[...] = jnp.transpose(v)
    mult = mult_ref[...]
    bias = bias_ref[s]
    for h in range(heads):
        at = slice(h * head_dim, (h + 1) * head_dim)
        q = q_ref[:, at]
        inv = lax.rsqrt(jnp.mean(q * q, axis=1, keepdims=True) + epsilon)
        q_hat = q * inv
        q16 = (q_hat * mult).astype(jnp.bfloat16)
        go = go_ref[:, at]
        weights = jnp.exp(dot(k, q16, NT) + bias)
        over = 1.0 / jnp.sum(weights, axis=0, keepdims=True)
        out_t = dot(vt_ref[...], weights.astype(jnp.bfloat16)) * over
        delta = jnp.sum(jnp.transpose(go.astype(jnp.float32)) * out_t, axis=0, keepdims=True)
        probs = weights * over
        dv_ref[pl.ds(offset, span), :] += dot(probs.astype(jnp.bfloat16), go)
        d_scores = (probs * (dot(v, go, NT) - delta)).astype(jnp.bfloat16)
        dk_ref[pl.ds(offset, span), :] += dot(d_scores, q16)
        d_query = jnp.transpose(dot(kt_ref[...], d_scores))
        u = d_query * mult
        dq_ref[:, at] = (
            inv * (u - q_hat * jnp.mean(u * q_hat, axis=1, keepdims=True))
        ).astype(jnp.bfloat16)
        sum_ref[...] += jnp.sum(d_query * q_hat, axis=0, keepdims=True)

    @pl.when(s == last)
    def _():
        for at, ref in enumerate((d_far_ref, d_near_ref, d_own_ref)):
            ref[0] = dk_ref[pl.ds(at * tokens, tokens), :].astype(ref.dtype)
            ref[1] = dv_ref[pl.ds(at * tokens, tokens), :].astype(ref.dtype)


def attention(start, ends, q_raw, go, own, near, far, mult, kv_heads, head_dim):
    tokens, q_cols = q_raw.shape
    heads = q_cols // (kv_heads * head_dim)
    rows = min(256, tokens)
    steps = tokens // rows
    span = WIN + rows
    stacked = pl.BlockSpec((2, tokens, head_dim), lambda g, s, *_: (0, 0, g))
    by_query = pl.BlockSpec((rows, heads * head_dim), lambda g, s, *_: (s, g))
    row = pl.BlockSpec((1, head_dim), lambda g, s, *_: (0, 0))
    half = jax.ShapeDtypeStruct(own.shape, jnp.bfloat16)
    keys = WIN + tokens
    return pl.pallas_call(
        functools.partial(attention_body, rows=rows, heads=heads, segments=ends.shape[0]),
        grid_spec=pltpu.PrefetchScalarGridSpec(
            num_scalar_prefetch=2,
            grid=(kv_heads, steps),
            in_specs=[by_query, by_query, stacked, stacked, stacked, row],
            out_specs=(by_query, stacked, stacked, stacked, row),
            scratch_shapes=[
                pltpu.VMEM((steps, span, rows), jnp.float32),
                pltpu.VMEM((keys, head_dim), jnp.bfloat16),
                pltpu.VMEM((keys, head_dim), jnp.bfloat16),
                pltpu.VMEM((head_dim, span), jnp.bfloat16),
                pltpu.VMEM((head_dim, span), jnp.bfloat16),
                pltpu.VMEM((keys, head_dim), jnp.float32),
                pltpu.VMEM((keys, head_dim), jnp.float32),
            ],
        ),
        out_shape=(
            jax.ShapeDtypeStruct((tokens, q_cols), jnp.bfloat16),
            jax.ShapeDtypeStruct(own.shape, jnp.float32),
            half,
            half,
            jax.ShapeDtypeStruct((1, head_dim), jnp.float32),
        ),
        compiler_params=pltpu.CompilerParams(
            dimension_semantics=("arbitrary", "arbitrary"), vmem_limit_bytes=48 << 20
        ),
        name="attention",
    )(start, ends, q_raw, go, own, near, far, mult)


def layer(
    inputs,
    output_cotangent,
    w_query,
    key_projection,
    value_projection,
    norm_gain,
    q_gain,
    key_norm_gain,
    half_lengths,
):
    tokens, model_width = inputs.shape
    head_dim = q_gain.shape[0]
    kv_cols = key_projection.shape[1]
    kv_heads = kv_cols // head_dim
    ctx_count = lax.axis_size("ctx")
    fsdp_count = lax.axis_size("fsdp")
    ctx_index = lax.axis_index("ctx")
    fsdp_index = lax.axis_index("fsdp")
    on_first_core = ctx_index % 2 == 0
    grad_scale = float(tokens * ctx_count) ** (-0.5)
    shard_rows = w_query.shape[0]
    features = model_width // fsdp_count

    key_value = jnp.concatenate([key_projection, value_projection], axis=1)
    wide_kv = lax.all_gather(key_value, "ctx", axis=0, tiled=True)
    wide_q = lax.all_gather(w_query, "ctx", axis=0, tiled=True)

    widened = inputs.astype(jnp.float32)
    turned = jnp.transpose(inputs)
    inv_rms = lax.rsqrt(jnp.mean(widened * widened, axis=1, keepdims=True) + epsilon)
    x_hat = widened * inv_rms
    normed = lax.optimization_barrier((x_hat * norm_gain).astype(jnp.bfloat16))
    inv_row = jnp.transpose(inv_rms)

    kv_raw = dot(normed, wide_kv)
    own = key_rows_of(kv_raw, key_norm_gain, kv_heads, head_dim)
    normed_turned = (turned.astype(jnp.float32) * inv_row * norm_gain[:, None]).astype(
        jnp.bfloat16
    )
    blocks, own = lax.optimization_barrier((share_of_columns(normed_turned, shard_rows), own))
    far = shift(own, "ctx", REACH)
    picked = jnp.where(on_first_core, own, far)
    near = swap(picked, "ctx", 1)

    blocks, _ = lax.optimization_barrier((blocks, wide_q))
    pieces = start_columns(blocks)
    q_raw = dot(normed, wide_q)
    query_multiplier = (q_gain * query_scale)[None, :]
    dq16, d_own, d_near, d_far, q_sum = attention(
        jnp.full((1,), ctx_index * tokens, jnp.int32),
        jnp.cumsum(half_lengths).astype(jnp.int32),
        q_raw,
        output_cotangent,
        own,
        near,
        far,
        query_multiplier,
        kv_heads,
        head_dim,
    )

    crossed = swap(d_near, "ctx", 1)
    nothing = jnp.zeros_like(crossed)
    outgoing = d_far + jnp.where(on_first_core, nothing, crossed)
    returned = shift(outgoing, "ctx", -REACH)
    gated, returned = lax.optimization_barrier((dq16, returned))
    all_dq = lax.all_gather(gated, "ctx", axis=0, tiled=True)
    query_part = dot(wide_q, dq16, NT)
    query_part = lax.optimization_barrier(query_part)
    dk16, dv16, k_sum = key_grads_of(
        d_own,
        jnp.where(on_first_core, crossed, nothing),
        returned,
        kv_raw,
        key_norm_gain,
        kv_heads,
        head_dim,
    )
    dkv16 = jnp.concatenate([dk16, dv16], axis=1)
    all_dkv = lax.all_gather(dkv16, "ctx", axis=0, tiled=True)

    columns = finish_columns(pieces, dq16)

    head_part = (query_part + dot(wide_kv, dkv16, NT)).astype(jnp.bfloat16)
    row_dot = everywhere(
        jnp.sum(
            head_part.astype(jnp.float32) * (turned.astype(jnp.float32) * norm_gain[:, None]),
            axis=0,
            keepdims=True,
        )
        * inv_row,
        ("fsdp",),
    )

    def part_of(array, index):
        return lax.dynamic_slice_in_dim(array, index * features, features, 0)

    sent = [part_of(head_part, fsdp_index ^ m) for m in range(1, fsdp_count)]
    sent = [swap(part, "fsdp", 1 + m) for m, part in enumerate(sent)]
    d_mine = part_of(head_part, fsdp_index).astype(jnp.float32)
    for part in sent:
        d_mine = d_mine + part.astype(jnp.float32)
    hat_mine = part_of(turned, fsdp_index).astype(jnp.float32) * inv_row
    upstream = d_mine * part_of(norm_gain, fsdp_index)[:, None]
    grad_inputs = jnp.transpose(
        (inv_row * (upstream - hat_mine * row_dot / model_width)).astype(jnp.bfloat16)
    )
    norm_row_dots = row_dot[0] * float(model_width) ** (-0.5)
    gain_term = grad_scale * jnp.sum(d_mine * hat_mine, axis=1)
    gain_sum = lax.dynamic_slice_in_dim(
        everywhere(gain_term, ("ctx",)),
        ctx_index * (features // ctx_count),
        features // ctx_count,
        0,
    )

    q_weights = (grad_scale * dot(columns, all_dq)).astype(jnp.bfloat16)
    k_weights = (grad_scale * dot(columns, all_dkv[:, :kv_cols])).astype(jnp.bfloat16)
    v_weights = (grad_scale * dot(columns, all_dkv[:, kv_cols:])).astype(jnp.bfloat16)

    gains = jnp.concatenate([q_sum * (grad_scale * query_scale), k_sum * grad_scale], axis=0)
    gains = everywhere(gains, ("fsdp",))
    gains = everywhere(gains, ("ctx",))
    return (
        grad_inputs,
        q_weights,
        k_weights,
        v_weights,
        gain_sum,
        gains[0],
        gains[1],
        norm_row_dots,
    )


def solution(mesh):
    placed = (
        P("ctx", None),
        P("ctx", "fsdp"),
        P("ctx", "fsdp"),
        P("ctx", "fsdp"),
        P("ctx", "fsdp"),
        P(),
        P(),
        P(),
        P(),
    )
    return jax.shard_map(
        layer,
        mesh=mesh,
        in_specs=placed,
        out_specs=(
            P("ctx", "fsdp"),
            P("ctx", "fsdp"),
            P("ctx", "fsdp"),
            P("ctx", "fsdp"),
            P(("fsdp", "ctx")),
            P(),
            P(),
            P("ctx"),
        ),
        check_vma=False,
    )
```

```python
import functools

import jax
import jax.numpy as jnp
from jax import lax
from jax.experimental import pallas as pl
from jax.experimental.pallas import tpu as pltpu
from jax.sharding import PartitionSpec as P


WIN = 1024
REACH = 2
BLOCKED = -1e30

epsilon = 1e-06
query_scale = 168.0 ** (-0.5)

NT = (((1,), (1,)), ((), ()))


def shift(value, axis, steps):
    count = lax.axis_size(axis)
    initial, last = (max(0, -steps), min(count, count - steps))
    return lax.ppermute(value, axis, [(s, s + steps) for s in range(initial, last)])


def swap(value, axis, flip):
    return lax.ppermute(value, axis, [(s, s ^ flip) for s in range(lax.axis_size(axis))])


def dot(a, b, dims=(((1,), (0,)), ((), ()))):
    return lax.dot_general(a, b, dims, preferred_element_type=jnp.float32)


def everywhere(value, axes):
    for axis in axes:
        flip = 1
        while flip < lax.axis_size(axis):
            value = value + swap(value, axis, flip)
            flip *= 2
    return value


def share_of_columns(normed_turned, shard_rows):
    chips = lax.axis_size("ctx") // 2
    shares = lax.axis_size("fsdp")
    tokens = normed_turned.shape[1]
    blocks = normed_turned.reshape(chips, 2, shares, shard_rows // shares, tokens)
    return lax.dynamic_index_in_dim(blocks, lax.axis_index("fsdp"), 2, keepdims=False)


def pick_columns(blocks):
    chip = lax.axis_index("ctx") // 2
    return [
        lax.dynamic_index_in_dim(blocks, chip ^ m, 0, keepdims=False)
        for m in range(blocks.shape[0])
    ]


def start_columns(pieces):
    return pieces[:1] + [swap(piece, "ctx", 2 + 2 * m) for m, piece in enumerate(pieces[1:])]


def finish_columns(pieces, gate):
    chips = len(pieces)
    chip = lax.axis_index("ctx") // 2
    core = lax.axis_index("ctx") % 2
    shares = lax.axis_size("fsdp")
    share = lax.axis_index("fsdp")
    pieces, _ = lax.optimization_barrier((jnp.stack(pieces), gate))
    piece, tokens = pieces.shape[2:]
    kept = lax.dynamic_index_in_dim(pieces, core, 1, keepdims=False)
    other = lax.dynamic_index_in_dim(pieces, 1 - core, 1, keepdims=False)
    other = swap(other, "ctx", 1)
    first, second = jnp.where(core == 0, kept, other), jnp.where(core == 0, other, kept)
    both = jnp.stack([first, second], axis=1)
    bit = 1
    while bit < chips:
        grouped = both.reshape(chips // (2 * bit), 2, bit, 2, piece, tokens)
        both = jnp.where((chip & bit) > 0, grouped[:, ::-1], grouped).reshape(both.shape)
        bit *= 2
    mine = jnp.transpose(both, (2, 0, 1, 3)).reshape(piece, chips * 2 * tokens)
    columns = jnp.zeros((shares,) + mine.shape, mine.dtype)
    columns = lax.dynamic_update_index_in_dim(columns, mine, share, 0)
    for m in range(1, shares):
        part = swap(mine, "fsdp", m)
        columns = lax.dynamic_update_index_in_dim(columns, part, share ^ m, 0)
    return columns.reshape(shares * piece, chips * 2 * tokens)


def key_body(k_ref, v_ref, gain_ref, kv_ref):
    k = k_ref[...]
    inv = lax.rsqrt(jnp.mean(k * k, axis=1, keepdims=True) + epsilon)
    kv_ref[0] = (k * inv * gain_ref[...]).astype(jnp.bfloat16)
    kv_ref[1] = v_ref[...].astype(jnp.bfloat16)


def key_rows_of(projected, gain, kv_heads, head_dim):
    tokens = projected.shape[0]
    return pl.pallas_call(
        key_body,
        grid=(kv_heads,),
        in_specs=[
            pl.BlockSpec((tokens, head_dim), lambda g: (0, g)),
            pl.BlockSpec((tokens, head_dim), lambda g: (0, kv_heads + g)),
            pl.BlockSpec((1, head_dim), lambda g: (0, 0)),
        ],
        out_specs=pl.BlockSpec((2, tokens, head_dim), lambda g: (0, 0, g)),
        out_shape=jax.ShapeDtypeStruct((2, tokens, kv_heads * head_dim), jnp.bfloat16),
        name="key_rows",
    )(projected, projected, gain[None, :])


def key_grad_body(own_ref, near_ref, far_ref, k_ref, gain_ref, dk_ref, dv_ref, sum_ref):
    total = own_ref[...] + near_ref[...].astype(jnp.float32) + far_ref[...].astype(jnp.float32)
    k = k_ref[...]
    inv = lax.rsqrt(jnp.mean(k * k, axis=1, keepdims=True) + epsilon)
    k_hat = k * inv
    d = total[0]
    u = d * gain_ref[...]
    dk_ref[...] = (inv * (u - k_hat * jnp.mean(u * k_hat, axis=1, keepdims=True))).astype(
        jnp.bfloat16
    )
    dv_ref[...] = total[1].astype(jnp.bfloat16)

    @pl.when(pl.program_id(0) == 0)
    def _():
        sum_ref[...] = jnp.zeros_like(sum_ref)

    sum_ref[...] += jnp.sum(d * k_hat, axis=0, keepdims=True)


def key_grads_of(own, near, far, projected, gain, kv_heads, head_dim):
    tokens = projected.shape[0]
    stacked = pl.BlockSpec((2, tokens, head_dim), lambda g: (0, 0, g))
    flat = pl.BlockSpec((tokens, head_dim), lambda g: (0, g))
    row = pl.BlockSpec((1, head_dim), lambda g: (0, 0))
    half = jax.ShapeDtypeStruct((tokens, kv_heads * head_dim), jnp.bfloat16)
    return pl.pallas_call(
        key_grad_body,
        grid=(kv_heads,),
        in_specs=[stacked, stacked, stacked, flat, row],
        out_specs=(flat, flat, row),
        out_shape=(half, half, jax.ShapeDtypeStruct((1, head_dim), jnp.float32)),
        name="key_grads",
    )(own, near, far, projected, gain[None, :])


def attention_body(
    start_ref,
    ends_ref,
    q_ref,
    go_ref,
    own_ref,
    near_ref,
    far_ref,
    mult_ref,
    dq_ref,
    d_own_ref,
    d_near_ref,
    d_far_ref,
    sum_ref,
    bias_ref,
    k_ref,
    v_ref,
    kt_ref,
    vt_ref,
    dk_ref,
    dv_ref,
    *,
    rows,
    heads,
    segments,
):
    g = pl.program_id(0)
    s = pl.program_id(1)
    last = pl.num_programs(1) - 1
    tokens, head_dim = own_ref.shape[1:]
    reach = WIN
    span = reach + rows
    offset = pl.multiple_of(s * rows, rows)

    @pl.when(g == 0)
    def _():
        first = start_ref[0]
        key_pos = (first - reach + s * rows) + lax.broadcasted_iota(jnp.int32, (span, 1), 0)
        query_pos = (first + s * rows) + lax.broadcasted_iota(jnp.int32, (1, rows), 1)
        key_seg = jnp.zeros((span, 1), jnp.int32)
        query_seg = jnp.zeros((1, rows), jnp.int32)
        for i in range(segments):
            key_seg += (ends_ref[i] <= key_pos).astype(jnp.int32)
            query_seg += (ends_ref[i] <= query_pos).astype(jnp.int32)
        distance = query_pos - key_pos
        allowed = (
            (key_seg == query_seg) & (distance >= 0) & (distance < WIN) & (key_pos >= 0)
        )
        bias_ref[s] = jnp.where(allowed, 0.0, BLOCKED)

    @pl.when(s == 0)
    def _():
        for at, ref in enumerate((far_ref, near_ref, own_ref)):
            k_ref[pl.ds(at * tokens, tokens), :] = ref[0]
            v_ref[pl.ds(at * tokens, tokens), :] = ref[1]
        dk_ref[...] = jnp.zeros_like(dk_ref)
        dv_ref[...] = jnp.zeros_like(dv_ref)

    @pl.when((s == 0) & (g == 0))
    def _():
        sum_ref[...] = jnp.zeros_like(sum_ref)

    k = k_ref[pl.ds(offset, span), :]
    v = v_ref[pl.ds(offset, span), :]
    kt_ref[...] = jnp.transpose(k)
    vt_ref[...] = jnp.transpose(v)
    mult = mult_ref[...]
    bias = bias_ref[s]
    for h in range(heads):
        at = slice(h * head_dim, (h + 1) * head_dim)
        q = q_ref[:, at]
        inv = lax.rsqrt(jnp.mean(q * q, axis=1, keepdims=True) + epsilon)
        q_hat = q * inv
        q16 = (q_hat * mult).astype(jnp.bfloat16)
        go = go_ref[:, at]
        weights = jnp.exp(dot(k, q16, NT) + bias)
        over = 1.0 / jnp.sum(weights, axis=0, keepdims=True)
        out_t = dot(vt_ref[...], weights.astype(jnp.bfloat16)) * over
        delta = jnp.sum(jnp.transpose(go.astype(jnp.float32)) * out_t, axis=0, keepdims=True)
        probs = weights * over
        dv_ref[pl.ds(offset, span), :] += dot(probs.astype(jnp.bfloat16), go)
        d_scores = (probs * (dot(v, go, NT) - delta)).astype(jnp.bfloat16)
        dk_ref[pl.ds(offset, span), :] += dot(d_scores, q16)
        d_query = jnp.transpose(dot(kt_ref[...], d_scores))
        u = d_query * mult
        dq_ref[:, at] = (
            inv * (u - q_hat * jnp.mean(u * q_hat, axis=1, keepdims=True))
        ).astype(jnp.bfloat16)
        sum_ref[...] += jnp.sum(d_query * q_hat, axis=0, keepdims=True)

    @pl.when(s == last)
    def _():
        for at, ref in enumerate((d_far_ref, d_near_ref, d_own_ref)):
            ref[0] = dk_ref[pl.ds(at * tokens, tokens), :].astype(ref.dtype)
            ref[1] = dv_ref[pl.ds(at * tokens, tokens), :].astype(ref.dtype)


def attention_rest(start, ends, q, go, own, near, far, mult, *refs, **sizes):
    attention_body(start, ends, q, go, own, near, far, mult, *refs[3:], **sizes)


def attention(start, ends, q_raw, go, own, near, far, mult, kv_heads, head_dim, skip, carry):
    tokens, q_cols = q_raw.shape
    heads = q_cols // (kv_heads * head_dim)
    rows = min(256, tokens)
    steps = tokens // rows
    span = WIN + rows
    stacked = pl.BlockSpec((2, tokens, head_dim), lambda g, s, *_: (0, 0, skip + g))
    by_query = pl.BlockSpec((rows, heads * head_dim), lambda g, s, *_: (s, g))
    by_skipped = pl.BlockSpec((rows, heads * head_dim), lambda g, s, *_: (s, skip + g))
    whole = pl.BlockSpec(memory_space=pl.ANY)
    row = pl.BlockSpec((1, head_dim), lambda g, s, *_: (0, 0))
    half = jax.ShapeDtypeStruct(own.shape, jnp.bfloat16)
    keys = WIN + tokens
    return pl.pallas_call(
        functools.partial(
            attention_rest if carry else attention_body,
            rows=rows,
            heads=heads,
            segments=ends.shape[0],
        ),
        grid_spec=pltpu.PrefetchScalarGridSpec(
            num_scalar_prefetch=2,
            grid=(kv_heads, steps),
            in_specs=[by_query, by_skipped, stacked, stacked, stacked, row]
            + [whole for _ in carry],
            out_specs=(by_query, stacked, stacked, stacked, row),
            scratch_shapes=[
                pltpu.VMEM((steps, span, rows), jnp.float32),
                pltpu.VMEM((keys, head_dim), jnp.bfloat16),
                pltpu.VMEM((keys, head_dim), jnp.bfloat16),
                pltpu.VMEM((head_dim, span), jnp.bfloat16),
                pltpu.VMEM((head_dim, span), jnp.bfloat16),
                pltpu.VMEM((keys, head_dim), jnp.float32),
                pltpu.VMEM((keys, head_dim), jnp.float32),
            ],
        ),
        out_shape=(
            jax.ShapeDtypeStruct((tokens, q_cols), jnp.bfloat16),
            jax.ShapeDtypeStruct(own.shape, jnp.float32),
            half,
            half,
            jax.ShapeDtypeStruct((1, head_dim), jnp.float32),
        ),
        compiler_params=pltpu.CompilerParams(
            dimension_semantics=("arbitrary", "arbitrary"), vmem_limit_bytes=48 << 20
        ),
        input_output_aliases={8 + i: 1 + i for i in range(len(carry))},
        name="attention",
    )(start, ends, q_raw, go, own, near, far, mult, *carry)


def layer(
    inputs,
    output_cotangent,
    w_query,
    key_projection,
    value_projection,
    norm_gain,
    q_gain,
    key_norm_gain,
    half_lengths,
):
    tokens, model_width = inputs.shape
    head_dim = q_gain.shape[0]
    kv_cols = key_projection.shape[1]
    kv_heads = kv_cols // head_dim
    ctx_count = lax.axis_size("ctx")
    fsdp_count = lax.axis_size("fsdp")
    ctx_index = lax.axis_index("ctx")
    fsdp_index = lax.axis_index("fsdp")
    on_first_core = ctx_index % 2 == 0
    grad_scale = float(tokens * ctx_count) ** (-0.5)
    shard_rows = w_query.shape[0]
    features = model_width // fsdp_count

    key_value = jnp.concatenate([key_projection, value_projection], axis=1)
    wide_kv = lax.all_gather(key_value, "ctx", axis=0, tiled=True)
    half = w_query.shape[1] // 2
    wide_qa = lax.all_gather(w_query[:, :half], "ctx", axis=0, tiled=True)
    wide_qb = lax.all_gather(w_query[:, half:], "ctx", axis=0, tiled=True)

    widened = inputs.astype(jnp.float32)
    turned = jnp.transpose(inputs)
    inv_rms = lax.rsqrt(jnp.mean(widened * widened, axis=1, keepdims=True) + epsilon)
    x_hat = widened * inv_rms
    normed = lax.optimization_barrier((x_hat * norm_gain).astype(jnp.bfloat16))
    inv_row = jnp.transpose(inv_rms)

    kv_raw = dot(normed, wide_kv)
    own = key_rows_of(kv_raw, key_norm_gain, kv_heads, head_dim)
    normed_turned = (turned.astype(jnp.float32) * inv_row * norm_gain[:, None]).astype(
        jnp.bfloat16
    )
    blocks, own = lax.optimization_barrier((share_of_columns(normed_turned, shard_rows), own))
    far = shift(own, "ctx", REACH)
    picked = jnp.where(on_first_core, own, far)
    near = swap(picked, "ctx", 1)

    query_multiplier = (q_gain * query_scale)[None, :]

    def attend(q_raw, skip, carry):
        return attention(
            jnp.full((1,), ctx_index * tokens, jnp.int32),
            jnp.cumsum(half_lengths).astype(jnp.int32),
            q_raw,
            output_cotangent,
            own,
            near,
            far,
            query_multiplier,
            kv_heads // 2,
            head_dim,
            skip,
            carry,
        )

    dqa, *carry, qa_sum = attend(dot(normed, wide_qa), 0, ())
    all_dqa = lax.all_gather(dqa, "ctx", axis=0, tiled=True)
    blocks, _ = lax.optimization_barrier((blocks, dqa))
    pieces = pick_columns(blocks)
    pieces = start_columns(pieces)
    dqb, d_own, d_near, d_far, qb_sum = attend(dot(normed, wide_qb), kv_heads // 2, carry)
    q_sum = qa_sum + qb_sum

    crossed = swap(d_near, "ctx", 1)
    nothing = jnp.zeros_like(crossed)
    outgoing = d_far + jnp.where(on_first_core, nothing, crossed)
    returned = shift(outgoing, "ctx", -REACH)
    gated, returned = lax.optimization_barrier((dqb, returned))
    all_dqb = lax.all_gather(gated, "ctx", axis=0, tiled=True)
    query_part = dot(wide_qa, dqa, NT) + dot(wide_qb, dqb, NT)
    query_part = lax.optimization_barrier(query_part)
    dk16, dv16, k_sum = key_grads_of(
        d_own,
        jnp.where(on_first_core, crossed, nothing),
        returned,
        kv_raw,
        key_norm_gain,
        kv_heads,
        head_dim,
    )
    dkv16 = jnp.concatenate([dk16, dv16], axis=1)
    all_dkv = lax.all_gather(dkv16, "ctx", axis=0, tiled=True)

    columns = finish_columns(pieces, dqb)

    head_part = (query_part + dot(wide_kv, dkv16, NT)).astype(jnp.bfloat16)
    row_dot = everywhere(
        jnp.sum(
            head_part.astype(jnp.float32) * (turned.astype(jnp.float32) * norm_gain[:, None]),
            axis=0,
            keepdims=True,
        )
        * inv_row,
        ("fsdp",),
    )

    def part_of(array, index):
        return lax.dynamic_slice_in_dim(array, index * features, features, 0)

    sent = [part_of(head_part, fsdp_index ^ m) for m in range(1, fsdp_count)]
    sent = [swap(part, "fsdp", 1 + m) for m, part in enumerate(sent)]
    d_mine = part_of(head_part, fsdp_index).astype(jnp.float32)
    for part in sent:
        d_mine = d_mine + part.astype(jnp.float32)
    hat_mine = part_of(turned, fsdp_index).astype(jnp.float32) * inv_row
    upstream = d_mine * part_of(norm_gain, fsdp_index)[:, None]
    grad_inputs = jnp.transpose(
        (inv_row * (upstream - hat_mine * row_dot / model_width)).astype(jnp.bfloat16)
    )
    norm_row_dots = row_dot[0] * float(model_width) ** (-0.5)
    gain_term = grad_scale * jnp.sum(d_mine * hat_mine, axis=1)
    gain_sum = lax.dynamic_slice_in_dim(
        everywhere(gain_term, ("ctx",)),
        ctx_index * (features // ctx_count),
        features // ctx_count,
        0,
    )

    q_weights = jnp.concatenate(
        [
            (grad_scale * dot(columns, part)).astype(jnp.bfloat16)
            for part in (all_dqa, all_dqb)
        ],
        axis=1,
    )
    k_weights = (grad_scale * dot(columns, all_dkv[:, :kv_cols])).astype(jnp.bfloat16)
    v_weights = (grad_scale * dot(columns, all_dkv[:, kv_cols:])).astype(jnp.bfloat16)

    gains = jnp.concatenate([q_sum * (grad_scale * query_scale), k_sum * grad_scale], axis=0)
    gains = everywhere(gains, ("fsdp",))
    gains = everywhere(gains, ("ctx",))
    return (
        grad_inputs,
        q_weights,
        k_weights,
        v_weights,
        gain_sum,
        gains[0],
        gains[1],
        norm_row_dots,
    )


def solution(mesh):
    placed = (
        P("ctx", None),
        P("ctx", "fsdp"),
        P("ctx", "fsdp"),
        P("ctx", "fsdp"),
        P("ctx", "fsdp"),
        P(),
        P(),
        P(),
        P(),
    )
    return jax.shard_map(
        layer,
        mesh=mesh,
        in_specs=placed,
        out_specs=(
            P("ctx", "fsdp"),
            P("ctx", "fsdp"),
            P("ctx", "fsdp"),
            P("ctx", "fsdp"),
            P(("fsdp", "ctx")),
            P(),
            P(),
            P("ctx"),
        ),
        check_vma=False,
    )
```

```python
import functools

import jax
import jax.numpy as jnp
from jax import lax
from jax.experimental import pallas as pl
from jax.experimental.pallas import tpu as pltpu
from jax.sharding import PartitionSpec as P


WIN = 1024
REACH = 2
BLOCKED = -1e30

epsilon = 1e-06
query_scale = 168.0 ** (-0.5)

NT = (((1,), (1,)), ((), ()))


def shift(value, axis, steps):
    count = lax.axis_size(axis)
    initial, last = (max(0, -steps), min(count, count - steps))
    return lax.ppermute(value, axis, [(s, s + steps) for s in range(initial, last)])


def swap(value, axis, flip):
    return lax.ppermute(value, axis, [(s, s ^ flip) for s in range(lax.axis_size(axis))])


def dot(a, b, dims=(((1,), (0,)), ((), ()))):
    return lax.dot_general(a, b, dims, preferred_element_type=jnp.float32)


def everywhere(value, axes):
    for axis in axes:
        flip = 1
        while flip < lax.axis_size(axis):
            value = value + swap(value, axis, flip)
            flip *= 2
    return value


def share_of_columns(normed_turned, shard_rows):
    chips = lax.axis_size("ctx") // 2
    shares = lax.axis_size("fsdp")
    tokens = normed_turned.shape[1]
    blocks = normed_turned.reshape(chips, 2, shares, shard_rows // shares, tokens)
    return lax.dynamic_index_in_dim(blocks, lax.axis_index("fsdp"), 2, keepdims=False)


def pick_columns(blocks):
    chip = lax.axis_index("ctx") // 2
    return [
        lax.dynamic_index_in_dim(blocks, chip ^ m, 0, keepdims=False)
        for m in range(blocks.shape[0])
    ]


def start_columns(pieces):
    return pieces[:1] + [swap(piece, "ctx", 2 + 2 * m) for m, piece in enumerate(pieces[1:])]


def finish_columns(pieces, gate):
    chips = len(pieces)
    chip = lax.axis_index("ctx") // 2
    core = lax.axis_index("ctx") % 2
    shares = lax.axis_size("fsdp")
    share = lax.axis_index("fsdp")
    pieces, _ = lax.optimization_barrier((jnp.stack(pieces), gate))
    piece, tokens = pieces.shape[2:]
    kept = lax.dynamic_index_in_dim(pieces, core, 1, keepdims=False)
    other = lax.dynamic_index_in_dim(pieces, 1 - core, 1, keepdims=False)
    other = swap(other, "ctx", 1)
    first, second = jnp.where(core == 0, kept, other), jnp.where(core == 0, other, kept)
    both = jnp.stack([first, second], axis=1)
    bit = 1
    while bit < chips:
        grouped = both.reshape(chips // (2 * bit), 2, bit, 2, piece, tokens)
        both = jnp.where((chip & bit) > 0, grouped[:, ::-1], grouped).reshape(both.shape)
        bit *= 2
    mine = jnp.transpose(both, (2, 0, 1, 3)).reshape(piece, chips * 2 * tokens)
    columns = jnp.zeros((shares,) + mine.shape, mine.dtype)
    columns = lax.dynamic_update_index_in_dim(columns, mine, share, 0)
    for m in range(1, shares):
        part = swap(mine, "fsdp", m)
        columns = lax.dynamic_update_index_in_dim(columns, part, share ^ m, 0)
    return columns.reshape(shares * piece, chips * 2 * tokens)


def key_body(k_ref, v_ref, gain_ref, kv_ref):
    k = k_ref[...]
    inv = lax.rsqrt(jnp.mean(k * k, axis=1, keepdims=True) + epsilon)
    kv_ref[0] = (k * inv * gain_ref[...]).astype(jnp.bfloat16)
    kv_ref[1] = v_ref[...].astype(jnp.bfloat16)


def key_rows_of(projected, gain, kv_heads, head_dim):
    tokens = projected.shape[0]
    return pl.pallas_call(
        key_body,
        grid=(kv_heads,),
        in_specs=[
            pl.BlockSpec((tokens, head_dim), lambda g: (0, g)),
            pl.BlockSpec((tokens, head_dim), lambda g: (0, kv_heads + g)),
            pl.BlockSpec((1, head_dim), lambda g: (0, 0)),
        ],
        out_specs=pl.BlockSpec((2, tokens, head_dim), lambda g: (0, 0, g)),
        out_shape=jax.ShapeDtypeStruct((2, tokens, kv_heads * head_dim), jnp.bfloat16),
        name="key_rows",
    )(projected, projected, gain[None, :])


def key_grad_body(own_ref, near_ref, far_ref, k_ref, gain_ref, dk_ref, dv_ref, sum_ref):
    total = own_ref[...] + near_ref[...].astype(jnp.float32) + far_ref[...].astype(jnp.float32)
    k = k_ref[...]
    inv = lax.rsqrt(jnp.mean(k * k, axis=1, keepdims=True) + epsilon)
    k_hat = k * inv
    d = total[0]
    u = d * gain_ref[...]
    dk_ref[...] = (inv * (u - k_hat * jnp.mean(u * k_hat, axis=1, keepdims=True))).astype(
        jnp.bfloat16
    )
    dv_ref[...] = total[1].astype(jnp.bfloat16)

    @pl.when(pl.program_id(0) == 0)
    def _():
        sum_ref[...] = jnp.zeros_like(sum_ref)

    sum_ref[...] += jnp.sum(d * k_hat, axis=0, keepdims=True)


def key_grads_of(own, near, far, projected, gain, kv_heads, head_dim):
    tokens = projected.shape[0]
    stacked = pl.BlockSpec((2, tokens, head_dim), lambda g: (0, 0, g))
    flat = pl.BlockSpec((tokens, head_dim), lambda g: (0, g))
    row = pl.BlockSpec((1, head_dim), lambda g: (0, 0))
    half = jax.ShapeDtypeStruct((tokens, kv_heads * head_dim), jnp.bfloat16)
    return pl.pallas_call(
        key_grad_body,
        grid=(kv_heads,),
        in_specs=[stacked, stacked, stacked, flat, row],
        out_specs=(flat, flat, row),
        out_shape=(half, half, jax.ShapeDtypeStruct((1, head_dim), jnp.float32)),
        name="key_grads",
    )(own, near, far, projected, gain[None, :])


def attention_body(
    start_ref,
    ends_ref,
    q_ref,
    go_ref,
    own_ref,
    near_ref,
    far_ref,
    mult_ref,
    dq_ref,
    d_own_ref,
    d_near_ref,
    d_far_ref,
    sum_ref,
    bias_ref,
    k_ref,
    v_ref,
    kt_ref,
    vt_ref,
    dk_ref,
    dv_ref,
    *,
    rows,
    heads,
    segments,
):
    g = pl.program_id(0)
    s = pl.program_id(1)
    last = pl.num_programs(1) - 1
    tokens, head_dim = own_ref.shape[1:]
    reach = WIN
    span = reach + rows
    offset = pl.multiple_of(s * rows, rows)

    @pl.when(g == 0)
    def _():
        first = start_ref[0]
        key_pos = (first - reach + s * rows) + lax.broadcasted_iota(jnp.int32, (span, 1), 0)
        query_pos = (first + s * rows) + lax.broadcasted_iota(jnp.int32, (1, rows), 1)
        key_seg = jnp.zeros((span, 1), jnp.int32)
        query_seg = jnp.zeros((1, rows), jnp.int32)
        for i in range(segments):
            key_seg += (ends_ref[i] <= key_pos).astype(jnp.int32)
            query_seg += (ends_ref[i] <= query_pos).astype(jnp.int32)
        distance = query_pos - key_pos
        allowed = (
            (key_seg == query_seg) & (distance >= 0) & (distance < WIN) & (key_pos >= 0)
        )
        bias_ref[s] = jnp.where(allowed, 0.0, BLOCKED)

    @pl.when(s == 0)
    def _():
        for at, ref in enumerate((far_ref, near_ref, own_ref)):
            k_ref[pl.ds(at * tokens, tokens), :] = ref[0]
            v_ref[pl.ds(at * tokens, tokens), :] = ref[1]
        dk_ref[...] = jnp.zeros_like(dk_ref)
        dv_ref[...] = jnp.zeros_like(dv_ref)

    @pl.when((s == 0) & (g == 0))
    def _():
        sum_ref[...] = jnp.zeros_like(sum_ref)

    k = k_ref[pl.ds(offset, span), :]
    v = v_ref[pl.ds(offset, span), :]
    kt_ref[...] = jnp.transpose(k)
    vt_ref[...] = jnp.transpose(v)
    mult = mult_ref[...]
    bias = bias_ref[s]
    for h in range(heads):
        at = slice(h * head_dim, (h + 1) * head_dim)
        q = q_ref[:, at]
        inv = lax.rsqrt(jnp.mean(q * q, axis=1, keepdims=True) + epsilon)
        q_hat = q * inv
        q16 = (q_hat * mult).astype(jnp.bfloat16)
        go = go_ref[:, at]
        weights = jnp.exp(dot(k, q16, NT) + bias)
        over = 1.0 / jnp.sum(weights, axis=0, keepdims=True)
        out_t = dot(vt_ref[...], weights.astype(jnp.bfloat16)) * over
        delta = jnp.sum(jnp.transpose(go.astype(jnp.float32)) * out_t, axis=0, keepdims=True)
        probs = weights * over
        dv_ref[pl.ds(offset, span), :] += dot(probs.astype(jnp.bfloat16), go)
        d_scores = (probs * (dot(v, go, NT) - delta)).astype(jnp.bfloat16)
        dk_ref[pl.ds(offset, span), :] += dot(d_scores, q16)
        d_query = jnp.transpose(dot(kt_ref[...], d_scores))
        u = d_query * mult
        dq_ref[:, at] = (
            inv * (u - q_hat * jnp.mean(u * q_hat, axis=1, keepdims=True))
        ).astype(jnp.bfloat16)
        sum_ref[...] += jnp.sum(d_query * q_hat, axis=0, keepdims=True)

    @pl.when(s == last)
    def _():
        for at, ref in enumerate((d_far_ref, d_near_ref, d_own_ref)):
            ref[0] = dk_ref[pl.ds(at * tokens, tokens), :].astype(ref.dtype)
            ref[1] = dv_ref[pl.ds(at * tokens, tokens), :].astype(ref.dtype)


def attention_rest(start, ends, q, go, own, near, far, mult, *refs, **sizes):
    attention_body(start, ends, q, go, own, near, far, mult, *refs[4:], **sizes)


def attention(start, ends, q_raw, go, own, near, far, mult, kv_heads, head_dim, skip, carry):
    tokens, q_cols = q_raw.shape
    heads = q_cols // (kv_heads * head_dim)
    rows = min(256, tokens)
    steps = tokens // rows
    span = WIN + rows
    stacked = pl.BlockSpec((2, tokens, head_dim), lambda g, s, *_: (0, 0, skip + g))
    by_query = pl.BlockSpec((rows, heads * head_dim), lambda g, s, *_: (s, g))
    by_skipped = pl.BlockSpec((rows, heads * head_dim), lambda g, s, *_: (s, skip + g))
    whole = pl.BlockSpec(memory_space=pl.ANY)
    row = pl.BlockSpec((1, head_dim), lambda g, s, *_: (0, 0))
    half = jax.ShapeDtypeStruct(own.shape, jnp.bfloat16)
    keys = WIN + tokens
    return pl.pallas_call(
        functools.partial(
            attention_rest if carry else attention_body,
            rows=rows,
            heads=heads,
            segments=ends.shape[0],
        ),
        grid_spec=pltpu.PrefetchScalarGridSpec(
            num_scalar_prefetch=2,
            grid=(kv_heads, steps),
            in_specs=[by_query, by_skipped, stacked, stacked, stacked, row]
            + [whole for _ in carry],
            out_specs=(by_skipped, stacked, stacked, stacked, row),
            scratch_shapes=[
                pltpu.VMEM((steps, span, rows), jnp.float32),
                pltpu.VMEM((keys, head_dim), jnp.bfloat16),
                pltpu.VMEM((keys, head_dim), jnp.bfloat16),
                pltpu.VMEM((head_dim, span), jnp.bfloat16),
                pltpu.VMEM((head_dim, span), jnp.bfloat16),
                pltpu.VMEM((keys, head_dim), jnp.float32),
                pltpu.VMEM((keys, head_dim), jnp.float32),
            ],
        ),
        out_shape=(
            jax.ShapeDtypeStruct(go.shape, jnp.bfloat16),
            jax.ShapeDtypeStruct(own.shape, jnp.float32),
            half,
            half,
            jax.ShapeDtypeStruct((1, head_dim), jnp.float32),
        ),
        compiler_params=pltpu.CompilerParams(
            dimension_semantics=("arbitrary", "arbitrary"), vmem_limit_bytes=48 << 20
        ),
        input_output_aliases={8 + i: i for i in range(len(carry))},
        name="attention",
    )(start, ends, q_raw, go, own, near, far, mult, *carry)


def layer(
    inputs,
    output_cotangent,
    w_query,
    key_projection,
    value_projection,
    norm_gain,
    q_gain,
    key_norm_gain,
    half_lengths,
):
    tokens, model_width = inputs.shape
    head_dim = q_gain.shape[0]
    kv_cols = key_projection.shape[1]
    kv_heads = kv_cols // head_dim
    ctx_count = lax.axis_size("ctx")
    fsdp_count = lax.axis_size("fsdp")
    ctx_index = lax.axis_index("ctx")
    fsdp_index = lax.axis_index("fsdp")
    on_first_core = ctx_index % 2 == 0
    grad_scale = float(tokens * ctx_count) ** (-0.5)
    shard_rows = w_query.shape[0]
    features = model_width // fsdp_count

    half = w_query.shape[1] // 2
    wide = lax.all_gather(
        jnp.concatenate([key_projection, value_projection, w_query[:, :half]], axis=1),
        "ctx",
        axis=0,
        tiled=True,
    )
    wide_kv, wide_qa = wide[:, : 2 * kv_cols], wide[:, 2 * kv_cols :]
    wide_qb = lax.all_gather(w_query[:, half:], "ctx", axis=0, tiled=True)

    widened = inputs.astype(jnp.float32)
    turned = jnp.transpose(inputs)
    inv_rms = lax.rsqrt(jnp.mean(widened * widened, axis=1, keepdims=True) + epsilon)
    x_hat = widened * inv_rms
    normed = lax.optimization_barrier((x_hat * norm_gain).astype(jnp.bfloat16))
    inv_row = jnp.transpose(inv_rms)

    kv_raw = dot(normed, wide_kv)
    own = key_rows_of(kv_raw, key_norm_gain, kv_heads, head_dim)
    normed_turned = (turned.astype(jnp.float32) * inv_row * norm_gain[:, None]).astype(
        jnp.bfloat16
    )
    blocks, own = lax.optimization_barrier((share_of_columns(normed_turned, shard_rows), own))
    far = shift(own, "ctx", REACH)
    blocks, far = lax.optimization_barrier((blocks, far))
    picked = jnp.where(on_first_core, own, far)
    near = swap(picked, "ctx", 1)
    pieces = pick_columns(blocks)
    pieces = start_columns(pieces)

    query_multiplier = (q_gain * query_scale)[None, :]

    def attend(q_raw, skip, carry):
        return attention(
            jnp.full((1,), ctx_index * tokens, jnp.int32),
            jnp.cumsum(half_lengths).astype(jnp.int32),
            q_raw,
            output_cotangent,
            own,
            near,
            far,
            query_multiplier,
            kv_heads // 2,
            head_dim,
            skip,
            carry,
        )

    *carry, qa_sum = attend(dot(normed, wide_qa), 0, ())
    dq16, d_own, d_near, d_far, qb_sum = attend(dot(normed, wide_qb), kv_heads // 2, carry)
    q_sum = qa_sum + qb_sum

    crossed = swap(d_near, "ctx", 1)
    nothing = jnp.zeros_like(crossed)
    outgoing = d_far + jnp.where(on_first_core, nothing, crossed)
    returned = shift(outgoing, "ctx", -REACH)
    gated, returned = lax.optimization_barrier((dq16, returned))
    all_dq = lax.all_gather(gated, "ctx", axis=0, tiled=True)
    query_part = dot(wide_qa, dq16[:, :half], NT) + dot(wide_qb, dq16[:, half:], NT)
    query_part = lax.optimization_barrier(query_part)
    dk16, dv16, k_sum = key_grads_of(
        d_own,
        jnp.where(on_first_core, crossed, nothing),
        returned,
        kv_raw,
        key_norm_gain,
        kv_heads,
        head_dim,
    )
    dkv16 = jnp.concatenate([dk16, dv16], axis=1)
    all_dkv = lax.all_gather(dkv16, "ctx", axis=0, tiled=True)

    columns = finish_columns(pieces, dq16)

    head_part = (query_part + dot(wide_kv, dkv16, NT)).astype(jnp.bfloat16)
    row_dot = everywhere(
        jnp.sum(
            head_part.astype(jnp.float32) * (turned.astype(jnp.float32) * norm_gain[:, None]),
            axis=0,
            keepdims=True,
        )
        * inv_row,
        ("fsdp",),
    )

    def part_of(array, index):
        return lax.dynamic_slice_in_dim(array, index * features, features, 0)

    sent = [part_of(head_part, fsdp_index ^ m) for m in range(1, fsdp_count)]
    sent = [swap(part, "fsdp", 1 + m) for m, part in enumerate(sent)]
    d_mine = part_of(head_part, fsdp_index).astype(jnp.float32)
    for part in sent:
        d_mine = d_mine + part.astype(jnp.float32)
    hat_mine = part_of(turned, fsdp_index).astype(jnp.float32) * inv_row
    upstream = d_mine * part_of(norm_gain, fsdp_index)[:, None]
    grad_inputs = jnp.transpose(
        (inv_row * (upstream - hat_mine * row_dot / model_width)).astype(jnp.bfloat16)
    )
    norm_row_dots = row_dot[0] * float(model_width) ** (-0.5)
    gain_term = grad_scale * jnp.sum(d_mine * hat_mine, axis=1)
    gain_sum = lax.dynamic_slice_in_dim(
        everywhere(gain_term, ("ctx",)),
        ctx_index * (features // ctx_count),
        features // ctx_count,
        0,
    )

    q_weights = (grad_scale * dot(columns, all_dq)).astype(jnp.bfloat16)
    k_weights = (grad_scale * dot(columns, all_dkv[:, :kv_cols])).astype(jnp.bfloat16)
    v_weights = (grad_scale * dot(columns, all_dkv[:, kv_cols:])).astype(jnp.bfloat16)

    gains = jnp.concatenate([q_sum * (grad_scale * query_scale), k_sum * grad_scale], axis=0)
    gains = everywhere(gains, ("fsdp",))
    gains = everywhere(gains, ("ctx",))
    return (
        grad_inputs,
        q_weights,
        k_weights,
        v_weights,
        gain_sum,
        gains[0],
        gains[1],
        norm_row_dots,
    )


def solution(mesh):
    placed = (
        P("ctx", None),
        P("ctx", "fsdp"),
        P("ctx", "fsdp"),
        P("ctx", "fsdp"),
        P("ctx", "fsdp"),
        P(),
        P(),
        P(),
        P(),
    )
    return jax.shard_map(
        layer,
        mesh=mesh,
        in_specs=placed,
        out_specs=(
            P("ctx", "fsdp"),
            P("ctx", "fsdp"),
            P("ctx", "fsdp"),
            P("ctx", "fsdp"),
            P(("fsdp", "ctx")),
            P(),
            P(),
            P("ctx"),
        ),
        check_vma=False,
    )
```

```python
import functools

import jax
import jax.numpy as jnp
from jax import lax
from jax.experimental import pallas as pl
from jax.experimental.pallas import tpu as pltpu
from jax.sharding import PartitionSpec as P


WIN = 1024
REACH = 2
BLOCKED = -1e30

epsilon = 1e-06
query_scale = 168.0 ** (-0.5)

NT = (((1,), (1,)), ((), ()))


def shift(value, axis, steps):
    count = lax.axis_size(axis)
    initial, last = (max(0, -steps), min(count, count - steps))
    return lax.ppermute(value, axis, [(s, s + steps) for s in range(initial, last)])


def swap(value, axis, flip):
    return lax.ppermute(value, axis, [(s, s ^ flip) for s in range(lax.axis_size(axis))])


def dot(a, b, dims=(((1,), (0,)), ((), ()))):
    return lax.dot_general(a, b, dims, preferred_element_type=jnp.float32)


def everywhere(value, axes):
    for axis in axes:
        flip = 1
        while flip < lax.axis_size(axis):
            value = value + swap(value, axis, flip)
            flip *= 2
    return value


def share_of_columns(normed_turned, shard_rows):
    chips = lax.axis_size("ctx") // 2
    shares = lax.axis_size("fsdp")
    tokens = normed_turned.shape[1]
    blocks = normed_turned.reshape(chips, 2, shares, shard_rows // shares, tokens)
    return lax.dynamic_index_in_dim(blocks, lax.axis_index("fsdp"), 2, keepdims=False)


def start_columns(blocks):
    chips = blocks.shape[0]
    chip = lax.axis_index("ctx") // 2
    pieces = []
    for m in range(chips):
        piece = lax.dynamic_index_in_dim(blocks, chip ^ m, 0, keepdims=False)
        if m:
            piece = swap(piece, "ctx", 2 * m)
        pieces.append(piece)
    return pieces


def finish_columns(pieces, gate):
    chips = len(pieces)
    chip = lax.axis_index("ctx") // 2
    core = lax.axis_index("ctx") % 2
    shares = lax.axis_size("fsdp")
    share = lax.axis_index("fsdp")
    pieces, _ = lax.optimization_barrier((jnp.stack(pieces), gate))
    piece, tokens = pieces.shape[2:]
    kept = lax.dynamic_index_in_dim(pieces, core, 1, keepdims=False)
    other = lax.dynamic_index_in_dim(pieces, 1 - core, 1, keepdims=False)
    other = swap(other, "ctx", 1)
    first, second = jnp.where(core == 0, kept, other), jnp.where(core == 0, other, kept)
    both = jnp.stack([first, second], axis=1)
    bit = 1
    while bit < chips:
        grouped = both.reshape(chips // (2 * bit), 2, bit, 2, piece, tokens)
        both = jnp.where((chip & bit) > 0, grouped[:, ::-1], grouped).reshape(both.shape)
        bit *= 2
    mine = jnp.transpose(both, (2, 0, 1, 3)).reshape(piece, chips * 2 * tokens)
    columns = jnp.zeros((shares,) + mine.shape, mine.dtype)
    columns = lax.dynamic_update_index_in_dim(columns, mine, share, 0)
    for m in range(1, shares):
        part = swap(mine, "fsdp", m)
        columns = lax.dynamic_update_index_in_dim(columns, part, share ^ m, 0)
    return columns.reshape(shares * piece, chips * 2 * tokens)


def key_body(k_ref, v_ref, gain_ref, kv_ref):
    k = k_ref[...]
    inv = lax.rsqrt(jnp.mean(k * k, axis=1, keepdims=True) + epsilon)
    kv_ref[0] = (k * inv * gain_ref[...]).astype(jnp.bfloat16)
    kv_ref[1] = v_ref[...].astype(jnp.bfloat16)


def key_rows_of(projected, gain, kv_heads, head_dim):
    tokens = projected.shape[0]
    return pl.pallas_call(
        key_body,
        grid=(kv_heads,),
        in_specs=[
            pl.BlockSpec((tokens, head_dim), lambda g: (0, g)),
            pl.BlockSpec((tokens, head_dim), lambda g: (0, kv_heads + g)),
            pl.BlockSpec((1, head_dim), lambda g: (0, 0)),
        ],
        out_specs=pl.BlockSpec((2, tokens, head_dim), lambda g: (0, 0, g)),
        out_shape=jax.ShapeDtypeStruct((2, tokens, kv_heads * head_dim), jnp.bfloat16),
        name="key_rows",
    )(projected, projected, gain[None, :])


def key_grad_body(own_ref, near_ref, far_ref, k_ref, gain_ref, out_ref, sum_ref):
    total = own_ref[0] + near_ref[0].astype(jnp.float32) + far_ref[0].astype(jnp.float32)

    @pl.when((pl.program_id(0) == 0) & (pl.program_id(1) == 0))
    def _():
        sum_ref[...] = jnp.zeros_like(sum_ref)

    @pl.when(pl.program_id(0) == 0)
    def _():
        k = k_ref[...]
        inv = lax.rsqrt(jnp.mean(k * k, axis=1, keepdims=True) + epsilon)
        k_hat = k * inv
        u = total * gain_ref[...]
        out_ref[...] = (
            inv * (u - k_hat * jnp.mean(u * k_hat, axis=1, keepdims=True))
        ).astype(jnp.bfloat16)
        sum_ref[...] += jnp.sum(total * k_hat, axis=0, keepdims=True)

    @pl.when(pl.program_id(0) == 1)
    def _():
        out_ref[...] = total.astype(jnp.bfloat16)


def key_grads_of(own, near, far, projected, gain, kv_heads, head_dim):
    tokens = projected.shape[0]
    stacked = pl.BlockSpec((1, tokens, head_dim), lambda t, g: (t, 0, g))
    row = pl.BlockSpec((1, head_dim), lambda t, g: (0, 0))
    return pl.pallas_call(
        key_grad_body,
        grid=(2, kv_heads),
        in_specs=[
            stacked,
            stacked,
            stacked,
            pl.BlockSpec((tokens, head_dim), lambda t, g: (0, g)),
            row,
        ],
        out_specs=(
            pl.BlockSpec((tokens, head_dim), lambda t, g: (0, t * kv_heads + g)),
            row,
        ),
        out_shape=(
            jax.ShapeDtypeStruct((tokens, 2 * kv_heads * head_dim), jnp.bfloat16),
            jax.ShapeDtypeStruct((1, head_dim), jnp.float32),
        ),
        name="key_grads",
    )(own, near, far, projected, gain[None, :])


def normed_grad_body(part_ref, wide_ref, d_ref, x_ref, gain_ref, out_ref, dots_ref):
    rounded = (part_ref[...] + dot(wide_ref[...], d_ref[...], NT)).astype(jnp.bfloat16)
    out_ref[...] = rounded

    @pl.when(pl.program_id(0) == 0)
    def _():
        dots_ref[...] = jnp.zeros_like(dots_ref)

    gained = x_ref[...].astype(jnp.float32) * gain_ref[...]
    dots_ref[...] += jnp.sum(rounded.astype(jnp.float32) * gained, axis=0, keepdims=True)


def normed_grad(part, wide, d, turned, gain):
    width, tokens = part.shape
    cols = wide.shape[1]
    rows = max(r for r in range(128, 513, 128) if width % r == 0)
    by_row = pl.BlockSpec((rows, tokens), lambda i: (i, 0))
    return pl.pallas_call(
        normed_grad_body,
        grid=(width // rows,),
        in_specs=[
            by_row,
            pl.BlockSpec((rows, cols), lambda i: (i, 0)),
            pl.BlockSpec((tokens, cols), lambda i: (0, 0)),
            by_row,
            pl.BlockSpec((rows, 1), lambda i: (i, 0)),
        ],
        out_specs=(by_row, pl.BlockSpec((1, tokens), lambda i: (0, 0))),
        out_shape=(
            jax.ShapeDtypeStruct((width, tokens), jnp.bfloat16),
            jax.ShapeDtypeStruct((1, tokens), jnp.float32),
        ),
        name="normed_grad",
    )(part, wide, d, turned, gain[:, None])


def weight_grad_body(columns_ref, d_ref, k_ref, v_ref, sum_ref, *, scale):
    step = pl.program_id(0)
    product = dot(columns_ref[...], d_ref[...])

    @pl.when(step == 0)
    def _():
        sum_ref[...] = product

    @pl.when(step > 0)
    def _():
        sum_ref[...] += product

    @pl.when(step == pl.num_programs(0) - 1)
    def _():
        cut = k_ref.shape[1]
        k_ref[...] = (scale * sum_ref[:, :cut]).astype(k_ref.dtype)
        v_ref[...] = (scale * sum_ref[:, cut:]).astype(v_ref.dtype)


def weight_grads(columns, d, scale):
    rows, tokens = columns.shape
    cols = d.shape[1]
    chunk = tokens // 4
    out = pl.BlockSpec((rows, cols // 2), lambda i: (0, 0))
    shape = jax.ShapeDtypeStruct((rows, cols // 2), jnp.bfloat16)
    return pl.pallas_call(
        functools.partial(weight_grad_body, scale=scale),
        grid=(4,),
        in_specs=[
            pl.BlockSpec((rows, chunk), lambda i: (0, i)),
            pl.BlockSpec((chunk, cols), lambda i: (i, 0)),
        ],
        out_specs=(out, out),
        out_shape=(shape, shape),
        scratch_shapes=[pltpu.VMEM((rows, cols), jnp.float32)],
        compiler_params=pltpu.CompilerParams(vmem_limit_bytes=40 << 20),
        name="weight_grads",
    )(columns, d)


def attention_body(
    start_ref,
    ends_ref,
    q_ref,
    go_ref,
    own_ref,
    near_ref,
    far_ref,
    mult_ref,
    dq_ref,
    d_own_ref,
    d_near_ref,
    d_far_ref,
    sum_ref,
    bias_ref,
    k_ref,
    v_ref,
    kt_ref,
    vt_ref,
    dk_ref,
    dv_ref,
    *,
    rows,
    heads,
    segments,
):
    g = pl.program_id(0)
    s = pl.program_id(1)
    last = pl.num_programs(1) - 1
    tokens, head_dim = own_ref.shape[1:]
    reach = WIN
    span = reach + rows
    offset = pl.multiple_of(s * rows, rows)

    @pl.when(g == 0)
    def _():
        first = start_ref[0]
        key_pos = (first - reach + s * rows) + lax.broadcasted_iota(jnp.int32, (span, 1), 0)
        query_pos = (first + s * rows) + lax.broadcasted_iota(jnp.int32, (1, rows), 1)
        key_seg = jnp.zeros((span, 1), jnp.int32)
        query_seg = jnp.zeros((1, rows), jnp.int32)
        for i in range(segments):
            key_seg += (ends_ref[i] <= key_pos).astype(jnp.int32)
            query_seg += (ends_ref[i] <= query_pos).astype(jnp.int32)
        distance = query_pos - key_pos
        allowed = (
            (key_seg == query_seg) & (distance >= 0) & (distance < WIN) & (key_pos >= 0)
        )
        bias_ref[s] = jnp.where(allowed, 0.0, BLOCKED)

    @pl.when(s == 0)
    def _():
        for at, ref in enumerate((far_ref, near_ref, own_ref)):
            k_ref[pl.ds(at * tokens, tokens), :] = ref[0]
            v_ref[pl.ds(at * tokens, tokens), :] = ref[1]
        dk_ref[...] = jnp.zeros_like(dk_ref)
        dv_ref[...] = jnp.zeros_like(dv_ref)

    @pl.when((s == 0) & (g == 0))
    def _():
        sum_ref[...] = jnp.zeros_like(sum_ref)

    k = k_ref[pl.ds(offset, span), :]
    v = v_ref[pl.ds(offset, span), :]
    kt_ref[...] = jnp.transpose(k)
    vt_ref[...] = jnp.transpose(v)
    mult = mult_ref[...]
    bias = bias_ref[s]
    for h in range(heads):
        at = slice(h * head_dim, (h + 1) * head_dim)
        q = q_ref[:, at]
        inv = lax.rsqrt(jnp.mean(q * q, axis=1, keepdims=True) + epsilon)
        q_hat = q * inv
        q16 = (q_hat * mult).astype(jnp.bfloat16)
        go = go_ref[:, at]
        weights = jnp.exp(dot(k, q16, NT) + bias)
        over = 1.0 / jnp.sum(weights, axis=0, keepdims=True)
        out_t = dot(vt_ref[...], weights.astype(jnp.bfloat16)) * over
        delta = jnp.sum(jnp.transpose(go.astype(jnp.float32)) * out_t, axis=0, keepdims=True)
        probs = weights * over
        dv_ref[pl.ds(offset, span), :] += dot(probs.astype(jnp.bfloat16), go)
        d_scores = (probs * (dot(v, go, NT) - delta)).astype(jnp.bfloat16)
        dk_ref[pl.ds(offset, span), :] += dot(d_scores, q16)
        d_query = jnp.transpose(dot(kt_ref[...], d_scores))
        u = d_query * mult
        dq_ref[:, at] = (
            inv * (u - q_hat * jnp.mean(u * q_hat, axis=1, keepdims=True))
        ).astype(jnp.bfloat16)
        sum_ref[...] += jnp.sum(d_query * q_hat, axis=0, keepdims=True)

    @pl.when(s == last)
    def _():
        for at, ref in enumerate((d_far_ref, d_near_ref, d_own_ref)):
            ref[0] = dk_ref[pl.ds(at * tokens, tokens), :].astype(ref.dtype)
            ref[1] = dv_ref[pl.ds(at * tokens, tokens), :].astype(ref.dtype)


def attention(start, ends, q_raw, go, own, near, far, mult, kv_heads, head_dim):
    tokens, q_cols = q_raw.shape
    heads = q_cols // (kv_heads * head_dim)
    rows = min(256, tokens)
    steps = tokens // rows
    span = WIN + rows
    stacked = pl.BlockSpec((2, tokens, head_dim), lambda g, s, *_: (0, 0, g))
    by_query = pl.BlockSpec((rows, heads * head_dim), lambda g, s, *_: (s, g))
    row = pl.BlockSpec((1, head_dim), lambda g, s, *_: (0, 0))
    half = jax.ShapeDtypeStruct(own.shape, jnp.bfloat16)
    keys = WIN + tokens
    return pl.pallas_call(
        functools.partial(attention_body, rows=rows, heads=heads, segments=ends.shape[0]),
        grid_spec=pltpu.PrefetchScalarGridSpec(
            num_scalar_prefetch=2,
            grid=(kv_heads, steps),
            in_specs=[by_query, by_query, stacked, stacked, stacked, row],
            out_specs=(by_query, stacked, stacked, stacked, row),
            scratch_shapes=[
                pltpu.VMEM((steps, span, rows), jnp.float32),
                pltpu.VMEM((keys, head_dim), jnp.bfloat16),
                pltpu.VMEM((keys, head_dim), jnp.bfloat16),
                pltpu.VMEM((head_dim, span), jnp.bfloat16),
                pltpu.VMEM((head_dim, span), jnp.bfloat16),
                pltpu.VMEM((keys, head_dim), jnp.float32),
                pltpu.VMEM((keys, head_dim), jnp.float32),
            ],
        ),
        out_shape=(
            jax.ShapeDtypeStruct((tokens, q_cols), jnp.bfloat16),
            jax.ShapeDtypeStruct(own.shape, jnp.float32),
            half,
            half,
            jax.ShapeDtypeStruct((1, head_dim), jnp.float32),
        ),
        compiler_params=pltpu.CompilerParams(
            dimension_semantics=("arbitrary", "arbitrary"), vmem_limit_bytes=48 << 20
        ),
        name="attention",
    )(start, ends, q_raw, go, own, near, far, mult)


def layer(
    inputs,
    output_cotangent,
    w_query,
    key_projection,
    value_projection,
    norm_gain,
    q_gain,
    key_norm_gain,
    half_lengths,
):
    tokens, model_width = inputs.shape
    head_dim = q_gain.shape[0]
    kv_cols = key_projection.shape[1]
    kv_heads = kv_cols // head_dim
    ctx_count = lax.axis_size("ctx")
    fsdp_count = lax.axis_size("fsdp")
    ctx_index = lax.axis_index("ctx")
    fsdp_index = lax.axis_index("fsdp")
    on_first_core = ctx_index % 2 == 0
    grad_scale = float(tokens * ctx_count) ** (-0.5)
    shard_rows = w_query.shape[0]
    features = model_width // fsdp_count

    key_value = jnp.concatenate([key_projection, value_projection], axis=1)
    wide_kv = lax.all_gather(key_value, "ctx", axis=0, tiled=True)
    wide_q = lax.all_gather(w_query, "ctx", axis=0, tiled=True)

    widened = inputs.astype(jnp.float32)
    turned = jnp.transpose(inputs)
    inv_rms = lax.rsqrt(jnp.mean(widened * widened, axis=1, keepdims=True) + epsilon)
    x_hat = widened * inv_rms
    normed = lax.optimization_barrier((x_hat * norm_gain).astype(jnp.bfloat16))
    inv_row = jnp.transpose(inv_rms)

    kv_raw = dot(normed, wide_kv)
    own = key_rows_of(kv_raw, key_norm_gain, kv_heads, head_dim)
    normed_turned = (turned.astype(jnp.float32) * inv_row * norm_gain[:, None]).astype(
        jnp.bfloat16
    )
    blocks, own = lax.optimization_barrier((share_of_columns(normed_turned, shard_rows), own))
    far = shift(own, "ctx", REACH)
    picked = jnp.where(on_first_core, own, far)
    near = swap(picked, "ctx", 1)

    blocks, _ = lax.optimization_barrier((blocks, wide_q))
    pieces = start_columns(blocks)
    q_raw = dot(normed, wide_q)
    query_multiplier = (q_gain * query_scale)[None, :]
    dq16, d_own, d_near, d_far, q_sum = attention(
        jnp.full((1,), ctx_index * tokens, jnp.int32),
        jnp.cumsum(half_lengths).astype(jnp.int32),
        q_raw,
        output_cotangent,
        own,
        near,
        far,
        query_multiplier,
        kv_heads,
        head_dim,
    )

    crossed = swap(d_near, "ctx", 1)
    nothing = jnp.zeros_like(crossed)
    outgoing = d_far + jnp.where(on_first_core, nothing, crossed)
    returned = shift(outgoing, "ctx", -REACH)
    all_dq = lax.all_gather(dq16, "ctx", axis=0, tiled=True)
    query_part = dot(wide_q, dq16, NT)
    query_part = lax.optimization_barrier(query_part)
    dkv16, k_sum = key_grads_of(
        d_own,
        jnp.where(on_first_core, crossed, nothing),
        returned,
        kv_raw,
        key_norm_gain,
        kv_heads,
        head_dim,
    )
    all_dkv = lax.all_gather(dkv16, "ctx", axis=0, tiled=True)

    columns = finish_columns(pieces, dq16)

    head_part, row_dot = normed_grad(query_part, wide_kv, dkv16, turned, norm_gain)
    row_dot = everywhere(row_dot * inv_row, ("fsdp",))

    def part_of(array, index):
        return lax.dynamic_slice_in_dim(array, index * features, features, 0)

    sent = [part_of(head_part, fsdp_index ^ m) for m in range(1, fsdp_count)]
    sent = [swap(part, "fsdp", 1 + m) for m, part in enumerate(sent)]
    d_mine = part_of(head_part, fsdp_index).astype(jnp.float32)
    for part in sent:
        d_mine = d_mine + part.astype(jnp.float32)
    hat_mine = part_of(turned, fsdp_index).astype(jnp.float32) * inv_row
    upstream = d_mine * part_of(norm_gain, fsdp_index)[:, None]
    grad_inputs = jnp.transpose(
        (inv_row * (upstream - hat_mine * row_dot / model_width)).astype(jnp.bfloat16)
    )
    norm_row_dots = row_dot[0] * float(model_width) ** (-0.5)
    gain_term = grad_scale * jnp.sum(d_mine * hat_mine, axis=1)
    gain_sum = lax.dynamic_slice_in_dim(
        everywhere(gain_term, ("ctx",)),
        ctx_index * (features // ctx_count),
        features // ctx_count,
        0,
    )

    q_weights = (grad_scale * dot(columns, all_dq)).astype(jnp.bfloat16)
    k_weights, v_weights = weight_grads(columns, all_dkv, grad_scale)

    gains = jnp.concatenate([q_sum * (grad_scale * query_scale), k_sum * grad_scale], axis=0)
    gains = everywhere(gains, ("fsdp",))
    gains = everywhere(gains, ("ctx",))
    return (
        grad_inputs,
        q_weights,
        k_weights,
        v_weights,
        gain_sum,
        gains[0],
        gains[1],
        norm_row_dots,
    )


def solution(mesh):
    placed = (
        P("ctx", None),
        P("ctx", "fsdp"),
        P("ctx", "fsdp"),
        P("ctx", "fsdp"),
        P("ctx", "fsdp"),
        P(),
        P(),
        P(),
        P(),
    )
    return jax.shard_map(
        layer,
        mesh=mesh,
        in_specs=placed,
        out_specs=(
            P("ctx", "fsdp"),
            P("ctx", "fsdp"),
            P("ctx", "fsdp"),
            P("ctx", "fsdp"),
            P(("fsdp", "ctx")),
            P(),
            P(),
            P("ctx"),
        ),
        check_vma=False,
    )
```

```python
import functools

import jax
import jax.numpy as jnp
from jax import lax
from jax.experimental import pallas as pl
from jax.experimental.pallas import tpu as pltpu
from jax.sharding import PartitionSpec as P


WIN = 1024
REACH = 2
BLOCKED = -1e30

epsilon = 1e-06
query_scale = 168.0 ** (-0.5)

NT = (((1,), (1,)), ((), ()))


def shift(value, axis, steps):
    count = lax.axis_size(axis)
    initial, last = (max(0, -steps), min(count, count - steps))
    return lax.ppermute(value, axis, [(s, s + steps) for s in range(initial, last)])


def swap(value, axis, flip):
    return lax.ppermute(value, axis, [(s, s ^ flip) for s in range(lax.axis_size(axis))])


def dot(a, b, dims=(((1,), (0,)), ((), ()))):
    return lax.dot_general(a, b, dims, preferred_element_type=jnp.float32)


def everywhere(value, axes):
    for axis in axes:
        flip = 1
        while flip < lax.axis_size(axis):
            value = value + swap(value, axis, flip)
            flip *= 2
    return value


def share_of_columns(normed_turned, shard_rows):
    chips = lax.axis_size("ctx") // 2
    shares = lax.axis_size("fsdp")
    tokens = normed_turned.shape[1]
    blocks = normed_turned.reshape(chips, 2, shares, shard_rows // shares, tokens)
    return lax.dynamic_index_in_dim(blocks, lax.axis_index("fsdp"), 2, keepdims=False)


def start_columns(blocks):
    chips = blocks.shape[0]
    chip = lax.axis_index("ctx") // 2
    pieces = []
    for m in range(chips):
        piece = lax.dynamic_index_in_dim(blocks, chip ^ m, 0, keepdims=False)
        if m:
            piece = swap(piece, "ctx", 2 * m)
        pieces.append(piece)
    return pieces


def finish_columns(pieces, gate):
    chips = len(pieces)
    chip = lax.axis_index("ctx") // 2
    core = lax.axis_index("ctx") % 2
    shares = lax.axis_size("fsdp")
    share = lax.axis_index("fsdp")
    pieces, _ = lax.optimization_barrier((jnp.stack(pieces), gate))
    piece, tokens = pieces.shape[2:]
    kept = lax.dynamic_index_in_dim(pieces, core, 1, keepdims=False)
    other = lax.dynamic_index_in_dim(pieces, 1 - core, 1, keepdims=False)
    other = swap(other, "ctx", 1)
    first, second = jnp.where(core == 0, kept, other), jnp.where(core == 0, other, kept)
    both = jnp.stack([first, second], axis=1)
    bit = 1
    while bit < chips:
        grouped = both.reshape(chips // (2 * bit), 2, bit, 2, piece, tokens)
        both = jnp.where((chip & bit) > 0, grouped[:, ::-1], grouped).reshape(both.shape)
        bit *= 2
    mine = jnp.transpose(both, (2, 0, 1, 3)).reshape(piece, chips * 2 * tokens)
    columns = jnp.zeros((shares,) + mine.shape, mine.dtype)
    columns = lax.dynamic_update_index_in_dim(columns, mine, share, 0)
    for m in range(1, shares):
        part = swap(mine, "fsdp", m)
        columns = lax.dynamic_update_index_in_dim(columns, part, share ^ m, 0)
    return columns.reshape(shares * piece, chips * 2 * tokens)


def key_body(k_ref, v_ref, gain_ref, kv_ref):
    k = k_ref[...]
    inv = lax.rsqrt(jnp.mean(k * k, axis=1, keepdims=True) + epsilon)
    kv_ref[0] = (k * inv * gain_ref[...]).astype(jnp.bfloat16)
    kv_ref[1] = v_ref[...].astype(jnp.bfloat16)


def key_rows_of(projected, gain, kv_heads, head_dim):
    tokens = projected.shape[0]
    return pl.pallas_call(
        key_body,
        grid=(kv_heads,),
        in_specs=[
            pl.BlockSpec((tokens, head_dim), lambda g: (0, g)),
            pl.BlockSpec((tokens, head_dim), lambda g: (0, kv_heads + g)),
            pl.BlockSpec((1, head_dim), lambda g: (0, 0)),
        ],
        out_specs=pl.BlockSpec((2, tokens, head_dim), lambda g: (0, 0, g)),
        out_shape=jax.ShapeDtypeStruct((2, tokens, kv_heads * head_dim), jnp.bfloat16),
        name="key_rows",
    )(projected, projected, gain[None, :])


def key_grad_body(own_ref, near_ref, far_ref, k_ref, gain_ref, out_ref, sum_ref):
    total = own_ref[0] + near_ref[0].astype(jnp.float32) + far_ref[0].astype(jnp.float32)

    @pl.when((pl.program_id(0) == 0) & (pl.program_id(1) == 0))
    def _():
        sum_ref[...] = jnp.zeros_like(sum_ref)

    @pl.when(pl.program_id(0) == 0)
    def _():
        k = k_ref[...]
        inv = lax.rsqrt(jnp.mean(k * k, axis=1, keepdims=True) + epsilon)
        k_hat = k * inv
        u = total * gain_ref[...]
        out_ref[...] = (
            inv * (u - k_hat * jnp.mean(u * k_hat, axis=1, keepdims=True))
        ).astype(jnp.bfloat16)
        sum_ref[...] += jnp.sum(total * k_hat, axis=0, keepdims=True)

    @pl.when(pl.program_id(0) == 1)
    def _():
        out_ref[...] = total.astype(jnp.bfloat16)


def key_grads_of(own, near, far, projected, gain, kv_heads, head_dim):
    tokens = projected.shape[0]
    stacked = pl.BlockSpec((1, tokens, head_dim), lambda t, g: (t, 0, g))
    row = pl.BlockSpec((1, head_dim), lambda t, g: (0, 0))
    return pl.pallas_call(
        key_grad_body,
        grid=(2, kv_heads),
        in_specs=[
            stacked,
            stacked,
            stacked,
            pl.BlockSpec((tokens, head_dim), lambda t, g: (0, g)),
            row,
        ],
        out_specs=(
            pl.BlockSpec((tokens, head_dim), lambda t, g: (0, t * kv_heads + g)),
            row,
        ),
        out_shape=(
            jax.ShapeDtypeStruct((tokens, 2 * kv_heads * head_dim), jnp.bfloat16),
            jax.ShapeDtypeStruct((1, head_dim), jnp.float32),
        ),
        name="key_grads",
    )(own, near, far, projected, gain[None, :])


def normed_grad_body(part_ref, wide_ref, d_ref, x_ref, gain_ref, out_ref, dots_ref, dt_ref):
    @pl.when(pl.program_id(0) == 0)
    def _():
        dots_ref[...] = jnp.zeros_like(dots_ref)
        dt_ref[...] = jnp.transpose(d_ref[...])

    rounded = (part_ref[...] + dot(wide_ref[...], dt_ref[...])).astype(jnp.bfloat16)
    out_ref[...] = rounded
    gained = x_ref[...].astype(jnp.float32) * gain_ref[...]
    dots_ref[...] += jnp.sum(rounded.astype(jnp.float32) * gained, axis=0, keepdims=True)


def normed_grad(part, wide, d, turned, gain_column):
    width, tokens = part.shape
    cols = wide.shape[1]
    rows = max(r for r in range(128, 897, 128) if width % r == 0)
    by_row = pl.BlockSpec((rows, tokens), lambda i: (i, 0))
    return pl.pallas_call(
        normed_grad_body,
        grid=(width // rows,),
        in_specs=[
            by_row,
            pl.BlockSpec((rows, cols), lambda i: (i, 0)),
            pl.BlockSpec((tokens, cols), lambda i: (0, 0)),
            by_row,
            pl.BlockSpec((rows, 1), lambda i: (i, 0)),
        ],
        out_specs=(by_row, pl.BlockSpec((1, tokens), lambda i: (0, 0))),
        out_shape=(
            jax.ShapeDtypeStruct((width, tokens), jnp.bfloat16),
            jax.ShapeDtypeStruct((1, tokens), jnp.float32),
        ),
        scratch_shapes=[pltpu.VMEM((cols, tokens), jnp.bfloat16)],
        compiler_params=pltpu.CompilerParams(vmem_limit_bytes=40 << 20),
        name="normed_grad",
    )(part, wide, d, turned, gain_column)


def weight_grad_body(columns_ref, d_ref, k_ref, v_ref, sum_ref, *, scale):
    step = pl.program_id(0)
    product = dot(columns_ref[...], d_ref[...])

    @pl.when(step == 0)
    def _():
        sum_ref[...] = product

    @pl.when(step > 0)
    def _():
        sum_ref[...] += product

    @pl.when(step == pl.num_programs(0) - 1)
    def _():
        cut = k_ref.shape[1]
        k_ref[...] = (scale * sum_ref[:, :cut]).astype(k_ref.dtype)
        v_ref[...] = (scale * sum_ref[:, cut:]).astype(v_ref.dtype)


def weight_grads(columns, d, scale):
    rows, tokens = columns.shape
    cols = d.shape[1]
    chunk = tokens // 4
    out = pl.BlockSpec((rows, cols // 2), lambda i: (0, 0))
    shape = jax.ShapeDtypeStruct((rows, cols // 2), jnp.bfloat16)
    return pl.pallas_call(
        functools.partial(weight_grad_body, scale=scale),
        grid=(4,),
        in_specs=[
            pl.BlockSpec((rows, chunk), lambda i: (0, i)),
            pl.BlockSpec((chunk, cols), lambda i: (i, 0)),
        ],
        out_specs=(out, out),
        out_shape=(shape, shape),
        scratch_shapes=[pltpu.VMEM((rows, cols), jnp.float32)],
        compiler_params=pltpu.CompilerParams(vmem_limit_bytes=40 << 20),
        name="weight_grads",
    )(columns, d)


def attention_body(
    start_ref,
    ends_ref,
    q_ref,
    go_ref,
    own_ref,
    near_ref,
    far_ref,
    mult_ref,
    dq_ref,
    d_own_ref,
    d_near_ref,
    d_far_ref,
    sum_ref,
    bias_ref,
    k_ref,
    v_ref,
    kt_ref,
    vt_ref,
    dk_ref,
    dv_ref,
    *,
    rows,
    heads,
    segments,
):
    g = pl.program_id(0)
    s = pl.program_id(1)
    last = pl.num_programs(1) - 1
    tokens, head_dim = own_ref.shape[1:]
    reach = WIN
    span = reach + rows
    offset = pl.multiple_of(s * rows, rows)

    @pl.when(g == 0)
    def _():
        first = start_ref[0]
        key_pos = (first - reach + s * rows) + lax.broadcasted_iota(jnp.int32, (span, 1), 0)
        query_pos = (first + s * rows) + lax.broadcasted_iota(jnp.int32, (1, rows), 1)
        key_seg = jnp.zeros((span, 1), jnp.int32)
        query_seg = jnp.zeros((1, rows), jnp.int32)
        for i in range(segments):
            key_seg += (ends_ref[i] <= key_pos).astype(jnp.int32)
            query_seg += (ends_ref[i] <= query_pos).astype(jnp.int32)
        distance = query_pos - key_pos
        allowed = (
            (key_seg == query_seg) & (distance >= 0) & (distance < WIN) & (key_pos >= 0)
        )
        bias_ref[s] = jnp.where(allowed, 0.0, BLOCKED)

    @pl.when(s == 0)
    def _():
        for at, ref in enumerate((far_ref, near_ref, own_ref)):
            k_ref[pl.ds(at * tokens, tokens), :] = ref[0]
            v_ref[pl.ds(at * tokens, tokens), :] = ref[1]
        dk_ref[...] = jnp.zeros_like(dk_ref)
        dv_ref[...] = jnp.zeros_like(dv_ref)

    @pl.when((s == 0) & (g == 0))
    def _():
        sum_ref[...] = jnp.zeros_like(sum_ref)

    k = k_ref[pl.ds(offset, span), :]
    v = v_ref[pl.ds(offset, span), :]
    kt_ref[...] = jnp.transpose(k)
    vt_ref[...] = jnp.transpose(v)
    mult = mult_ref[...]
    bias = bias_ref[s]
    for h in range(heads):
        at = slice(h * head_dim, (h + 1) * head_dim)
        q = q_ref[:, at]
        inv = lax.rsqrt(jnp.mean(q * q, axis=1, keepdims=True) + epsilon)
        q_hat = q * inv
        q16 = (q_hat * mult).astype(jnp.bfloat16)
        go = go_ref[:, at]
        weights = jnp.exp(dot(k, q16, NT) + bias)
        over = 1.0 / jnp.sum(weights, axis=0, keepdims=True)
        out_t = dot(vt_ref[...], weights.astype(jnp.bfloat16)) * over
        delta = jnp.sum(jnp.transpose(go.astype(jnp.float32)) * out_t, axis=0, keepdims=True)
        probs = weights * over
        dv_ref[pl.ds(offset, span), :] += dot(probs.astype(jnp.bfloat16), go)
        d_scores = (probs * (dot(v, go, NT) - delta)).astype(jnp.bfloat16)
        dk_ref[pl.ds(offset, span), :] += dot(d_scores, q16)
        d_query = jnp.transpose(dot(kt_ref[...], d_scores))
        u = d_query * mult
        dq_ref[:, at] = (
            inv * (u - q_hat * jnp.mean(u * q_hat, axis=1, keepdims=True))
        ).astype(jnp.bfloat16)
        sum_ref[...] += jnp.sum(d_query * q_hat, axis=0, keepdims=True)

    @pl.when(s == last)
    def _():
        for at, ref in enumerate((d_far_ref, d_near_ref, d_own_ref)):
            ref[0] = dk_ref[pl.ds(at * tokens, tokens), :].astype(ref.dtype)
            ref[1] = dv_ref[pl.ds(at * tokens, tokens), :].astype(ref.dtype)


def attention(start, ends, q_raw, go, own, near, far, mult, kv_heads, head_dim):
    tokens, q_cols = q_raw.shape
    heads = q_cols // (kv_heads * head_dim)
    rows = min(256, tokens)
    steps = tokens // rows
    span = WIN + rows
    stacked = pl.BlockSpec((2, tokens, head_dim), lambda g, s, *_: (0, 0, g))
    by_query = pl.BlockSpec((rows, heads * head_dim), lambda g, s, *_: (s, g))
    row = pl.BlockSpec((1, head_dim), lambda g, s, *_: (0, 0))
    half = jax.ShapeDtypeStruct(own.shape, jnp.bfloat16)
    keys = WIN + tokens
    return pl.pallas_call(
        functools.partial(attention_body, rows=rows, heads=heads, segments=ends.shape[0]),
        grid_spec=pltpu.PrefetchScalarGridSpec(
            num_scalar_prefetch=2,
            grid=(kv_heads, steps),
            in_specs=[by_query, by_query, stacked, stacked, stacked, row],
            out_specs=(by_query, stacked, stacked, stacked, row),
            scratch_shapes=[
                pltpu.VMEM((steps, span, rows), jnp.float32),
                pltpu.VMEM((keys, head_dim), jnp.bfloat16),
                pltpu.VMEM((keys, head_dim), jnp.bfloat16),
                pltpu.VMEM((head_dim, span), jnp.bfloat16),
                pltpu.VMEM((head_dim, span), jnp.bfloat16),
                pltpu.VMEM((keys, head_dim), jnp.float32),
                pltpu.VMEM((keys, head_dim), jnp.float32),
            ],
        ),
        out_shape=(
            jax.ShapeDtypeStruct((tokens, q_cols), jnp.bfloat16),
            jax.ShapeDtypeStruct(own.shape, jnp.float32),
            half,
            half,
            jax.ShapeDtypeStruct((1, head_dim), jnp.float32),
        ),
        compiler_params=pltpu.CompilerParams(
            dimension_semantics=("arbitrary", "arbitrary"), vmem_limit_bytes=48 << 20
        ),
        name="attention",
    )(start, ends, q_raw, go, own, near, far, mult)


def layer(
    inputs,
    output_cotangent,
    w_query,
    key_projection,
    value_projection,
    norm_gain,
    q_gain,
    key_norm_gain,
    half_lengths,
):
    tokens, model_width = inputs.shape
    head_dim = q_gain.shape[0]
    kv_cols = key_projection.shape[1]
    kv_heads = kv_cols // head_dim
    ctx_count = lax.axis_size("ctx")
    fsdp_count = lax.axis_size("fsdp")
    ctx_index = lax.axis_index("ctx")
    fsdp_index = lax.axis_index("fsdp")
    on_first_core = ctx_index % 2 == 0
    grad_scale = float(tokens * ctx_count) ** (-0.5)
    shard_rows = w_query.shape[0]
    features = model_width // fsdp_count

    key_value = jnp.concatenate([key_projection, value_projection], axis=1)
    wide_kv = lax.all_gather(key_value, "ctx", axis=0, tiled=True)
    wide_q = lax.all_gather(w_query, "ctx", axis=0, tiled=True)

    widened = inputs.astype(jnp.float32)
    turned = jnp.transpose(inputs)
    inv_rms = lax.rsqrt(jnp.mean(widened * widened, axis=1, keepdims=True) + epsilon)
    x_hat = widened * inv_rms
    normed = lax.optimization_barrier((x_hat * norm_gain).astype(jnp.bfloat16))
    inv_row = jnp.transpose(inv_rms)

    kv_raw = dot(normed, wide_kv)
    own = key_rows_of(kv_raw, key_norm_gain, kv_heads, head_dim)
    normed_turned = (turned.astype(jnp.float32) * inv_row * norm_gain[:, None]).astype(
        jnp.bfloat16
    )
    blocks, gain_column, own = lax.optimization_barrier(
        (share_of_columns(normed_turned, shard_rows), norm_gain[:, None], own)
    )
    far = shift(own, "ctx", REACH)
    picked = jnp.where(on_first_core, own, far)
    near = swap(picked, "ctx", 1)

    blocks, _ = lax.optimization_barrier((blocks, wide_q))
    pieces = start_columns(blocks)
    q_raw = dot(normed, wide_q)
    query_multiplier = (q_gain * query_scale)[None, :]
    dq16, d_own, d_near, d_far, q_sum = attention(
        jnp.full((1,), ctx_index * tokens, jnp.int32),
        jnp.cumsum(half_lengths).astype(jnp.int32),
        q_raw,
        output_cotangent,
        own,
        near,
        far,
        query_multiplier,
        kv_heads,
        head_dim,
    )

    crossed = swap(d_near, "ctx", 1)
    nothing = jnp.zeros_like(crossed)
    outgoing = d_far + jnp.where(on_first_core, nothing, crossed)
    returned = shift(outgoing, "ctx", -REACH)
    all_dq = lax.all_gather(dq16, "ctx", axis=0, tiled=True)
    query_part = dot(wide_q, dq16, NT)
    query_part = lax.optimization_barrier(query_part)
    dkv16, k_sum = key_grads_of(
        d_own,
        jnp.where(on_first_core, crossed, nothing),
        returned,
        kv_raw,
        key_norm_gain,
        kv_heads,
        head_dim,
    )
    all_dkv = lax.all_gather(dkv16, "ctx", axis=0, tiled=True)

    columns = finish_columns(pieces, dq16)

    head_part, row_dot = normed_grad(query_part, wide_kv, dkv16, turned, gain_column)
    row_dot = everywhere(row_dot * inv_row, ("fsdp",))

    def part_of(array, index):
        return lax.dynamic_slice_in_dim(array, index * features, features, 0)

    sent = [part_of(head_part, fsdp_index ^ m) for m in range(1, fsdp_count)]
    sent = [swap(part, "fsdp", 1 + m) for m, part in enumerate(sent)]
    d_mine = part_of(head_part, fsdp_index).astype(jnp.float32)
    for part in sent:
        d_mine = d_mine + part.astype(jnp.float32)
    hat_mine = part_of(turned, fsdp_index).astype(jnp.float32) * inv_row
    upstream = d_mine * part_of(norm_gain, fsdp_index)[:, None]
    grad_inputs = jnp.transpose(
        (inv_row * (upstream - hat_mine * row_dot / model_width)).astype(jnp.bfloat16)
    )
    norm_row_dots = row_dot[0] * float(model_width) ** (-0.5)
    gain_term = grad_scale * jnp.sum(d_mine * hat_mine, axis=1)
    gain_sum = lax.dynamic_slice_in_dim(
        everywhere(gain_term, ("ctx",)),
        ctx_index * (features // ctx_count),
        features // ctx_count,
        0,
    )

    q_weights = (grad_scale * dot(columns, all_dq)).astype(jnp.bfloat16)
    k_weights, v_weights = weight_grads(columns, all_dkv, grad_scale)

    gains = jnp.concatenate([q_sum * (grad_scale * query_scale), k_sum * grad_scale], axis=0)
    gains = everywhere(gains, ("fsdp",))
    gains = everywhere(gains, ("ctx",))
    return (
        grad_inputs,
        q_weights,
        k_weights,
        v_weights,
        gain_sum,
        gains[0],
        gains[1],
        norm_row_dots,
    )


def solution(mesh):
    placed = (
        P("ctx", None),
        P("ctx", "fsdp"),
        P("ctx", "fsdp"),
        P("ctx", "fsdp"),
        P("ctx", "fsdp"),
        P(),
        P(),
        P(),
        P(),
    )
    return jax.shard_map(
        layer,
        mesh=mesh,
        in_specs=placed,
        out_specs=(
            P("ctx", "fsdp"),
            P("ctx", "fsdp"),
            P("ctx", "fsdp"),
            P("ctx", "fsdp"),
            P(("fsdp", "ctx")),
            P(),
            P(),
            P("ctx"),
        ),
        check_vma=False,
    )
```

```python
import functools

import jax
import jax.numpy as jnp
from jax import lax
from jax.experimental import pallas as pl
from jax.experimental.pallas import tpu as pltpu
from jax.sharding import PartitionSpec as P


WIN = 1024
REACH = 2
BLOCKED = -1e30

epsilon = 1e-06
query_scale = 168.0 ** (-0.5)

NT = (((1,), (1,)), ((), ()))


def shift(value, axis, steps):
    count = lax.axis_size(axis)
    initial, last = (max(0, -steps), min(count, count - steps))
    return lax.ppermute(value, axis, [(s, s + steps) for s in range(initial, last)])


def swap(value, axis, flip):
    return lax.ppermute(value, axis, [(s, s ^ flip) for s in range(lax.axis_size(axis))])


def dot(a, b, dims=(((1,), (0,)), ((), ()))):
    return lax.dot_general(a, b, dims, preferred_element_type=jnp.float32)


def everywhere(value, axes):
    for axis in axes:
        flip = 1
        while flip < lax.axis_size(axis):
            value = value + swap(value, axis, flip)
            flip *= 2
    return value


def share_of_columns(normed_turned, shard_rows):
    chips = lax.axis_size("ctx") // 2
    shares = lax.axis_size("fsdp")
    tokens = normed_turned.shape[1]
    blocks = normed_turned.reshape(chips, 2, shares, shard_rows // shares, tokens)
    return lax.dynamic_index_in_dim(blocks, lax.axis_index("fsdp"), 2, keepdims=False)


def start_columns(blocks):
    chips = blocks.shape[0]
    chip = lax.axis_index("ctx") // 2
    pieces = []
    for m in range(chips):
        piece = lax.dynamic_index_in_dim(blocks, chip ^ m, 0, keepdims=False)
        if m:
            piece = swap(piece, "ctx", 2 * m)
        pieces.append(piece)
    return pieces


def finish_columns(pieces, gate):
    chips = len(pieces)
    chip = lax.axis_index("ctx") // 2
    core = lax.axis_index("ctx") % 2
    shares = lax.axis_size("fsdp")
    share = lax.axis_index("fsdp")
    pieces, _ = lax.optimization_barrier((jnp.stack(pieces), gate))
    piece, tokens = pieces.shape[2:]
    kept = lax.dynamic_index_in_dim(pieces, core, 1, keepdims=False)
    other = lax.dynamic_index_in_dim(pieces, 1 - core, 1, keepdims=False)
    other = swap(other, "ctx", 1)
    first, second = jnp.where(core == 0, kept, other), jnp.where(core == 0, other, kept)
    both = jnp.stack([first, second], axis=1)
    bit = 1
    while bit < chips:
        grouped = both.reshape(chips // (2 * bit), 2, bit, 2, piece, tokens)
        both = jnp.where((chip & bit) > 0, grouped[:, ::-1], grouped).reshape(both.shape)
        bit *= 2
    mine = jnp.transpose(both, (2, 0, 1, 3)).reshape(piece, chips * 2 * tokens)
    columns = jnp.zeros((shares,) + mine.shape, mine.dtype)
    columns = lax.dynamic_update_index_in_dim(columns, mine, share, 0)
    for m in range(1, shares):
        part = swap(mine, "fsdp", m)
        columns = lax.dynamic_update_index_in_dim(columns, part, share ^ m, 0)
    return columns.reshape(shares * piece, chips * 2 * tokens)


def key_body(k_ref, v_ref, gain_ref, kv_ref):
    k = k_ref[...]
    inv = lax.rsqrt(jnp.mean(k * k, axis=1, keepdims=True) + epsilon)
    kv_ref[0] = (k * inv * gain_ref[...]).astype(jnp.bfloat16)
    kv_ref[1] = v_ref[...].astype(jnp.bfloat16)


def key_rows_of(projected, gain, kv_heads, head_dim):
    tokens = projected.shape[0]
    return pl.pallas_call(
        key_body,
        grid=(kv_heads,),
        in_specs=[
            pl.BlockSpec((tokens, head_dim), lambda g: (0, g)),
            pl.BlockSpec((tokens, head_dim), lambda g: (0, kv_heads + g)),
            pl.BlockSpec((1, head_dim), lambda g: (0, 0)),
        ],
        out_specs=pl.BlockSpec((2, tokens, head_dim), lambda g: (0, 0, g)),
        out_shape=jax.ShapeDtypeStruct((2, tokens, kv_heads * head_dim), jnp.bfloat16),
        name="key_rows",
    )(projected, projected, gain[None, :])


def key_grad_body(own_ref, near_ref, far_ref, k_ref, gain_ref, out_ref, sum_ref):
    total = own_ref[0] + near_ref[0].astype(jnp.float32) + far_ref[0].astype(jnp.float32)

    @pl.when((pl.program_id(0) == 0) & (pl.program_id(1) == 0))
    def _():
        sum_ref[...] = jnp.zeros_like(sum_ref)

    @pl.when(pl.program_id(0) == 0)
    def _():
        k = k_ref[...]
        inv = lax.rsqrt(jnp.mean(k * k, axis=1, keepdims=True) + epsilon)
        k_hat = k * inv
        u = total * gain_ref[...]
        out_ref[...] = (
            inv * (u - k_hat * jnp.mean(u * k_hat, axis=1, keepdims=True))
        ).astype(jnp.bfloat16)
        sum_ref[...] += jnp.sum(total * k_hat, axis=0, keepdims=True)

    @pl.when(pl.program_id(0) == 1)
    def _():
        out_ref[...] = total.astype(jnp.bfloat16)


def key_grads_of(own, near, far, projected, gain, kv_heads, head_dim):
    tokens = projected.shape[0]
    stacked = pl.BlockSpec((1, tokens, head_dim), lambda t, g: (t, 0, g))
    row = pl.BlockSpec((1, head_dim), lambda t, g: (0, 0))
    return pl.pallas_call(
        key_grad_body,
        grid=(2, kv_heads),
        in_specs=[
            stacked,
            stacked,
            stacked,
            pl.BlockSpec((tokens, head_dim), lambda t, g: (0, g)),
            row,
        ],
        out_specs=(
            pl.BlockSpec((tokens, head_dim), lambda t, g: (0, t * kv_heads + g)),
            row,
        ),
        out_shape=(
            jax.ShapeDtypeStruct((tokens, 2 * kv_heads * head_dim), jnp.bfloat16),
            jax.ShapeDtypeStruct((1, head_dim), jnp.float32),
        ),
        name="key_grads",
    )(own, near, far, projected, gain[None, :])


def normed_grad_body(part_ref, wide_ref, d_ref, x_ref, gain_ref, out_ref, dots_ref, dt_ref):
    @pl.when(pl.program_id(0) == 0)
    def _():
        dots_ref[...] = jnp.zeros_like(dots_ref)
        dt_ref[...] = jnp.transpose(d_ref[...])

    rounded = (part_ref[...] + dot(wide_ref[...], dt_ref[...])).astype(jnp.bfloat16)
    out_ref[...] = rounded
    gained = x_ref[...].astype(jnp.float32) * gain_ref[...]
    dots_ref[...] += jnp.sum(rounded.astype(jnp.float32) * gained, axis=0, keepdims=True)


def normed_grad(part, wide, d, turned, gain_column):
    width, tokens = part.shape
    cols = wide.shape[1]
    rows = max(r for r in range(128, 897, 128) if width % r == 0)
    by_row = pl.BlockSpec((rows, tokens), lambda i: (i, 0))
    return pl.pallas_call(
        normed_grad_body,
        grid=(width // rows,),
        in_specs=[
            by_row,
            pl.BlockSpec((rows, cols), lambda i: (i, 0)),
            pl.BlockSpec((tokens, cols), lambda i: (0, 0)),
            by_row,
            pl.BlockSpec((rows, 1), lambda i: (i, 0)),
        ],
        out_specs=(by_row, pl.BlockSpec((1, tokens), lambda i: (0, 0))),
        out_shape=(
            jax.ShapeDtypeStruct((width, tokens), jnp.bfloat16),
            jax.ShapeDtypeStruct((1, tokens), jnp.float32),
        ),
        scratch_shapes=[pltpu.VMEM((cols, tokens), jnp.bfloat16)],
        compiler_params=pltpu.CompilerParams(vmem_limit_bytes=40 << 20),
        name="normed_grad",
    )(part, wide, d, turned, gain_column)


CHUNKS = 4


def weight_grad_body(
    columns_ref, d_ref, k_ref, v_ref, left_ref, right_ref, sum_ref, left_sems, right_sems, *, scale
):
    chunk = right_ref.shape[1]

    def fetch(i):
        at = pl.ds(pl.multiple_of(i * chunk, chunk), chunk)
        return (
            pltpu.make_async_copy(columns_ref.at[:, at], left_ref.at[i], left_sems.at[i]),
            pltpu.make_async_copy(d_ref.at[at, :], right_ref.at[i], right_sems.at[i]),
        )

    for i in range(CHUNKS):
        for copy in fetch(i):
            copy.start()
    sum_ref[...] = jnp.zeros_like(sum_ref)

    @pl.loop(0, CHUNKS)
    def _(i):
        for copy in fetch(i):
            copy.wait()
        sum_ref[...] += dot(left_ref[i], right_ref[i])

    cut = k_ref.shape[1]
    k_ref[...] = (scale * sum_ref[:, :cut]).astype(k_ref.dtype)
    v_ref[...] = (scale * sum_ref[:, cut:]).astype(v_ref.dtype)


def weight_grads(columns, d, scale):
    rows, tokens = columns.shape
    cols = d.shape[1]
    chunk = tokens // CHUNKS
    vmem = pl.BlockSpec(memory_space=pltpu.MemorySpace.VMEM)
    hbm = pl.BlockSpec(memory_space=pltpu.MemorySpace.HBM)
    shape = jax.ShapeDtypeStruct((rows, cols // 2), jnp.bfloat16)
    return pl.pallas_call(
        functools.partial(weight_grad_body, scale=scale),
        in_specs=[hbm, hbm],
        out_specs=(vmem, vmem),
        out_shape=(shape, shape),
        scratch_shapes=[
            pltpu.VMEM((CHUNKS, rows, chunk), jnp.bfloat16),
            pltpu.VMEM((CHUNKS, chunk, cols), jnp.bfloat16),
            pltpu.VMEM((rows, cols), jnp.float32),
            pltpu.SemaphoreType.DMA((CHUNKS,)),
            pltpu.SemaphoreType.DMA((CHUNKS,)),
        ],
        compiler_params=pltpu.CompilerParams(vmem_limit_bytes=58 << 20),
        name="weight_grads",
    )(columns, d)


def attention_body(
    start_ref,
    ends_ref,
    q_ref,
    go_ref,
    own_ref,
    near_ref,
    far_ref,
    mult_ref,
    dq_ref,
    d_own_ref,
    d_near_ref,
    d_far_ref,
    sum_ref,
    bias_ref,
    k_ref,
    v_ref,
    kt_ref,
    vt_ref,
    dk_ref,
    dv_ref,
    *,
    rows,
    heads,
    segments,
):
    g = pl.program_id(0)
    s = pl.program_id(1)
    last = pl.num_programs(1) - 1
    tokens, head_dim = own_ref.shape[1:]
    reach = WIN
    span = reach + rows
    offset = pl.multiple_of(s * rows, rows)

    @pl.when(g == 0)
    def _():
        first = start_ref[0]
        key_pos = (first - reach + s * rows) + lax.broadcasted_iota(jnp.int32, (span, 1), 0)
        query_pos = (first + s * rows) + lax.broadcasted_iota(jnp.int32, (1, rows), 1)
        key_seg = jnp.zeros((span, 1), jnp.int32)
        query_seg = jnp.zeros((1, rows), jnp.int32)
        for i in range(segments):
            key_seg += (ends_ref[i] <= key_pos).astype(jnp.int32)
            query_seg += (ends_ref[i] <= query_pos).astype(jnp.int32)
        distance = query_pos - key_pos
        allowed = (
            (key_seg == query_seg) & (distance >= 0) & (distance < WIN) & (key_pos >= 0)
        )
        bias_ref[s] = jnp.where(allowed, 0.0, BLOCKED)

    @pl.when(s == 0)
    def _():
        for at, ref in enumerate((far_ref, near_ref, own_ref)):
            k_ref[pl.ds(at * tokens, tokens), :] = ref[0]
            v_ref[pl.ds(at * tokens, tokens), :] = ref[1]
        dk_ref[...] = jnp.zeros_like(dk_ref)
        dv_ref[...] = jnp.zeros_like(dv_ref)

    @pl.when((s == 0) & (g == 0))
    def _():
        sum_ref[...] = jnp.zeros_like(sum_ref)

    k = k_ref[pl.ds(offset, span), :]
    v = v_ref[pl.ds(offset, span), :]
    kt_ref[...] = jnp.transpose(k)
    vt_ref[...] = jnp.transpose(v)
    mult = mult_ref[...]
    bias = bias_ref[s]
    for h in range(heads):
        at = slice(h * head_dim, (h + 1) * head_dim)
        q = q_ref[:, at]
        inv = lax.rsqrt(jnp.mean(q * q, axis=1, keepdims=True) + epsilon)
        q_hat = q * inv
        q16 = (q_hat * mult).astype(jnp.bfloat16)
        go = go_ref[:, at]
        weights = jnp.exp(dot(k, q16, NT) + bias)
        over = 1.0 / jnp.sum(weights, axis=0, keepdims=True)
        out_t = dot(vt_ref[...], weights.astype(jnp.bfloat16)) * over
        delta = jnp.sum(jnp.transpose(go.astype(jnp.float32)) * out_t, axis=0, keepdims=True)
        probs = weights * over
        dv_ref[pl.ds(offset, span), :] += dot(probs.astype(jnp.bfloat16), go)
        d_scores = (probs * (dot(v, go, NT) - delta)).astype(jnp.bfloat16)
        dk_ref[pl.ds(offset, span), :] += dot(d_scores, q16)
        d_query = jnp.transpose(dot(kt_ref[...], d_scores))
        u = d_query * mult
        dq_ref[:, at] = (
            inv * (u - q_hat * jnp.mean(u * q_hat, axis=1, keepdims=True))
        ).astype(jnp.bfloat16)
        sum_ref[...] += jnp.sum(d_query * q_hat, axis=0, keepdims=True)

    @pl.when(s == last)
    def _():
        for at, ref in enumerate((d_far_ref, d_near_ref, d_own_ref)):
            ref[0] = dk_ref[pl.ds(at * tokens, tokens), :].astype(ref.dtype)
            ref[1] = dv_ref[pl.ds(at * tokens, tokens), :].astype(ref.dtype)


def attention(start, ends, q_raw, go, own, near, far, mult, kv_heads, head_dim):
    tokens, q_cols = q_raw.shape
    heads = q_cols // (kv_heads * head_dim)
    rows = min(256, tokens)
    steps = tokens // rows
    span = WIN + rows
    stacked = pl.BlockSpec((2, tokens, head_dim), lambda g, s, *_: (0, 0, g))
    by_query = pl.BlockSpec((rows, heads * head_dim), lambda g, s, *_: (s, g))
    row = pl.BlockSpec((1, head_dim), lambda g, s, *_: (0, 0))
    half = jax.ShapeDtypeStruct(own.shape, jnp.bfloat16)
    keys = WIN + tokens
    return pl.pallas_call(
        functools.partial(attention_body, rows=rows, heads=heads, segments=ends.shape[0]),
        grid_spec=pltpu.PrefetchScalarGridSpec(
            num_scalar_prefetch=2,
            grid=(kv_heads, steps),
            in_specs=[by_query, by_query, stacked, stacked, stacked, row],
            out_specs=(by_query, stacked, stacked, stacked, row),
            scratch_shapes=[
                pltpu.VMEM((steps, span, rows), jnp.float32),
                pltpu.VMEM((keys, head_dim), jnp.bfloat16),
                pltpu.VMEM((keys, head_dim), jnp.bfloat16),
                pltpu.VMEM((head_dim, span), jnp.bfloat16),
                pltpu.VMEM((head_dim, span), jnp.bfloat16),
                pltpu.VMEM((keys, head_dim), jnp.float32),
                pltpu.VMEM((keys, head_dim), jnp.float32),
            ],
        ),
        out_shape=(
            jax.ShapeDtypeStruct((tokens, q_cols), jnp.bfloat16),
            jax.ShapeDtypeStruct(own.shape, jnp.float32),
            half,
            half,
            jax.ShapeDtypeStruct((1, head_dim), jnp.float32),
        ),
        compiler_params=pltpu.CompilerParams(
            dimension_semantics=("arbitrary", "arbitrary"), vmem_limit_bytes=48 << 20
        ),
        name="attention",
    )(start, ends, q_raw, go, own, near, far, mult)


def layer(
    inputs,
    output_cotangent,
    w_query,
    key_projection,
    value_projection,
    norm_gain,
    q_gain,
    key_norm_gain,
    half_lengths,
):
    tokens, model_width = inputs.shape
    head_dim = q_gain.shape[0]
    kv_cols = key_projection.shape[1]
    kv_heads = kv_cols // head_dim
    ctx_count = lax.axis_size("ctx")
    fsdp_count = lax.axis_size("fsdp")
    ctx_index = lax.axis_index("ctx")
    fsdp_index = lax.axis_index("fsdp")
    on_first_core = ctx_index % 2 == 0
    grad_scale = float(tokens * ctx_count) ** (-0.5)
    shard_rows = w_query.shape[0]
    features = model_width // fsdp_count

    key_value = jnp.concatenate([key_projection, value_projection], axis=1)
    wide_kv = lax.all_gather(key_value, "ctx", axis=0, tiled=True)
    wide_q = lax.all_gather(w_query, "ctx", axis=0, tiled=True)

    widened = inputs.astype(jnp.float32)
    turned = jnp.transpose(inputs)
    inv_rms = lax.rsqrt(jnp.mean(widened * widened, axis=1, keepdims=True) + epsilon)
    x_hat = widened * inv_rms
    normed = lax.optimization_barrier((x_hat * norm_gain).astype(jnp.bfloat16))
    inv_row = jnp.transpose(inv_rms)

    kv_raw = dot(normed, wide_kv)
    own = key_rows_of(kv_raw, key_norm_gain, kv_heads, head_dim)
    normed_turned = (turned.astype(jnp.float32) * inv_row * norm_gain[:, None]).astype(
        jnp.bfloat16
    )
    blocks, gain_column, own = lax.optimization_barrier(
        (share_of_columns(normed_turned, shard_rows), norm_gain[:, None], own)
    )
    far = shift(own, "ctx", REACH)
    picked = jnp.where(on_first_core, own, far)
    near = swap(picked, "ctx", 1)

    blocks, _ = lax.optimization_barrier((blocks, wide_q))
    pieces = start_columns(blocks)
    q_raw = dot(normed, wide_q)
    query_multiplier = (q_gain * query_scale)[None, :]
    dq16, d_own, d_near, d_far, q_sum = attention(
        jnp.full((1,), ctx_index * tokens, jnp.int32),
        jnp.cumsum(half_lengths).astype(jnp.int32),
        q_raw,
        output_cotangent,
        own,
        near,
        far,
        query_multiplier,
        kv_heads,
        head_dim,
    )

    crossed = swap(d_near, "ctx", 1)
    nothing = jnp.zeros_like(crossed)
    outgoing = d_far + jnp.where(on_first_core, nothing, crossed)
    returned = shift(outgoing, "ctx", -REACH)
    all_dq = lax.all_gather(dq16, "ctx", axis=0, tiled=True)
    query_part = dot(wide_q, dq16, NT)
    query_part = lax.optimization_barrier(query_part)
    dkv16, k_sum = key_grads_of(
        d_own,
        jnp.where(on_first_core, crossed, nothing),
        returned,
        kv_raw,
        key_norm_gain,
        kv_heads,
        head_dim,
    )
    all_dkv = lax.all_gather(dkv16, "ctx", axis=0, tiled=True)

    columns = finish_columns(pieces, dq16)

    head_part, row_dot = normed_grad(query_part, wide_kv, dkv16, turned, gain_column)
    row_dot = everywhere(row_dot * inv_row, ("fsdp",))

    def part_of(array, index):
        return lax.dynamic_slice_in_dim(array, index * features, features, 0)

    sent = [part_of(head_part, fsdp_index ^ m) for m in range(1, fsdp_count)]
    sent = [swap(part, "fsdp", 1 + m) for m, part in enumerate(sent)]
    d_mine = part_of(head_part, fsdp_index).astype(jnp.float32)
    for part in sent:
        d_mine = d_mine + part.astype(jnp.float32)
    hat_mine = part_of(turned, fsdp_index).astype(jnp.float32) * inv_row
    upstream = d_mine * part_of(norm_gain, fsdp_index)[:, None]
    grad_inputs = jnp.transpose(
        (inv_row * (upstream - hat_mine * row_dot / model_width)).astype(jnp.bfloat16)
    )
    norm_row_dots = row_dot[0] * float(model_width) ** (-0.5)
    gain_term = grad_scale * jnp.sum(d_mine * hat_mine, axis=1)
    gain_sum = lax.dynamic_slice_in_dim(
        everywhere(gain_term, ("ctx",)),
        ctx_index * (features // ctx_count),
        features // ctx_count,
        0,
    )

    q_weights = (grad_scale * dot(columns, all_dq)).astype(jnp.bfloat16)
    k_weights, v_weights = weight_grads(columns, all_dkv, grad_scale)

    gains = jnp.concatenate([q_sum * (grad_scale * query_scale), k_sum * grad_scale], axis=0)
    gains = everywhere(gains, ("fsdp",))
    gains = everywhere(gains, ("ctx",))
    return (
        grad_inputs,
        q_weights,
        k_weights,
        v_weights,
        gain_sum,
        gains[0],
        gains[1],
        norm_row_dots,
    )


def solution(mesh):
    placed = (
        P("ctx", None),
        P("ctx", "fsdp"),
        P("ctx", "fsdp"),
        P("ctx", "fsdp"),
        P("ctx", "fsdp"),
        P(),
        P(),
        P(),
        P(),
    )
    return jax.shard_map(
        layer,
        mesh=mesh,
        in_specs=placed,
        out_specs=(
            P("ctx", "fsdp"),
            P("ctx", "fsdp"),
            P("ctx", "fsdp"),
            P("ctx", "fsdp"),
            P(("fsdp", "ctx")),
            P(),
            P(),
            P("ctx"),
        ),
        check_vma=False,
    )
```

```python
import functools

import jax
import jax.numpy as jnp
from jax import lax
from jax.experimental import pallas as pl
from jax.experimental.pallas import tpu as pltpu
from jax.sharding import PartitionSpec as P


WIN = 1024
REACH = 2
BLOCKED = -1e30

epsilon = 1e-06
query_scale = 168.0 ** (-0.5)

NT = (((1,), (1,)), ((), ()))


def shift(value, axis, steps):
    count = lax.axis_size(axis)
    initial, last = (max(0, -steps), min(count, count - steps))
    return lax.ppermute(value, axis, [(s, s + steps) for s in range(initial, last)])


def swap(value, axis, flip):
    return lax.ppermute(value, axis, [(s, s ^ flip) for s in range(lax.axis_size(axis))])


def dot(a, b, dims=(((1,), (0,)), ((), ()))):
    return lax.dot_general(a, b, dims, preferred_element_type=jnp.float32)


def everywhere(value, axes):
    for axis in axes:
        flip = 1
        while flip < lax.axis_size(axis):
            value = value + swap(value, axis, flip)
            flip *= 2
    return value


def share_of_columns(normed_turned, shard_rows):
    chips = lax.axis_size("ctx") // 2
    shares = lax.axis_size("fsdp")
    tokens = normed_turned.shape[1]
    blocks = normed_turned.reshape(chips, 2, shares, shard_rows // shares, tokens)
    return lax.dynamic_index_in_dim(blocks, lax.axis_index("fsdp"), 2, keepdims=False)


def start_columns(blocks):
    chips = blocks.shape[0]
    chip = lax.axis_index("ctx") // 2
    pieces = []
    for m in range(chips):
        piece = lax.dynamic_index_in_dim(blocks, chip ^ m, 0, keepdims=False)
        if m:
            piece = swap(piece, "ctx", 2 * m)
        pieces.append(piece)
    return pieces


def finish_columns(pieces, gate):
    chips = len(pieces)
    chip = lax.axis_index("ctx") // 2
    core = lax.axis_index("ctx") % 2
    shares = lax.axis_size("fsdp")
    share = lax.axis_index("fsdp")
    pieces, _ = lax.optimization_barrier((jnp.stack(pieces), gate))
    piece, tokens = pieces.shape[2:]
    kept = lax.dynamic_index_in_dim(pieces, core, 1, keepdims=False)
    other = lax.dynamic_index_in_dim(pieces, 1 - core, 1, keepdims=False)
    other = swap(other, "ctx", 1)
    first, second = jnp.where(core == 0, kept, other), jnp.where(core == 0, other, kept)
    both = jnp.stack([first, second], axis=1)
    bit = 1
    while bit < chips:
        grouped = both.reshape(chips // (2 * bit), 2, bit, 2, piece, tokens)
        both = jnp.where((chip & bit) > 0, grouped[:, ::-1], grouped).reshape(both.shape)
        bit *= 2
    mine = jnp.transpose(both, (2, 0, 1, 3)).reshape(piece, chips * 2 * tokens)
    columns = jnp.zeros((shares,) + mine.shape, mine.dtype)
    columns = lax.dynamic_update_index_in_dim(columns, mine, share, 0)
    for m in range(1, shares):
        part = swap(mine, "fsdp", m)
        columns = lax.dynamic_update_index_in_dim(columns, part, share ^ m, 0)
    return columns.reshape(shares * piece, chips * 2 * tokens)


def key_body(k_ref, v_ref, gain_ref, kv_ref):
    k = k_ref[...]
    inv = lax.rsqrt(jnp.mean(k * k, axis=1, keepdims=True) + epsilon)
    kv_ref[0] = (k * inv * gain_ref[...]).astype(jnp.bfloat16)
    kv_ref[1] = v_ref[...].astype(jnp.bfloat16)


def key_rows_of(projected, gain, kv_heads, head_dim):
    tokens = projected.shape[0]
    return pl.pallas_call(
        key_body,
        grid=(kv_heads,),
        in_specs=[
            pl.BlockSpec((tokens, head_dim), lambda g: (0, g)),
            pl.BlockSpec((tokens, head_dim), lambda g: (0, kv_heads + g)),
            pl.BlockSpec((1, head_dim), lambda g: (0, 0)),
        ],
        out_specs=pl.BlockSpec((2, tokens, head_dim), lambda g: (0, 0, g)),
        out_shape=jax.ShapeDtypeStruct((2, tokens, kv_heads * head_dim), jnp.bfloat16),
        name="key_rows",
    )(projected, projected, gain[None, :])


def key_grad_body(own_ref, near_ref, far_ref, k_ref, gain_ref, late_ref, out_ref, sum_ref):
    total = own_ref[0] + near_ref[0].astype(jnp.float32) + far_ref[0].astype(jnp.float32)

    @pl.when((pl.program_id(0) == 0) & (pl.program_id(1) == 0))
    def _():
        sum_ref[...] = jnp.zeros_like(sum_ref)

    @pl.when(pl.program_id(0) == 0)
    def _():
        k = k_ref[...]
        inv = lax.rsqrt(jnp.mean(k * k, axis=1, keepdims=True) + epsilon)
        k_hat = k * inv
        u = total * gain_ref[...]
        out_ref[...] = (
            inv * (u - k_hat * jnp.mean(u * k_hat, axis=1, keepdims=True))
        ).astype(jnp.bfloat16)
        sum_ref[...] += jnp.sum(total * k_hat, axis=0, keepdims=True)

    @pl.when(pl.program_id(0) == 1)
    def _():
        out_ref[...] = total.astype(jnp.bfloat16)


def key_grads_of(own, near, far, projected, gain, late, kv_heads, head_dim):
    tokens = projected.shape[0]
    stacked = pl.BlockSpec((1, tokens, head_dim), lambda t, g: (t, 0, g))
    row = pl.BlockSpec((1, head_dim), lambda t, g: (0, 0))
    return pl.pallas_call(
        key_grad_body,
        grid=(2, kv_heads),
        in_specs=[
            stacked,
            stacked,
            stacked,
            pl.BlockSpec((tokens, head_dim), lambda t, g: (0, g)),
            row,
            pl.BlockSpec(memory_space=pl.ANY),
        ],
        out_specs=(
            pl.BlockSpec((tokens, head_dim), lambda t, g: (0, t * kv_heads + g)),
            row,
        ),
        out_shape=(
            jax.ShapeDtypeStruct(late.shape, jnp.bfloat16),
            jax.ShapeDtypeStruct((1, head_dim), jnp.float32),
        ),
        input_output_aliases={5: 0},
        name="key_grads",
    )(own, near, far, projected, gain[None, :], late)


def normed_grad_body(part_ref, wide_ref, d_ref, x_ref, gain_ref, out_ref, dots_ref, dt_ref):
    @pl.when(pl.program_id(0) == 0)
    def _():
        dots_ref[...] = jnp.zeros_like(dots_ref)
        dt_ref[...] = jnp.transpose(d_ref[...])

    rounded = (part_ref[...] + dot(wide_ref[...], dt_ref[...])).astype(jnp.bfloat16)
    out_ref[...] = rounded
    gained = x_ref[...].astype(jnp.float32) * gain_ref[...]
    dots_ref[...] += jnp.sum(rounded.astype(jnp.float32) * gained, axis=0, keepdims=True)


def normed_grad(part, wide, d, turned, gain_column):
    width, tokens = part.shape
    cols = wide.shape[1]
    rows = max(r for r in range(128, 897, 128) if width % r == 0)
    by_row = pl.BlockSpec((rows, tokens), lambda i: (i, 0))
    return pl.pallas_call(
        normed_grad_body,
        grid=(width // rows,),
        in_specs=[
            by_row,
            pl.BlockSpec((rows, cols), lambda i: (i, 0)),
            pl.BlockSpec((tokens, cols), lambda i: (0, 0)),
            by_row,
            pl.BlockSpec((rows, 1), lambda i: (i, 0)),
        ],
        out_specs=(by_row, pl.BlockSpec((1, tokens), lambda i: (0, 0))),
        out_shape=(
            jax.ShapeDtypeStruct((width, tokens), jnp.bfloat16),
            jax.ShapeDtypeStruct((1, tokens), jnp.float32),
        ),
        scratch_shapes=[pltpu.VMEM((cols, tokens), jnp.bfloat16)],
        compiler_params=pltpu.CompilerParams(vmem_limit_bytes=40 << 20),
        name="normed_grad",
    )(part, wide, d, turned, gain_column)


CHUNKS = 4


def weight_grad_body(
    columns_ref,
    d_ref,
    first_ref,
    q_ref,
    k_ref,
    v_ref,
    left_ref,
    right_ref,
    sum_ref,
    left_sems,
    right_sems,
    *,
    scale,
):
    chunk = right_ref.shape[1]

    def fetch(i):
        at = pl.ds(pl.multiple_of(i * chunk, chunk), chunk)
        return (
            pltpu.make_async_copy(columns_ref.at[:, at], left_ref.at[i], left_sems.at[i]),
            pltpu.make_async_copy(d_ref.at[at, :], right_ref.at[i], right_sems.at[i]),
        )

    for i in range(CHUNKS):
        for copy in fetch(i):
            copy.start()
    sum_ref[...] = jnp.zeros_like(sum_ref)

    @pl.loop(0, CHUNKS)
    def _(i):
        for copy in fetch(i):
            copy.wait()
        sum_ref[...] += dot(left_ref[i], right_ref[i])

    cut = k_ref.shape[1]
    k_ref[...] = (scale * sum_ref[:, :cut]).astype(k_ref.dtype)
    v_ref[...] = (scale * sum_ref[:, cut : 2 * cut]).astype(v_ref.dtype)
    half = first_ref.shape[1]
    q_ref[:, :half] = first_ref[...]
    q_ref[:, half:] = (scale * sum_ref[:, 2 * cut :]).astype(q_ref.dtype)


def weight_grads(columns, d, first, scale):
    rows, tokens = columns.shape
    cols = d.shape[1]
    chunk = tokens // CHUNKS
    vmem = pl.BlockSpec(memory_space=pltpu.MemorySpace.VMEM)
    hbm = pl.BlockSpec(memory_space=pltpu.MemorySpace.HBM)
    half = first.shape[1]
    shape = jax.ShapeDtypeStruct((rows, (cols - half) // 2), jnp.bfloat16)
    return pl.pallas_call(
        functools.partial(weight_grad_body, scale=scale),
        in_specs=[hbm, hbm, vmem],
        out_specs=(vmem, vmem, vmem),
        out_shape=(jax.ShapeDtypeStruct((rows, 2 * half), jnp.bfloat16), shape, shape),
        scratch_shapes=[
            pltpu.VMEM((CHUNKS, rows, chunk), jnp.bfloat16),
            pltpu.VMEM((CHUNKS, chunk, cols), jnp.bfloat16),
            pltpu.VMEM((rows, cols), jnp.float32),
            pltpu.SemaphoreType.DMA((CHUNKS,)),
            pltpu.SemaphoreType.DMA((CHUNKS,)),
        ],
        compiler_params=pltpu.CompilerParams(vmem_limit_bytes=58 << 20),
        name="weight_grads",
    )(columns, d, first)


def attention_body(
    start_ref,
    ends_ref,
    q_ref,
    go_ref,
    own_ref,
    near_ref,
    far_ref,
    mult_ref,
    dq_ref,
    d_own_ref,
    d_near_ref,
    d_far_ref,
    sum_ref,
    bias_ref,
    k_ref,
    v_ref,
    kt_ref,
    vt_ref,
    dk_ref,
    dv_ref,
    *,
    rows,
    heads,
    segments,
):
    g = pl.program_id(0)
    s = pl.program_id(1)
    last = pl.num_programs(1) - 1
    tokens, head_dim = own_ref.shape[1:]
    reach = WIN
    span = reach + rows
    offset = pl.multiple_of(s * rows, rows)

    @pl.when(g == 0)
    def _():
        first = start_ref[0]
        key_pos = (first - reach + s * rows) + lax.broadcasted_iota(jnp.int32, (span, 1), 0)
        query_pos = (first + s * rows) + lax.broadcasted_iota(jnp.int32, (1, rows), 1)
        key_seg = jnp.zeros((span, 1), jnp.int32)
        query_seg = jnp.zeros((1, rows), jnp.int32)
        for i in range(segments):
            key_seg += (ends_ref[i] <= key_pos).astype(jnp.int32)
            query_seg += (ends_ref[i] <= query_pos).astype(jnp.int32)
        distance = query_pos - key_pos
        allowed = (
            (key_seg == query_seg) & (distance >= 0) & (distance < WIN) & (key_pos >= 0)
        )
        bias_ref[s] = jnp.where(allowed, 0.0, BLOCKED)

    @pl.when(s == 0)
    def _():
        for at, ref in enumerate((far_ref, near_ref, own_ref)):
            k_ref[pl.ds(at * tokens, tokens), :] = ref[0]
            v_ref[pl.ds(at * tokens, tokens), :] = ref[1]
        dk_ref[...] = jnp.zeros_like(dk_ref)
        dv_ref[...] = jnp.zeros_like(dv_ref)

    @pl.when((s == 0) & (g == 0))
    def _():
        sum_ref[...] = jnp.zeros_like(sum_ref)

    k = k_ref[pl.ds(offset, span), :]
    v = v_ref[pl.ds(offset, span), :]
    kt_ref[...] = jnp.transpose(k)
    vt_ref[...] = jnp.transpose(v)
    mult = mult_ref[...]
    bias = bias_ref[s]
    for h in range(heads):
        at = slice(h * head_dim, (h + 1) * head_dim)
        q = q_ref[:, at]
        inv = lax.rsqrt(jnp.mean(q * q, axis=1, keepdims=True) + epsilon)
        q_hat = q * inv
        q16 = (q_hat * mult).astype(jnp.bfloat16)
        go = go_ref[:, at]
        weights = jnp.exp(dot(k, q16, NT) + bias)
        over = 1.0 / jnp.sum(weights, axis=0, keepdims=True)
        out_t = dot(vt_ref[...], weights.astype(jnp.bfloat16)) * over
        delta = jnp.sum(jnp.transpose(go.astype(jnp.float32)) * out_t, axis=0, keepdims=True)
        probs = weights * over
        dv_ref[pl.ds(offset, span), :] += dot(probs.astype(jnp.bfloat16), go)
        d_scores = (probs * (dot(v, go, NT) - delta)).astype(jnp.bfloat16)
        dk_ref[pl.ds(offset, span), :] += dot(d_scores, q16)
        d_query = jnp.transpose(dot(kt_ref[...], d_scores))
        u = d_query * mult
        dq_ref[:, at] = (
            inv * (u - q_hat * jnp.mean(u * q_hat, axis=1, keepdims=True))
        ).astype(jnp.bfloat16)
        sum_ref[...] += jnp.sum(d_query * q_hat, axis=0, keepdims=True)

    @pl.when(s == last)
    def _():
        for at, ref in enumerate((d_far_ref, d_near_ref, d_own_ref)):
            ref[0] = dk_ref[pl.ds(at * tokens, tokens), :].astype(ref.dtype)
            ref[1] = dv_ref[pl.ds(at * tokens, tokens), :].astype(ref.dtype)


def attention_rest(start, ends, q, go, own, near, far, mult, *refs, **sizes):
    attention_body(start, ends, q, go, own, near, far, mult, *refs[3:], **sizes)


def attention(start, ends, q_raw, go, own, near, far, mult, head_dim, part, carry, place):
    tokens, q_cols = q_raw.shape
    all_kv = own.shape[2] // head_dim
    heads = q_cols // (all_kv * head_dim)
    kv_heads = all_kv // 2
    skip = part * kv_heads
    to = place // (heads * head_dim)
    rows = min(256, tokens)
    steps = tokens // rows
    span = WIN + rows
    stacked = pl.BlockSpec((2, tokens, head_dim), lambda g, s, *_: (0, 0, skip + g))
    by_query = pl.BlockSpec((rows, heads * head_dim), lambda g, s, *_: (s, skip + g))
    by_place = pl.BlockSpec((rows, heads * head_dim), lambda g, s, *_: (s, to + g))
    whole = pl.BlockSpec(memory_space=pl.ANY)
    row = pl.BlockSpec((1, head_dim), lambda g, s, *_: (0, 0))
    half = jax.ShapeDtypeStruct(own.shape, jnp.bfloat16)
    keys = WIN + tokens
    return pl.pallas_call(
        functools.partial(
            attention_rest if carry else attention_body,
            rows=rows,
            heads=heads,
            segments=ends.shape[0],
        ),
        grid_spec=pltpu.PrefetchScalarGridSpec(
            num_scalar_prefetch=2,
            grid=(kv_heads, steps),
            in_specs=[by_query, by_query, stacked, stacked, stacked, row]
            + [whole for _ in carry],
            out_specs=(by_place, stacked, stacked, stacked, row),
            scratch_shapes=[
                pltpu.VMEM((steps, span, rows), jnp.float32),
                pltpu.VMEM((keys, head_dim), jnp.bfloat16),
                pltpu.VMEM((keys, head_dim), jnp.bfloat16),
                pltpu.VMEM((head_dim, span), jnp.bfloat16),
                pltpu.VMEM((head_dim, span), jnp.bfloat16),
                pltpu.VMEM((keys, head_dim), jnp.float32),
                pltpu.VMEM((keys, head_dim), jnp.float32),
            ],
        ),
        out_shape=(
            jax.ShapeDtypeStruct((tokens, place + q_cols // 2), jnp.bfloat16),
            jax.ShapeDtypeStruct(own.shape, jnp.float32),
            half,
            half,
            jax.ShapeDtypeStruct((1, head_dim), jnp.float32),
        ),
        compiler_params=pltpu.CompilerParams(
            dimension_semantics=("arbitrary", "arbitrary"), vmem_limit_bytes=48 << 20
        ),
        input_output_aliases={8 + i: 1 + i for i in range(len(carry))},
        name="attention",
    )(start, ends, q_raw, go, own, near, far, mult, *carry)


def layer(
    inputs,
    output_cotangent,
    w_query,
    key_projection,
    value_projection,
    norm_gain,
    q_gain,
    key_norm_gain,
    half_lengths,
):
    tokens, model_width = inputs.shape
    head_dim = q_gain.shape[0]
    kv_cols = key_projection.shape[1]
    kv_heads = kv_cols // head_dim
    ctx_count = lax.axis_size("ctx")
    fsdp_count = lax.axis_size("fsdp")
    ctx_index = lax.axis_index("ctx")
    fsdp_index = lax.axis_index("fsdp")
    on_first_core = ctx_index % 2 == 0
    grad_scale = float(tokens * ctx_count) ** (-0.5)
    shard_rows = w_query.shape[0]
    features = model_width // fsdp_count

    key_value = jnp.concatenate([key_projection, value_projection], axis=1)
    wide_kv = lax.all_gather(key_value, "ctx", axis=0, tiled=True)
    wide_q = lax.all_gather(w_query, "ctx", axis=0, tiled=True)

    widened = inputs.astype(jnp.float32)
    turned = jnp.transpose(inputs)
    inv_rms = lax.rsqrt(jnp.mean(widened * widened, axis=1, keepdims=True) + epsilon)
    x_hat = widened * inv_rms
    normed = lax.optimization_barrier((x_hat * norm_gain).astype(jnp.bfloat16))
    inv_row = jnp.transpose(inv_rms)

    kv_raw = dot(normed, wide_kv)
    own = key_rows_of(kv_raw, key_norm_gain, kv_heads, head_dim)
    normed_turned = (turned.astype(jnp.float32) * inv_row * norm_gain[:, None]).astype(
        jnp.bfloat16
    )
    blocks, gain_column, own = lax.optimization_barrier(
        (share_of_columns(normed_turned, shard_rows), norm_gain[:, None], own)
    )
    far = shift(own, "ctx", REACH)
    picked = jnp.where(on_first_core, own, far)
    near = swap(picked, "ctx", 1)

    blocks, _ = lax.optimization_barrier((blocks, wide_q))
    pieces = start_columns(blocks)
    q_raw = dot(normed, wide_q)
    query_multiplier = (q_gain * query_scale)[None, :]

    def attend(part, carry, place):
        return attention(
            jnp.full((1,), ctx_index * tokens, jnp.int32),
            jnp.cumsum(half_lengths).astype(jnp.int32),
            q_raw,
            output_cotangent,
            own,
            near,
            far,
            query_multiplier,
            head_dim,
            part,
            carry,
            place,
        )

    dqa, *carry, qa_sum = attend(0, (), 0)
    all_dqa = lax.all_gather(dqa, "ctx", axis=0, tiled=True)
    late, d_own, d_near, d_far, qb_sum = attend(1, carry, 2 * kv_cols)
    q_sum = qa_sum + qb_sum
    dqb = late[:, 2 * kv_cols :]

    crossed = swap(d_near, "ctx", 1)
    nothing = jnp.zeros_like(crossed)
    outgoing = d_far + jnp.where(on_first_core, nothing, crossed)
    returned = shift(outgoing, "ctx", -REACH)
    query_part = dot(wide_q, jnp.concatenate([dqa, dqb], axis=1), NT)
    query_part = lax.optimization_barrier(query_part)
    late, k_sum = key_grads_of(
        d_own,
        jnp.where(on_first_core, crossed, nothing),
        returned,
        kv_raw,
        key_norm_gain,
        late,
        kv_heads,
        head_dim,
    )
    all_late = lax.all_gather(late, "ctx", axis=0, tiled=True)

    columns = finish_columns(pieces, dqb)

    head_part, row_dot = normed_grad(query_part, wide_kv, late, turned, gain_column)
    row_dot = everywhere(row_dot * inv_row, ("fsdp",))

    def part_of(array, index):
        return lax.dynamic_slice_in_dim(array, index * features, features, 0)

    sent = [part_of(head_part, fsdp_index ^ m) for m in range(1, fsdp_count)]
    sent = [swap(part, "fsdp", 1 + m) for m, part in enumerate(sent)]
    d_mine = part_of(head_part, fsdp_index).astype(jnp.float32)
    for part in sent:
        d_mine = d_mine + part.astype(jnp.float32)
    hat_mine = part_of(turned, fsdp_index).astype(jnp.float32) * inv_row
    upstream = d_mine * part_of(norm_gain, fsdp_index)[:, None]
    grad_inputs = jnp.transpose(
        (inv_row * (upstream - hat_mine * row_dot / model_width)).astype(jnp.bfloat16)
    )
    norm_row_dots = row_dot[0] * float(model_width) ** (-0.5)
    gain_term = grad_scale * jnp.sum(d_mine * hat_mine, axis=1)
    gain_sum = lax.dynamic_slice_in_dim(
        everywhere(gain_term, ("ctx",)),
        ctx_index * (features // ctx_count),
        features // ctx_count,
        0,
    )

    first_weights = (grad_scale * dot(columns, all_dqa)).astype(jnp.bfloat16)
    q_weights, k_weights, v_weights = weight_grads(columns, all_late, first_weights, grad_scale)

    gains = jnp.concatenate([q_sum * (grad_scale * query_scale), k_sum * grad_scale], axis=0)
    gains = everywhere(gains, ("fsdp",))
    gains = everywhere(gains, ("ctx",))
    return (
        grad_inputs,
        q_weights,
        k_weights,
        v_weights,
        gain_sum,
        gains[0],
        gains[1],
        norm_row_dots,
    )


def solution(mesh):
    placed = (
        P("ctx", None),
        P("ctx", "fsdp"),
        P("ctx", "fsdp"),
        P("ctx", "fsdp"),
        P("ctx", "fsdp"),
        P(),
        P(),
        P(),
        P(),
    )
    return jax.shard_map(
        layer,
        mesh=mesh,
        in_specs=placed,
        out_specs=(
            P("ctx", "fsdp"),
            P("ctx", "fsdp"),
            P("ctx", "fsdp"),
            P("ctx", "fsdp"),
            P(("fsdp", "ctx")),
            P(),
            P(),
            P("ctx"),
        ),
        check_vma=False,
    )
```
